32 devices in a mesh: ctx: 8 (over y, x, core), head: 4 (over z).
Axes of the slice: x: 2, y: 2, z: 4, core: 2. Of those that a mesh axis runs over, the one named last changes fastest.
Arguments:
- queries: bfloat16 [8192, 2048], P('ctx', 'head'), may hold values from -18 to 18
- keys: bfloat16 [8192, 2048], P('ctx', 'head'), may hold values from -6 to 6
- values: bfloat16 [8192, 2048], P('ctx', 'head'), may hold values from -6 to 6
- rates: float32 [8192, 4], P('ctx', 'head'), may hold values from 0.00048828125 to 0.0048828125
- fast_w1: bfloat16 [4, 512, 512], P('head'), may hold values from -0.25 to 0.25
- fast_w2: bfloat16 [4, 512, 512], P('head'), may hold values from -2 to 2
- fast_w3: bfloat16 [4, 512, 512], P('head'), may hold values from -0.25 to 0.25
- norm_gain: bfloat16 [2048], P('head'), may hold values from 0.25 to 1.75
- out_weight: bfloat16 [2048, 2048], P('head'), may hold values from -0.125 to 0.125
Outputs:
- output: bfloat16 [8192, 2048], P(('ctx', 'head'))
The draws below stay inside these ranges and needn't reach their ends.
All inputs are finite; a program needn't handle non-finite values.
Results may differ from the reference program's by a relative error of at most 0.014.
Values may be sent and summed in bfloat16 or wider, within the bound.
No kernel may reach another device: no remote copies, remote signals or barrier semaphores. Data moves between devices by JAX's collectives and lax.ppermute only.
A program may use at most 64 MiB of HBM per device.

```python
import math
import jax
import jax.numpy as jnp
from jax import lax

D = 2048
HD = 512
HEADS = 4
WINDOW = 256
TOKENS = 8192


def pair_draw(key):
    folded = jax.random.fold_in(key, 11)
    query_seed, key_seed = jax.random.split(folded, 2)
    shape_all = (TOKENS, HEADS * HD)
    query_all = jnp.clip(jax.random.normal(query_seed, shape_all, jnp.float32), -6.0, 6.0)
    keys_all = jnp.clip(jax.random.normal(key_seed, shape_all, jnp.float32), -6.0, 6.0)
    return (query_all, keys_all)


def draw_queries(key, part):
    return pair_draw(key)[0].astype(jnp.bfloat16)


def draw_keys(key, part):
    return pair_draw(key)[1].astype(jnp.bfloat16)


def draw_fast_w2(key, part):
    folded = jax.random.fold_in(key, 23)
    head_scale = (1.0 + jnp.arange(HEADS, dtype=jnp.float32))[:, None, None] / math.sqrt(HD)
    values_raw = jnp.clip(jax.random.normal(folded, (HEADS, HD, HD), jnp.float32), -3.0, 3.0)
    return (values_raw * head_scale).astype(jnp.bfloat16)


def block_levels(rng, shape, cuts, low, largest):
    factor_of, own = 1.0, jax.random.fold_in(rng, 6)
    for position, blocks in cuts:
        steps = jnp.exp(jax.random.uniform(jax.random.fold_in(own, position), (blocks,), jnp.float32, low / len(cuts), largest / len(cuts)))
        factor_of = factor_of * jnp.repeat(steps, shape[position] // blocks).reshape([-1 if axis == position else 1 for axis in range(len(shape))])
    return factor_of


def bell_draw(rng, extent, spread, most, cuts=(), held_as=jnp.bfloat16):
    entries = jax.random.normal(rng, extent, jnp.float32) * spread
    if len(cuts) > 0:
        entries = block_levels(rng, extent, cuts, -0.22, 0.18) * entries
    return jnp.clip(entries, min=-most, max=most).astype(held_as)


def setup_inputs(seed: int = 0) -> dict:
    splits = jax.random.split(jax.random.key(seed), 10)
    return {
        "queries": draw_queries(jax.random.fold_in(splits[9], 71), 0),
        "keys": draw_keys(jax.random.fold_in(splits[9], 71), 0),
        "values": bell_draw(splits[2], (TOKENS, HEADS * HD), 1.0, 6.0, ((0, 8), (1, 4))),
        "rates": jnp.clip(jnp.exp(math.log(0.0048828125) - 2.3025851 * jax.random.uniform(splits[3], (TOKENS, HEADS), jnp.float32) ** block_levels(splits[3], (TOKENS, HEADS), ((0, 8), (1, 4)), -0.2, 0.2)), 0.00048828125, 0.0048828125),
        "fast_w1": bell_draw(splits[4], (HEADS, HD, HD), HD ** -0.5, 0.25, ((0, 4),)),
        "fast_w2": draw_fast_w2(jax.random.fold_in(splits[9], 71), 0),
        "fast_w3": bell_draw(splits[6], (HEADS, HD, HD), HD ** -0.5, 0.25, ((0, 4),)),
        "norm_gain": jnp.clip(1.0 + 0.15 * jax.random.normal(splits[7], (HEADS * HD,), jnp.float32), 0.25, 1.75).astype(jnp.bfloat16),
        "out_weight": bell_draw(splits[8], (HEADS * HD, D), (HEADS * HD) ** -0.5, 0.125, ((0, 4),)),
    }


EPSILON = 1e-06

def contract_rows(left_side, right_side):
    return lax.dot_general(left_side, right_side, (((0,), (0,)), ((), ())), preferred_element_type=jnp.float32)

def renorm(weight, push, axis_dim):
    widened = weight.astype(jnp.float32)
    updated = widened + push
    old_norm = jnp.sqrt(lax.optimization_barrier(jnp.mean(widened * widened, axis=axis_dim, keepdims=True)) + EPSILON)
    new_norm = jnp.sqrt(lax.optimization_barrier(jnp.mean(updated * updated, axis=axis_dim, keepdims=True)) + EPSILON)
    return (updated * (old_norm / new_norm)).astype(jnp.bfloat16)

def fast_pushes(key_rows, value_rows, rate_column, gate_weight, down_weight, up_weight):
    gate_part = jnp.dot(key_rows, gate_weight, preferred_element_type=jnp.float32)
    up_part = jnp.dot(key_rows, up_weight, preferred_element_type=jnp.float32)
    sigmoid_gate = jax.nn.sigmoid(gate_part)
    activation = (gate_part * sigmoid_gate * up_part).astype(jnp.bfloat16)
    scaled = (value_rows.astype(jnp.float32) * rate_column).astype(jnp.bfloat16)
    back_grad = lax.dot_general(scaled, down_weight, (((1,), (1,)), ((), ())), preferred_element_type=jnp.float32)
    grad_gate = (back_grad * up_part * sigmoid_gate * (1.0 + gate_part * (1.0 - sigmoid_gate))).astype(jnp.bfloat16)
    grad_up = (back_grad * gate_part * sigmoid_gate).astype(jnp.bfloat16)
    return (contract_rows(key_rows, grad_gate), contract_rows(activation, scaled), contract_rows(key_rows, grad_up))

def apply_fast(query_rows, gate_weight, down_weight, up_weight):
    gate_part = jnp.dot(query_rows, gate_weight, preferred_element_type=jnp.float32)
    up_part = jnp.dot(query_rows, up_weight, preferred_element_type=jnp.float32)
    mixed_act = (gate_part * jax.nn.sigmoid(gate_part) * up_part).astype(jnp.bfloat16)
    return jnp.dot(mixed_act, down_weight, preferred_element_type=jnp.float32)

def window_block(query_block, key_block, value_block, query_first, key_first):
    scores = lax.dot_general(query_block, key_block, (((1,), (1,)), ((), ())), preferred_element_type=jnp.float32)
    scores = scores * (1.0 / math.sqrt(query_block.shape[1]))
    query_pos = query_first + jnp.arange(query_block.shape[0], dtype=jnp.int32)
    key_pos = key_first + jnp.arange(key_block.shape[0], dtype=jnp.int32)
    allowed = (key_pos[None, :] <= query_pos[:, None]) & (key_pos[None, :] > query_pos[:, None] - WINDOW) & (key_pos[None, :] >= 0)
    scores = jnp.where(allowed, scores, -jnp.inf)
    row_peak = lax.optimization_barrier(jnp.max(scores, axis=1, keepdims=True))
    exponent = jnp.exp(scores - row_peak)
    weights = (exponent / lax.optimization_barrier(jnp.sum(exponent, axis=1, keepdims=True))).astype(jnp.bfloat16)
    return jnp.dot(weights, value_block, preferred_element_type=jnp.float32)

def window_head(query_rows, key_rows, value_rows):
    block_rows = min(512, TOKENS)
    padding = jnp.zeros((WINDOW, key_rows.shape[1]), key_rows.dtype)
    key_padded = jnp.concatenate([padding, key_rows], axis=0)
    value_padded = jnp.concatenate([padding, value_rows], axis=0)

    def one_block(block_index):
        first_row = (block_index * block_rows).astype(jnp.int32)
        query_block = lax.dynamic_slice_in_dim(query_rows, first_row, block_rows, 0)
        key_block = lax.dynamic_slice_in_dim(key_padded, first_row, block_rows + WINDOW, 0)
        value_block = lax.dynamic_slice_in_dim(value_padded, first_row, block_rows + WINDOW, 0)
        return window_block(query_block, key_block, value_block, first_row, first_row - WINDOW)
    stacked = lax.map(one_block, jnp.arange(TOKENS // block_rows, dtype=jnp.int32))
    return stacked.reshape(TOKENS, key_rows.shape[1])

def reference(queries, keys, values, rates, fast_w1, fast_w2, fast_w3, norm_gain, out_weight):
    head_outputs = []
    for head_index in range(HEADS):
        lower_col = head_index * HD
        upper_col = lower_col + HD
        query_rows = queries[:, lower_col:upper_col]
        key_rows = keys[:, lower_col:upper_col]
        value_rows = values[:, lower_col:upper_col]
        push_one, push_two, push_three = fast_pushes(key_rows, value_rows, rates[:, head_index:head_index + 1], fast_w1[head_index], fast_w2[head_index], fast_w3[head_index])
        new_gate = renorm(fast_w1[head_index], push_one, 0)
        new_down = renorm(fast_w2[head_index], push_two, 0)
        new_up = renorm(fast_w3[head_index], push_three, 0)
        fast_out = apply_fast(query_rows, new_gate, new_down, new_up)
        head_outputs.append(fast_out + window_head(query_rows, key_rows, value_rows))
    combined = jnp.concatenate(head_outputs, axis=1)
    mean_square = lax.optimization_barrier(jnp.mean(combined * combined, axis=1, keepdims=True))
    normed = (combined * lax.rsqrt(mean_square + EPSILON) * norm_gain.astype(jnp.float32)).astype(jnp.bfloat16)
    running = jnp.zeros((TOKENS, D), jnp.float32)
    for head_index in range(HEADS):
        lower_col = head_index * HD
        upper_col = lower_col + HD
        partial_out = jnp.dot(normed[:, lower_col:upper_col], out_weight[lower_col:upper_col], preferred_element_type=jnp.float32).astype(jnp.bfloat16)
        partial_out = lax.optimization_barrier(partial_out)
        running = running + partial_out.astype(jnp.float32)
    return running.astype(jnp.bfloat16)
```

```python
import math

import jax
import jax.numpy as jnp
from jax import lax
from jax.experimental import pallas as pl
from jax.experimental.pallas import tpu as pltpu
from jax.sharding import PartitionSpec as P

WINDOW = 256


EPSILON = 1e-06


def from_behind(value, axis, by):
    count = lax.axis_size(axis)
    pairs = [(i, i + by) for i in range(count) if 0 <= i + by < count]
    return lax.ppermute(value, axis, pairs)


def swap(value, axis, mask):
    return lax.ppermute(value, axis, [(i, i ^ mask) for i in range(lax.axis_size(axis))])


def contract_rows(left_side, right_side):
    return lax.dot_general(
        left_side, right_side, (((0,), (0,)), ((), ())), preferred_element_type=jnp.float32
    )


def fast_pushes(key_rows, value_rows, rate_column, gate_weight, down_weight, up_weight):
    gate_part = jnp.dot(key_rows, gate_weight, preferred_element_type=jnp.float32)
    up_part = jnp.dot(key_rows, up_weight, preferred_element_type=jnp.float32)
    sigmoid_gate = jax.nn.sigmoid(gate_part)
    activation = (gate_part * sigmoid_gate * up_part).astype(jnp.bfloat16)
    scaled = (value_rows.astype(jnp.float32) * rate_column).astype(jnp.bfloat16)
    back_grad = lax.dot_general(
        scaled, down_weight, (((1,), (1,)), ((), ())), preferred_element_type=jnp.float32
    )
    grad_gate = (
        back_grad * up_part * sigmoid_gate * (1.0 + gate_part * (1.0 - sigmoid_gate))
    ).astype(jnp.bfloat16)
    grad_up = (back_grad * gate_part * sigmoid_gate).astype(jnp.bfloat16)
    return (
        contract_rows(key_rows, grad_gate),
        contract_rows(activation, scaled),
        contract_rows(key_rows, grad_up),
    )


def apply_fast(query_rows, gate_weight, down_weight, up_weight):
    gate_part = jnp.dot(query_rows, gate_weight, preferred_element_type=jnp.float32)
    up_part = jnp.dot(query_rows, up_weight, preferred_element_type=jnp.float32)
    mixed_act = (gate_part * jax.nn.sigmoid(gate_part) * up_part).astype(jnp.bfloat16)
    return jnp.dot(mixed_act, down_weight, preferred_element_type=jnp.float32)


def window_block(query_block, key_block, value_block, query_first, key_first):
    scores = lax.dot_general(
        query_block, key_block, (((1,), (1,)), ((), ())), preferred_element_type=jnp.float32
    )
    scores = scores * (1.0 / math.sqrt(query_block.shape[1]))
    query_pos = query_first + jnp.arange(query_block.shape[0], dtype=jnp.int32)
    key_pos = key_first + jnp.arange(key_block.shape[0], dtype=jnp.int32)
    allowed = (
        (key_pos[None, :] <= query_pos[:, None])
        & (key_pos[None, :] > query_pos[:, None] - WINDOW)
        & (key_pos[None, :] >= 0)
    )
    scores = jnp.where(allowed, scores, -jnp.inf)
    row_peak = jnp.max(scores, axis=1, keepdims=True)
    exponent = jnp.exp(scores - row_peak)
    weights = (exponent / jnp.sum(exponent, axis=1, keepdims=True)).astype(jnp.bfloat16)
    return jnp.dot(weights, value_block, preferred_element_type=jnp.float32)


def project_kernel(part_ref, *refs):
    heads = len(refs) - 8
    x_refs = refs[:heads]
    own, near, near_c, far, far_c, out_ref, w_ref, sem = refs[heads:]
    part = part_ref[0]
    rows = near.shape[1]
    width = 4 * rows
    copies = [pltpu.make_async_copy(own, w_ref.at[0], sem.at[0])]
    for k in range(heads - 1):
        for j, src in enumerate((near, near_c, far, far_c)):
            place = pl.multiple_of((part ^ j) * rows, rows)
            copies.append(
                pltpu.make_async_copy(
                    src.at[k], w_ref.at[k + 1, pl.ds(place, rows), :], sem.at[1 + 4 * k + j]
                )
            )
    for copy in copies:
        copy.start()
    for copy in copies:
        copy.wait()
    total = None
    squares = None
    for k in range(heads):
        x = x_refs[k][...]
        y = jnp.dot(x, w_ref[k], preferred_element_type=jnp.float32)
        wide = x.astype(jnp.float32)
        s = jnp.sum(wide * wide, axis=1, keepdims=True)
        total = y if total is None else total + y
        squares = s if squares is None else squares + s
    scale = lax.rsqrt(squares / (heads * width) + EPSILON)
    out_ref[...] = (total * scale).astype(out_ref.dtype)


def project(part, blocks, own, near, near_c, far, far_c):
    heads = len(blocks)
    vmem = pl.BlockSpec(memory_space=pltpu.VMEM)
    hbm = pl.BlockSpec(memory_space=pl.ANY)
    return pl.pallas_call(
        project_kernel,
        out_shape=jax.ShapeDtypeStruct((blocks[0].shape[0], own.shape[1]), jnp.bfloat16),
        in_specs=[pl.BlockSpec(memory_space=pltpu.SMEM)] + [vmem] * heads + [hbm] * 5,
        out_specs=vmem,
        scratch_shapes=[
            pltpu.VMEM((heads,) + own.shape, jnp.bfloat16),
            pltpu.SemaphoreType.DMA((1 + 4 * (heads - 1),)),
        ],
        name="project",
    )(part, *blocks, own, near, near_c, far, far_c)


def body(queries, keys, values, rates, fast_w1, fast_w2, fast_w3, norm_gain, out_weight):
    tok_rows, width = queries.shape
    ctx_count = lax.axis_size("ctx")
    heads = lax.axis_size("head")
    me = lax.axis_index("ctx")
    head = lax.axis_index("head")
    bits = ctx_count.bit_length() - 1
    assert ctx_count == 1 << bits and bits >= 3
    core = me & 1
    parity = ((me >> 1) ^ (me >> 2)) & 1
    part = 2 * parity + core

    scaled_out = (
        out_weight.astype(jnp.float32) * norm_gain.astype(jnp.float32)[:, None]
    ).astype(jnp.bfloat16)
    part_rows = width // 4
    piece = lax.dynamic_slice_in_dim(scaled_out, part * part_rows, part_rows, 0)
    near = jnp.stack([swap(piece, "head", k) for k in range(1, heads)])

    key_tail, value_tail = from_behind(
        (keys[tok_rows - WINDOW :], values[tok_rows - WINDOW :]), "ctx", 1
    )

    push_one, push_two, push_three = fast_pushes(
        keys, values, rates, fast_w1[0], fast_w2[0], fast_w3[0]
    )
    pushes = jnp.stack([push_one, push_two, push_three])
    half = width // 2
    keep = lax.dynamic_slice_in_dim(pushes, core * half, half, 2)
    give = lax.dynamic_slice_in_dim(pushes, (1 - core) * half, half, 2)
    keep = keep + swap(give.astype(jnp.bfloat16), "ctx", 1).astype(jnp.float32)
    quarter = half // 2
    streams = [keep[:, :, :quarter], keep[:, :, quarter:]]
    masks = [1 << b for b in range(1, bits)]
    for forward, backward in zip(masks, masks[::-1]):
        got = [
            swap(streams[0].astype(jnp.bfloat16), "ctx", forward),
            swap(streams[1].astype(jnp.bfloat16), "ctx", backward),
        ]
        streams = [s + g.astype(jnp.float32) for s, g in zip(streams, got)]
    summed = jnp.concatenate(streams, axis=2)
    stacked = jnp.concatenate([fast_w1, fast_w2, fast_w3], axis=0)
    old = lax.dynamic_slice_in_dim(stacked, core * half, half, 2).astype(jnp.float32)
    updated = old + summed
    old_norm = jnp.sqrt(jnp.mean(old * old, axis=1, keepdims=True) + EPSILON)
    new_norm = jnp.sqrt(jnp.mean(updated * updated, axis=1, keepdims=True) + EPSILON)
    renewed = (updated * (old_norm / new_norm)).astype(jnp.bfloat16)
    other = swap(renewed, "ctx", 1)
    low = jnp.where(core == 0, renewed, other)
    high = jnp.where(core == 0, other, renewed)
    new_weights = jnp.concatenate([low, high], axis=2)

    cross = [(i, i ^ (4 if i & 1 else 2)) for i in range(ctx_count)]
    far = lax.ppermute(near, "ctx", cross)
    near_c = swap(near, "ctx", 1)
    far_c = swap(far, "ctx", 1)

    key_ext = jnp.concatenate([key_tail, keys], axis=0)
    value_ext = jnp.concatenate([value_tail, values], axis=0)
    offset = me * tok_rows
    block_rows = min(512, tok_rows)
    pieces = []
    for block_index in range(tok_rows // block_rows):
        first_row = block_index * block_rows
        pieces.append(
            window_block(
                queries[first_row : first_row + block_rows],
                key_ext[first_row : first_row + block_rows + WINDOW],
                value_ext[first_row : first_row + block_rows + WINDOW],
                offset + first_row,
                offset + first_row - WINDOW,
            )
        )
    window_out = jnp.concatenate(pieces, axis=0)

    dest_rows = tok_rows // heads
    blocks = [None] * heads
    for k in list(range(heads - 1, 0, -1)) + [0]:
        first = (head ^ k) * dest_rows
        rows = lax.dynamic_slice_in_dim(queries, first, dest_rows, 0)
        seen = lax.dynamic_slice_in_dim(window_out, first, dest_rows, 0)
        fast_out = apply_fast(rows, new_weights[0], new_weights[1], new_weights[2])
        combined = (fast_out + seen).astype(jnp.bfloat16)
        blocks[k] = swap(combined, "head", k) if k else combined
    return project(part.reshape(1), blocks, scaled_out, near, near_c, far, far_c)


def solution(mesh):
    placed = (
        P("ctx", "head"),
        P("ctx", "head"),
        P("ctx", "head"),
        P("ctx", "head"),
        P("head", None, None),
        P("head", None, None),
        P("head", None, None),
        P("head"),
        P("head", None),
    )
    return jax.shard_map(
        body, mesh=mesh, in_specs=placed, out_specs=P(("ctx", "head"), None), check_vma=False
    )
```

```python
import functools
import math

import jax
import jax.numpy as jnp
from jax import lax
from jax.experimental import pallas as pl
from jax.experimental.pallas import tpu as pltpu
from jax.sharding import PartitionSpec as P


WINDOW = 256
EPSILON = 1e-06

VMEM = pl.BlockSpec(memory_space=pltpu.VMEM)
SMEM = pl.BlockSpec(memory_space=pltpu.SMEM)
HBM = pl.BlockSpec(memory_space=pltpu.HBM)


def near_core(*arrays):
    return [pltpu.with_memory_space_constraint(a, pltpu.VMEM) for a in arrays]


def far_core(*arrays):
    return [pltpu.with_memory_space_constraint(a, pltpu.HBM) for a in arrays]


def grant(mib):
    return pltpu.CompilerParams(vmem_limit_bytes=mib << 20)


def swap(value, axis, mask):
    return lax.ppermute(value, axis, [(i, i ^ mask) for i in range(lax.axis_size(axis))])


def dot(left, right, left_dim=1, right_dim=0):
    return lax.dot_general(
        left, right, (((left_dim,), (right_dim,)), ((), ())), preferred_element_type=jnp.float32
    )


def push_kernel(core_ref, k_hbm, v_hbm, r_hbm, w1_hbm, w2_hbm, w3_hbm, give_ref, keep_ref, tail_hbm,
                k_ref, v_ref, r_ref, w1_ref, w2_ref, w3_ref, act_ref, g1_ref, g3_ref, sc_ref, sem):
    rows, width = k_ref.shape
    steps = 4
    block = rows // steps
    half = width // 2
    sources = [(w1_hbm, w1_ref), (w3_hbm, w3_ref), (w2_hbm, w2_ref)]
    copies = [pltpu.make_async_copy(src.at[0], dst, sem.at[j]) for j, (src, dst) in enumerate(sources)]
    copies.append(pltpu.make_async_copy(r_hbm, r_ref, sem.at[3]))
    streams = []
    for i in range(steps):
        at = pl.ds(i * block, block)
        streams.append([
            pltpu.make_async_copy(src.at[at, :], dst.at[at, :], sem.at[4 + 2 * i + j])
            for j, (src, dst) in enumerate([(k_hbm, k_ref), (v_hbm, v_ref)])
        ])
    last = pl.ds(rows - WINDOW, WINDOW)
    tails = [
        pltpu.make_async_copy(src.at[last, :], tail_hbm.at[pl.ds(j * WINDOW, WINDOW), :], sem.at[12 + j])
        for j, src in enumerate((k_hbm, v_hbm))
    ]
    streams[0][0].start()
    for copy in copies:
        copy.start()
    for i in range(steps):
        for copy in streams[i][1 if i == 0 else 0:]:
            copy.start()
    for copy in tails:
        copy.start()
    for i in range(steps):
        at = slice(i * block, (i + 1) * block)
        if i == 0:
            streams[0][0].wait()
            copies[0].wait()
            copies[1].wait()
        else:
            streams[i][0].wait()
        k = k_ref[at, :]
        gate = dot(k, w1_ref[...])
        up = dot(k, w3_ref[...])
        if i == 0:
            copies[2].wait()
            copies[3].wait()
        streams[i][1].wait()
        rate = jnp.transpose(jnp.broadcast_to(r_ref[:, at], (128, block)))
        rate = jnp.concatenate([rate] * (width // 128), axis=1)
        scaled = (v_ref[at, :].astype(jnp.float32) * rate).astype(jnp.bfloat16)
        back = dot(scaled, w2_ref[...], 1, 1)
        s = jax.nn.sigmoid(gate)
        gs = gate * s
        act_ref[at, :] = (gs * up).astype(jnp.bfloat16)
        sc_ref[at, :] = scaled
        g1_ref[at, :] = (back * up * (s + gs * (1.0 - s))).astype(jnp.bfloat16)
        g3_ref[at, :] = (back * gs).astype(jnp.bfloat16)
    core = core_ref[0]
    theirs = pl.ds(pl.multiple_of((1 - core) * half, half), half)
    mine = pl.ds(pl.multiple_of(core * half, half), half)
    for j, (left, right) in enumerate([(k_ref, g1_ref), (act_ref, sc_ref), (k_ref, g3_ref)]):
        left = left[...]
        give_ref[j] = dot(left, right[:, theirs], 0, 0).astype(jnp.bfloat16)
        keep_ref[j] = dot(left, right[:, mine], 0, 0)
    for copy in tails:
        copy.wait()


def pushes(core, keys, values, rates, w1, w2, w3):
    rows, width = keys.shape
    half = width // 2
    wide = pltpu.VMEM((rows, width), jnp.bfloat16)
    weight = pltpu.VMEM((width, width), jnp.bfloat16)
    return pl.pallas_call(
        push_kernel,
        out_shape=(
            pltpu.VMEM((3, width, half), jnp.bfloat16),
            pltpu.VMEM((3, width, half), jnp.float32),
            jax.ShapeDtypeStruct((2 * WINDOW, width), jnp.bfloat16),
        ),
        compiler_params=grant(24),
        in_specs=[SMEM] + [HBM] * 6,
        out_specs=(VMEM, VMEM, HBM),
        scratch_shapes=[wide, wide, pltpu.VMEM((1, rows), jnp.float32), weight, weight, weight,
                        wide, wide, wide, wide, pltpu.SemaphoreType.DMA((14,))],
        name="pushes",
    )(core, *far_core(keys, values, rates.reshape(1, rows), w1, w2, w3))


def first_add_kernel(keep_ref, got_ref, sum_ref, a_ref, b_ref):
    quarter = a_ref.shape[2]
    total = keep_ref[...] + got_ref[...].astype(jnp.float32)
    sum_ref[...] = total
    a_ref[...] = total[:, :, :quarter].astype(jnp.bfloat16)
    b_ref[...] = total[:, :, quarter:].astype(jnp.bfloat16)


def later_add_kernel(keep_ref, got_a_ref, got_b_ref, sum_ref, a_ref, b_ref):
    quarter = a_ref.shape[2]
    first = keep_ref[:, :, :quarter] + got_a_ref[...].astype(jnp.float32)
    second = keep_ref[:, :, quarter:] + got_b_ref[...].astype(jnp.float32)
    sum_ref[:, :, :quarter] = first
    sum_ref[:, :, quarter:] = second
    a_ref[...] = first.astype(jnp.bfloat16)
    b_ref[...] = second.astype(jnp.bfloat16)


def add(keep, *got):
    stream = pltpu.VMEM(keep.shape[:2] + (keep.shape[2] // 2,), jnp.bfloat16)
    return pl.pallas_call(
        first_add_kernel if len(got) == 1 else later_add_kernel,
        out_shape=(pltpu.VMEM(keep.shape, jnp.float32), stream, stream),
        compiler_params=grant(16),
        in_specs=[VMEM] * (1 + len(got)),
        out_specs=(VMEM,) * 3,
    )(*near_core(keep, *got))


def renorm_kernel(core_ref, keep_ref, got_a_ref, got_b_ref, w1_ref, w2_ref, w3_ref, out_ref):
    quarter = got_a_ref.shape[2]
    core = core_ref[0]
    for j, w_ref in enumerate((w1_ref, w2_ref, w3_ref)):
        for part, got_ref in enumerate((got_a_ref, got_b_ref)):
            at = slice(part * quarter, (part + 1) * quarter)
            start = pl.multiple_of(core * 2 * quarter + part * quarter, quarter)
            old = w_ref[0, :, pl.ds(start, quarter)].astype(jnp.float32)
            new = old + (keep_ref[j, :, at] + got_ref[j].astype(jnp.float32))
            old_norm = jnp.sqrt(jnp.mean(old * old, axis=0, keepdims=True) + EPSILON)
            new_norm = jnp.sqrt(jnp.mean(new * new, axis=0, keepdims=True) + EPSILON)
            out_ref[j, :, at] = (new * (old_norm / new_norm)).astype(jnp.bfloat16)


def renorm(core, keep, got_a, got_b, w1, w2, w3):
    return pl.pallas_call(
        renorm_kernel,
        out_shape=pltpu.VMEM(keep.shape, jnp.bfloat16),
        compiler_params=grant(16),
        in_specs=[SMEM] + [VMEM] * 6,
        out_specs=VMEM,
        name="renorm",
    )(core, *near_core(keep, got_a, got_b), w1, w2, w3)


def window_kernel(me_ref, q_hbm, k_hbm, v_hbm, tail_ref, out_ref, q_ref, k_ref, v_ref, sem):
    rows, width = q_ref.shape
    scale = 1.0 / math.sqrt(width)
    query = lax.broadcasted_iota(jnp.int32, (WINDOW, 2 * WINDOW), 0)
    key = lax.broadcasted_iota(jnp.int32, (WINDOW, 2 * WINDOW), 1)
    allowed = (key > query) & (key <= query + WINDOW)
    allowed_first = allowed & ((key >= WINDOW) | (me_ref[0] > 0))
    count = rows // WINDOW
    loads = [[
        pltpu.make_async_copy(tail_ref.at[pl.ds(j * WINDOW, WINDOW), :], dst.at[pl.ds(0, WINDOW), :], sem.at[j])
        for j, dst in enumerate((k_ref, v_ref))
    ]]
    for i in range(count):
        at, after = pl.ds(i * WINDOW, WINDOW), pl.ds((i + 1) * WINDOW, WINDOW)
        loads.append([
            pltpu.make_async_copy(q_hbm.at[at, :], q_ref.at[at, :], sem.at[3 * i + 2]),
            pltpu.make_async_copy(k_hbm.at[at, :], k_ref.at[after, :], sem.at[3 * i + 3]),
            pltpu.make_async_copy(v_hbm.at[at, :], v_ref.at[after, :], sem.at[3 * i + 4]),
        ])
    for group in loads:
        for load in group:
            load.start()
    for load in loads[0]:
        load.wait()
    for i in range(count):
        for load in loads[i + 1]:
            load.wait()
        at = slice(i * WINDOW, (i + 1) * WINDOW)
        seen = slice(i * WINDOW, (i + 2) * WINDOW)
        scores = dot(q_ref[at, :], k_ref[seen, :], 1, 1) * scale
        scores = jnp.where(allowed_first if i == 0 else allowed, scores, -jnp.inf)
        peak = jnp.max(scores, axis=1, keepdims=True)
        exponent = jnp.exp(scores - peak)
        weights = exponent / jnp.sum(exponent, axis=1, keepdims=True)
        out_ref[at, :] = dot(weights.astype(jnp.bfloat16), v_ref[seen, :])


def window(me, queries, keys, values, tail):
    rows, width = queries.shape
    return pl.pallas_call(
        window_kernel,
        out_shape=pltpu.VMEM(queries.shape, jnp.float32),
        compiler_params=grant(24),
        in_specs=[SMEM] + [HBM] * 3 + [VMEM],
        out_specs=VMEM,
        scratch_shapes=[pltpu.VMEM((rows, width), jnp.bfloat16)]
        + [pltpu.VMEM((rows + WINDOW, width), jnp.bfloat16)] * 2
        + [pltpu.SemaphoreType.DMA((2 + 3 * (rows // WINDOW),))],
        name="window",
    )(me, *far_core(queries, keys, values), *near_core(tail))


def apply_kernel(slot, core_ref, head_ref, q_ref, seen_ref, mine_ref, other_ref, out_ref):
    rows = out_ref.shape[0]
    half = mine_ref.shape[2]
    core = core_ref[0]
    own = pl.ds(pl.multiple_of(core * half, half), half)
    rest = pl.ds(pl.multiple_of((1 - core) * half, half), half)
    here = pl.ds(pl.multiple_of((head_ref[0] ^ slot) * rows, rows), rows)
    q = q_ref[here, :]

    def mixed(ref):
        gate = dot(q, ref[0])
        up = dot(q, ref[2])
        return (gate * jax.nn.sigmoid(gate) * up).astype(jnp.bfloat16)

    first, second = mixed(mine_ref), mixed(other_ref)
    for ref, at in ((mine_ref, own), (other_ref, rest)):
        fast = dot(first, ref[1, own, :]) + dot(second, ref[1, rest, :])
        out_ref[:, at] = (fast + seen_ref[here, at]).astype(jnp.bfloat16)


def apply_fast(slot, core, head, queries, seen, mine, other, rows):
    return pl.pallas_call(
        functools.partial(apply_kernel, slot),
        out_shape=pltpu.VMEM((rows, queries.shape[1]), jnp.bfloat16),
        compiler_params=grant(16),
        in_specs=[SMEM] * 2 + [VMEM] * 4,
        out_specs=VMEM,
        name="apply",
    )(core, head, *near_core(queries, seen, mine, other))


def own_project_kernel(x_ref, gain_ref, w_ref, out_ref, squares_ref):
    wide = x_ref[...].astype(jnp.float32)
    squares_ref[...] = jnp.sum(wide * wide, axis=1, keepdims=True)
    x = (wide * gain_ref[...].astype(jnp.float32)).astype(jnp.bfloat16)
    out_ref[...] = dot(x, w_ref[...])


def own_project(x, gain, weight):
    return pl.pallas_call(
        own_project_kernel,
        out_shape=(
            pltpu.VMEM((x.shape[0], weight.shape[1]), jnp.float32),
            pltpu.VMEM((x.shape[0], 1), jnp.float32),
        ),
        compiler_params=grant(16),
        in_specs=[VMEM] * 3,
        out_specs=(VMEM, VMEM),
        name="own_project",
    )(*near_core(x), gain, weight)


def project_kernel(part_ref, *refs):
    *xs, base_ref, squares_ref, near, near_c, far, far_c, out_ref, w_ref = refs
    rows = near.shape[1]
    heads = len(xs) + 1
    squares = squares_ref[...]
    for k in range(heads - 1):
        for j, src in enumerate((near, near_c, far, far_c)):
            place = pl.multiple_of((part_ref[0] ^ j) * rows, rows)
            w_ref[k, pl.ds(place, rows), :] = src[k]
        wide = xs[k][...].astype(jnp.float32)
        squares = squares + jnp.sum(wide * wide, axis=1, keepdims=True)
    scale = lax.rsqrt(squares / (heads * 4 * rows) + EPSILON)
    block = 512
    for start in range(0, out_ref.shape[1], block):
        at = slice(start, start + block)
        total = base_ref[:, at]
        for k in range(heads - 1):
            total = total + dot(xs[k][...], w_ref[k, :, at])
        out_ref[:, at] = (total * scale).astype(out_ref.dtype)


def project(part, xs, base, squares, pieces):
    rows, columns = base.shape
    count, piece_rows, _ = pieces[0].shape
    return pl.pallas_call(
        project_kernel,
        out_shape=jax.ShapeDtypeStruct((rows, columns), jnp.bfloat16),
        in_specs=[SMEM] + [VMEM] * (len(xs) + 6),
        out_specs=VMEM,
        scratch_shapes=[pltpu.VMEM((count, 4 * piece_rows, columns), jnp.bfloat16)],
        compiler_params=grant(16),
        name="project",
    )(part, *near_core(*xs, base, squares, *pieces))


def step(queries, keys, values, rates, fast_w1, fast_w2, fast_w3, norm_gain, out_weight):
    tok_rows, width = queries.shape
    ctx_count = lax.axis_size("ctx")
    heads = lax.axis_size("head")
    me = lax.axis_index("ctx").astype(jnp.int32)
    head = lax.axis_index("head").astype(jnp.int32)
    bits = ctx_count.bit_length() - 1
    assert ctx_count == 1 << bits and bits >= 3
    core = me & 1
    parity = ((me >> 1) ^ (me >> 2)) & 1
    part = 2 * parity + core
    core1 = core.reshape(1)

    give, keep, tail = pushes(core1, keys, values, rates, fast_w1, fast_w2, fast_w3)
    got = [swap(give, "ctx", 1)]
    masks = [1 << b for b in range(1, bits)]
    for forward, backward in zip(masks, masks[::-1]):
        keep, first, second = add(keep, *got)
        got = []
        got.append(swap(first, "ctx", forward))
        got.append(swap(second, "ctx", backward))
    mine = renorm(core1, keep, *got, fast_w1, fast_w2, fast_w3)
    other = swap(mine, "ctx", 1)

    tail = lax.ppermute(tail, "ctx", [(i, i + 1) for i in range(ctx_count - 1)])
    part_rows = width // 4
    piece = lax.dynamic_slice_in_dim(out_weight, part * part_rows, part_rows, 0)
    gain = lax.dynamic_slice_in_dim(norm_gain, part * part_rows, part_rows, 0)
    piece = (piece.astype(jnp.float32) * gain.astype(jnp.float32)[:, None]).astype(jnp.bfloat16)
    near = []
    for k in range(1, heads):
        near.append(swap(piece, "head", k))
    near = jnp.stack(near)
    far = lax.ppermute(near, "ctx", [(i, i ^ (4 if i & 1 else 2)) for i in range(ctx_count)])
    near_c = swap(near, "ctx", 1)
    far_c = swap(far, "ctx", 1)

    seen = window(me.reshape(1), queries, keys, values, tail)

    rows = tok_rows // heads
    blocks = [None] * heads
    for k in list(range(heads - 1, 0, -1)) + [0]:
        combined = apply_fast(k, core1, head.reshape(1), queries, seen, mine, other, rows)
        blocks[k] = swap(combined, "head", k) if k else combined
    base, squares = own_project(blocks[0], norm_gain.reshape(1, width), out_weight)
    return project(part.reshape(1), blocks[1:], base, squares, [near, near_c, far, far_c])


def solution(mesh):
    placed = (
        P("ctx", "head"),
        P("ctx", "head"),
        P("ctx", "head"),
        P("ctx", "head"),
        P("head", None, None),
        P("head", None, None),
        P("head", None, None),
        P("head"),
        P("head", None),
    )
    return jax.shard_map(
        step, mesh=mesh, in_specs=placed, out_specs=P(("ctx", "head"), None), check_vma=False
    )
```

```python
import functools
import math

import jax
import jax.numpy as jnp
from jax import lax
from jax.experimental import pallas as pl
from jax.experimental.pallas import tpu as pltpu
from jax.sharding import PartitionSpec as P


WINDOW = 256
EPSILON = 1e-06

VMEM = pl.BlockSpec(memory_space=pltpu.VMEM)
SMEM = pl.BlockSpec(memory_space=pltpu.SMEM)
HBM = pl.BlockSpec(memory_space=pltpu.HBM)


def near_core(*arrays):
    return [pltpu.with_memory_space_constraint(a, pltpu.VMEM) for a in arrays]


def far_core(*arrays):
    return [pltpu.with_memory_space_constraint(a, pltpu.HBM) for a in arrays]


def grant(mib):
    return pltpu.CompilerParams(vmem_limit_bytes=mib << 20)


def swap(value, axis, mask):
    return lax.ppermute(value, axis, [(i, i ^ mask) for i in range(lax.axis_size(axis))])


def dot(left, right, left_dim=1, right_dim=0):
    return lax.dot_general(
        left, right, (((left_dim,), (right_dim,)), ((), ())), preferred_element_type=jnp.float32
    )


def column(row, width):
    tall = jnp.transpose(jnp.broadcast_to(row, (128, row.shape[1])))
    return jnp.concatenate([tall] * (width // 128), axis=1)


def prepare_kernel(part_ref, k_hbm, v_hbm, gain_ref, w_hbm, tail_ref, piece_ref, w_ref, sem):
    rows, columns = piece_ref.shape
    first = pl.multiple_of(part_ref[0] * rows, rows)
    left = pl.multiple_of(part_ref[1] * columns, columns)
    load = pltpu.make_async_copy(w_hbm.at[pl.ds(first, rows), pl.ds(left, columns)], w_ref, sem.at[0])
    load.start()
    last = pl.ds(k_hbm.shape[0] - WINDOW, WINDOW)
    tails = [
        pltpu.make_async_copy(src.at[last, :], tail_ref.at[pl.ds(j * WINDOW, WINDOW), :], sem.at[1 + j])
        for j, src in enumerate((k_hbm, v_hbm))
    ]
    for tail in tails:
        tail.start()
    gain = column(gain_ref[:, pl.ds(first, rows)].astype(jnp.float32), columns)
    load.wait()
    piece_ref[...] = (w_ref[...].astype(jnp.float32) * gain).astype(jnp.bfloat16)
    for tail in tails:
        tail.wait()


def prepare(part, keys, values, gain, weight):
    piece = pltpu.VMEM((weight.shape[0] // 2, weight.shape[1] // 2), jnp.bfloat16)
    return pl.pallas_call(
        prepare_kernel,
        out_shape=(pltpu.VMEM((2 * WINDOW, keys.shape[1]), jnp.bfloat16), piece),
        compiler_params=grant(8),
        in_specs=[SMEM, HBM, HBM, VMEM, HBM],
        out_specs=(VMEM, VMEM),
        scratch_shapes=[piece, pltpu.SemaphoreType.DMA((3,))],
        name="prepare",
    )(part, *far_core(keys, values), gain, *far_core(weight))


def push_kernel(core_ref, k_ref, v_ref, r_ref, w1_ref, w2_ref, w3_ref, give_ref, keep_ref,
                act_ref, g1_ref, g3_ref, sc_ref):
    rows, width = k_ref.shape
    steps = 4
    block = rows // steps
    half = width // 2
    for i in range(steps):
        at = slice(i * block, (i + 1) * block)
        k = k_ref[at, :]
        gate = dot(k, w1_ref[0])
        up = dot(k, w3_ref[0])
        rate = column(r_ref[:, at], width)
        scaled = (v_ref[at, :].astype(jnp.float32) * rate).astype(jnp.bfloat16)
        back = dot(scaled, w2_ref[0], 1, 1)
        s = jax.nn.sigmoid(gate)
        gs = gate * s
        act_ref[at, :] = (gs * up).astype(jnp.bfloat16)
        sc_ref[at, :] = scaled
        g1_ref[at, :] = (back * up * (s + gs * (1.0 - s))).astype(jnp.bfloat16)
        g3_ref[at, :] = (back * gs).astype(jnp.bfloat16)
    core = core_ref[0]
    theirs = pl.ds(pl.multiple_of((1 - core) * half, half), half)
    mine = pl.ds(pl.multiple_of(core * half, half), half)
    for j, (left, right) in enumerate([(k_ref, g1_ref), (act_ref, sc_ref), (k_ref, g3_ref)]):
        left = left[...]
        give_ref[j] = dot(left, right[:, theirs], 0, 0).astype(jnp.bfloat16)
        keep_ref[j] = dot(left, right[:, mine], 0, 0)


def pushes(core, keys, values, rates, w1, w2, w3):
    rows, width = keys.shape
    half = width // 2
    wide = pltpu.VMEM((rows, width), jnp.bfloat16)
    return pl.pallas_call(
        push_kernel,
        out_shape=(
            pltpu.VMEM((3, width, half), jnp.bfloat16),
            pltpu.VMEM((3, width, half), jnp.float32),
        ),
        compiler_params=grant(16),
        in_specs=[SMEM] + [VMEM] * 6,
        out_specs=(VMEM, VMEM),
        scratch_shapes=[wide] * 4,
        name="pushes",
    )(core, *near_core(keys, values, rates.reshape(1, rows), w1, w2, w3))


def first_add_kernel(keep_ref, got_ref, sum_ref, a_ref, b_ref):
    quarter = a_ref.shape[2]
    total = keep_ref[...] + got_ref[...].astype(jnp.float32)
    sum_ref[...] = total
    a_ref[...] = total[:, :, :quarter].astype(jnp.bfloat16)
    b_ref[...] = total[:, :, quarter:].astype(jnp.bfloat16)


def later_add_kernel(keep_ref, got_a_ref, got_b_ref, sum_ref, a_ref, b_ref):
    quarter = a_ref.shape[2]
    first = keep_ref[:, :, :quarter] + got_a_ref[...].astype(jnp.float32)
    second = keep_ref[:, :, quarter:] + got_b_ref[...].astype(jnp.float32)
    sum_ref[:, :, :quarter] = first
    sum_ref[:, :, quarter:] = second
    a_ref[...] = first.astype(jnp.bfloat16)
    b_ref[...] = second.astype(jnp.bfloat16)


def add(keep, *got):
    stream = pltpu.VMEM(keep.shape[:2] + (keep.shape[2] // 2,), jnp.bfloat16)
    return pl.pallas_call(
        first_add_kernel if len(got) == 1 else later_add_kernel,
        out_shape=(pltpu.VMEM(keep.shape, jnp.float32), stream, stream),
        compiler_params=grant(16),
        in_specs=[VMEM] * (1 + len(got)),
        out_specs=(VMEM,) * 3,
    )(*near_core(keep, *got))


def renorm_kernel(core_ref, keep_ref, got_a_ref, got_b_ref, w1_ref, w2_ref, w3_ref, out_ref):
    quarter = got_a_ref.shape[2]
    core = core_ref[0]
    for j, w_ref in enumerate((w1_ref, w2_ref, w3_ref)):
        for part, got_ref in enumerate((got_a_ref, got_b_ref)):
            at = slice(part * quarter, (part + 1) * quarter)
            start = pl.multiple_of(core * 2 * quarter + part * quarter, quarter)
            old = w_ref[0, :, pl.ds(start, quarter)].astype(jnp.float32)
            new = old + (keep_ref[j, :, at] + got_ref[j].astype(jnp.float32))
            old_norm = jnp.sqrt(jnp.mean(old * old, axis=0, keepdims=True) + EPSILON)
            new_norm = jnp.sqrt(jnp.mean(new * new, axis=0, keepdims=True) + EPSILON)
            out_ref[j, :, at] = (new * (old_norm / new_norm)).astype(jnp.bfloat16)


def renorm(core, keep, got_a, got_b, w1, w2, w3):
    return pl.pallas_call(
        renorm_kernel,
        out_shape=pltpu.VMEM(keep.shape, jnp.bfloat16),
        compiler_params=grant(16),
        in_specs=[SMEM] + [VMEM] * 6,
        out_specs=VMEM,
        name="renorm",
    )(core, *near_core(keep, got_a, got_b), w1, w2, w3)


def window_kernel(me_ref, q_hbm, k_hbm, v_hbm, tail_ref, out_ref, q_ref, k_ref, v_ref, sem):
    rows, width = q_ref.shape
    scale = 1.0 / math.sqrt(width)
    query = lax.broadcasted_iota(jnp.int32, (WINDOW, 2 * WINDOW), 0)
    key = lax.broadcasted_iota(jnp.int32, (WINDOW, 2 * WINDOW), 1)
    allowed = (key > query) & (key <= query + WINDOW)
    allowed_first = allowed & ((key >= WINDOW) | (me_ref[0] > 0))
    count = rows // WINDOW
    loads = [[
        pltpu.make_async_copy(tail_ref.at[pl.ds(j * WINDOW, WINDOW), :], dst.at[pl.ds(0, WINDOW), :], sem.at[j])
        for j, dst in enumerate((k_ref, v_ref))
    ]]
    for i in range(count):
        at, after = pl.ds(i * WINDOW, WINDOW), pl.ds((i + 1) * WINDOW, WINDOW)
        loads.append([
            pltpu.make_async_copy(q_hbm.at[at, :], q_ref.at[at, :], sem.at[3 * i + 2]),
            pltpu.make_async_copy(k_hbm.at[at, :], k_ref.at[after, :], sem.at[3 * i + 3]),
            pltpu.make_async_copy(v_hbm.at[at, :], v_ref.at[after, :], sem.at[3 * i + 4]),
        ])
    for group in loads:
        for load in group:
            load.start()
    for load in loads[0]:
        load.wait()
    for i in range(count):
        for load in loads[i + 1]:
            load.wait()
        at = slice(i * WINDOW, (i + 1) * WINDOW)
        seen = slice(i * WINDOW, (i + 2) * WINDOW)
        scores = dot(q_ref[at, :], k_ref[seen, :], 1, 1) * scale
        scores = jnp.where(allowed_first if i == 0 else allowed, scores, -jnp.inf)
        peak = jnp.max(scores, axis=1, keepdims=True)
        exponent = jnp.exp(scores - peak)
        weights = exponent / jnp.sum(exponent, axis=1, keepdims=True)
        out_ref[at, :] = dot(weights.astype(jnp.bfloat16), v_ref[seen, :])


def window(me, queries, keys, values, tail):
    rows, width = queries.shape
    return pl.pallas_call(
        window_kernel,
        out_shape=pltpu.VMEM(queries.shape, jnp.float32),
        compiler_params=grant(24),
        in_specs=[SMEM] + [HBM] * 3 + [VMEM],
        out_specs=VMEM,
        scratch_shapes=[pltpu.VMEM((rows, width), jnp.bfloat16)]
        + [pltpu.VMEM((rows + WINDOW, width), jnp.bfloat16)] * 2
        + [pltpu.SemaphoreType.DMA((2 + 3 * (rows // WINDOW),))],
        name="window",
    )(me, *far_core(queries, keys, values), *near_core(tail))


def apply_kernel(slot, core_ref, head_ref, q_ref, seen_ref, mine_ref, other_ref, out_ref):
    rows = out_ref.shape[0]
    half = mine_ref.shape[2]
    core = core_ref[0]
    own = pl.ds(pl.multiple_of(core * half, half), half)
    rest = pl.ds(pl.multiple_of((1 - core) * half, half), half)
    here = pl.ds(pl.multiple_of((head_ref[0] ^ slot) * rows, rows), rows)
    q = q_ref[here, :]

    def mixed(ref):
        gate = dot(q, ref[0])
        up = dot(q, ref[2])
        return (gate * jax.nn.sigmoid(gate) * up).astype(jnp.bfloat16)

    first, second = mixed(mine_ref), mixed(other_ref)
    for ref, at in ((mine_ref, own), (other_ref, rest)):
        fast = dot(first, ref[1, own, :]) + dot(second, ref[1, rest, :])
        out_ref[:, at] = (fast + seen_ref[here, at]).astype(jnp.bfloat16)


def apply_fast(slot, core, head, queries, seen, mine, other, rows):
    return pl.pallas_call(
        functools.partial(apply_kernel, slot),
        out_shape=pltpu.VMEM((rows, queries.shape[1]), jnp.bfloat16),
        compiler_params=grant(16),
        in_specs=[SMEM] * 2 + [VMEM] * 4,
        out_specs=VMEM,
        name="apply",
    )(core, head, *near_core(queries, seen, mine, other))


def own_project_kernel(x_ref, gain_ref, w_ref, out_ref, squares_ref):
    wide = x_ref[...].astype(jnp.float32)
    squares_ref[...] = jnp.sum(wide * wide, axis=1, keepdims=True)
    x = (wide * gain_ref[...].astype(jnp.float32)).astype(jnp.bfloat16)
    out_ref[...] = dot(x, w_ref[...])


def own_project(x, gain, weight):
    return pl.pallas_call(
        own_project_kernel,
        out_shape=(
            pltpu.VMEM((x.shape[0], weight.shape[1]), jnp.float32),
            pltpu.VMEM((x.shape[0], 1), jnp.float32),
        ),
        compiler_params=grant(16),
        in_specs=[VMEM] * 3,
        out_specs=(VMEM, VMEM),
        name="own_project",
    )(*near_core(x), gain, weight)


def project_kernel(last, scale_by, part_ref, x_ref, base_ref, squares_ref, near, near_c, far, far_c, *outs):
    rows = near.shape[1]
    columns = near.shape[2]
    wide = x_ref[...].astype(jnp.float32)
    squares = squares_ref[...] + jnp.sum(wide * wide, axis=1, keepdims=True)
    x_near = x_ref[:, pl.ds(pl.multiple_of(part_ref[0] * rows, rows), rows)]
    x_far = x_ref[:, pl.ds(pl.multiple_of((1 - part_ref[0]) * rows, rows), rows)]
    scale = lax.rsqrt(squares * scale_by + EPSILON)
    for side, (w_near, w_far) in enumerate(((near, far), (near_c, far_c))):
        start = part_ref[1] if side == 0 else 1 - part_ref[1]
        block = columns // 2
        for j in range(2):
            at = pl.ds(pl.multiple_of(start * columns + j * block, block), block)
            here = slice(j * block, (j + 1) * block)
            total = base_ref[:, at] + dot(x_near, w_near[0, :, here]) + dot(x_far, w_far[0, :, here])
            outs[0][:, at] = (total * scale).astype(outs[0].dtype) if last else total
    if not last:
        outs[1][...] = squares


def project(last, scale_by, part, x, base, squares, index, pieces):
    rows, columns = base.shape
    shape = jax.ShapeDtypeStruct((rows, columns), jnp.bfloat16)
    if not last:
        shape = (pltpu.VMEM((rows, columns), jnp.float32), pltpu.VMEM((rows, 1), jnp.float32))
    return pl.pallas_call(
        functools.partial(select_piece, functools.partial(project_kernel, last, scale_by), index),
        out_shape=shape,
        in_specs=[SMEM] + [VMEM] * 7,
        out_specs=VMEM if last else (VMEM, VMEM),
        compiler_params=grant(16),
        name="project",
    )(part, *near_core(x, base, squares, *pieces))


def select_piece(kernel, index, part_ref, x_ref, base_ref, squares_ref, *refs):
    pieces = [ref.at[pl.ds(index, 1)] for ref in refs[:4]]
    kernel(part_ref, x_ref, base_ref, squares_ref, *pieces, *refs[4:])


def step(queries, keys, values, rates, fast_w1, fast_w2, fast_w3, norm_gain, out_weight):
    tok_rows, width = queries.shape
    ctx_count = lax.axis_size("ctx")
    heads = lax.axis_size("head")
    me = lax.axis_index("ctx").astype(jnp.int32)
    head = lax.axis_index("head").astype(jnp.int32)
    bits = ctx_count.bit_length() - 1
    assert ctx_count == 1 << bits and bits >= 3
    core = me & 1
    parity = ((me >> 1) ^ (me >> 2)) & 1
    core1 = core.reshape(1)
    part = jnp.stack([parity, core])
    gain = norm_gain.reshape(1, width)

    tail, piece = prepare(part, keys, values, gain, out_weight)
    tail = lax.ppermute(tail, "ctx", [(i, i + 1) for i in range(ctx_count - 1)])

    near = {0: piece}
    for level in reversed(range(heads.bit_length() - 1)):
        for k in sorted(near):
            near[k | 1 << level] = swap(near[k], "head", 1 << level)

    give, keep = pushes(core1, keys, values, rates, fast_w1, fast_w2, fast_w3)
    got = [swap(give, "ctx", 1)]
    masks = [1 << b for b in range(1, bits)]
    for forward, backward in zip(masks, masks[::-1]):
        keep, first, second = add(keep, *got)
        got = []
        got.append(swap(first, "ctx", forward))
        got.append(swap(second, "ctx", backward))
    mine = renorm(core1, keep, *got, fast_w1, fast_w2, fast_w3)
    other = swap(mine, "ctx", 1)

    seen = window(me.reshape(1), queries, keys, values, tail)

    early = jnp.stack([near[k] for k in range(1, heads - 1)])
    late = near[heads - 1].reshape(1, *piece.shape)
    cross = [(i, i ^ (4 if i & 1 else 2)) for i in range(ctx_count)]
    pieces = []
    for group in (early, late):
        far = lax.ppermute(group, "ctx", cross)
        near_c = swap(group, "ctx", 1)
        far_c = swap(far, "ctx", 1)
        pieces.append((group, near_c, far, far_c))

    rows = tok_rows // heads
    blocks = [None] * heads
    for k in list(range(heads - 1, 0, -1)) + [0]:
        combined = apply_fast(k, core1, head.reshape(1), queries, seen, mine, other, rows)
        blocks[k] = swap(combined, "head", k) if k else combined
    base, squares = own_project(blocks[0], gain, out_weight)
    scale_by = 1.0 / (heads * width)
    for k in range(heads - 1, 0, -1):
        which = pieces[1] if k == heads - 1 else pieces[0]
        index = 0 if k == heads - 1 else k - 1
        result = project(k == 1, scale_by, part, blocks[k], base, squares, index, which)
        if k > 1:
            base, squares = result
    return result


def solution(mesh):
    placed = (
        P("ctx", "head"),
        P("ctx", "head"),
        P("ctx", "head"),
        P("ctx", "head"),
        P("head", None, None),
        P("head", None, None),
        P("head", None, None),
        P("head"),
        P("head", None),
    )
    return jax.shard_map(
        step, mesh=mesh, in_specs=placed, out_specs=P(("ctx", "head"), None), check_vma=False
    )
```

```python
import functools
import math

import jax
import jax.numpy as jnp
from jax import lax
from jax.experimental import pallas as pl
from jax.experimental.pallas import tpu as pltpu
from jax.sharding import PartitionSpec as P


WINDOW = 256
EPSILON = 1e-06

VMEM = pl.BlockSpec(memory_space=pltpu.VMEM)
HBM = pl.BlockSpec(memory_space=pltpu.HBM)


def near_core(*arrays):
    return [pltpu.with_memory_space_constraint(a, pltpu.VMEM) for a in arrays]


def far_core(*arrays):
    return [pltpu.with_memory_space_constraint(a, pltpu.HBM) for a in arrays]


def grant(mib):
    return pltpu.CompilerParams(vmem_limit_bytes=mib << 20)


def swap(value, axis, mask):
    return lax.ppermute(value, axis, [(i, i ^ mask) for i in range(lax.axis_size(axis))])


def dot(left, right, left_dim=1, right_dim=0):
    return lax.dot_general(
        left, right, (((left_dim,), (right_dim,)), ((), ())), preferred_element_type=jnp.float32
    )


def place():
    me = lax.axis_index("ctx").astype(jnp.int32)
    return me & 1, ((me >> 1) ^ (me >> 2)) & 1


def column(row, width):
    tall = jnp.transpose(jnp.broadcast_to(row, (128, row.shape[1])))
    return jnp.concatenate([tall] * (width // 128), axis=1)


def load_kernel(k_hbm, v_hbm, w1_hbm, w2_hbm, w3_hbm, tail_ref, k_ref, v_ref, w1_ref, w2_ref, w3_ref, sem):
    last = pl.ds(k_hbm.shape[0] - WINDOW, WINDOW)
    moves = [(k_hbm.at[last, :], tail_ref.at[pl.ds(0, WINDOW), :])]
    moves += [(v_hbm.at[last, :], tail_ref.at[pl.ds(WINDOW, WINDOW), :])]
    moves += [(w1_hbm, w1_ref), (w3_hbm, w3_ref), (k_hbm, k_ref), (v_hbm, v_ref), (w2_hbm, w2_ref)]
    copies = [pltpu.make_async_copy(src, dst, sem.at[j]) for j, (src, dst) in enumerate(moves)]
    for copy in copies:
        copy.start()
    for copy in copies:
        copy.wait()


def load(keys, values, w1, w2, w3):
    arrays = (keys, values, w1, w2, w3)
    return pl.pallas_call(
        load_kernel,
        out_shape=[pltpu.VMEM((2 * WINDOW, keys.shape[1]), jnp.bfloat16)]
        + [pltpu.VMEM(a.shape, a.dtype) for a in arrays],
        compiler_params=grant(4),
        in_specs=[HBM] * 5,
        out_specs=[VMEM] * 6,
        scratch_shapes=[pltpu.SemaphoreType.DMA((7,))],
        name="load",
    )(*far_core(*arrays))


def push_kernel(k_ref, v_ref, r_ref, w1_ref, w2_ref, w3_ref, gain_ref, w_hbm,
                give_ref, keep_ref, piece_ref, act_ref, g1_ref, g3_ref, sc_ref, w_ref, sem):
    rows, width = k_ref.shape
    piece_rows, columns = piece_ref.shape
    core, side = place()
    first = pl.multiple_of(side * piece_rows, piece_rows)
    left = pl.multiple_of(core * columns, columns)
    load = pltpu.make_async_copy(w_hbm.at[pl.ds(first, piece_rows), pl.ds(left, columns)], w_ref, sem)
    load.start()
    steps = 4
    block = rows // steps
    half = width // 2
    for i in range(steps):
        at = slice(i * block, (i + 1) * block)
        k = k_ref[at, :]
        gate = dot(k, w1_ref[0])
        up = dot(k, w3_ref[0])
        rate = column(r_ref[:, at], width)
        scaled = (v_ref[at, :].astype(jnp.float32) * rate).astype(jnp.bfloat16)
        back = dot(scaled, w2_ref[0], 1, 1)
        s = jax.nn.sigmoid(gate)
        gs = gate * s
        act_ref[at, :] = (gs * up).astype(jnp.bfloat16)
        sc_ref[at, :] = scaled
        g1_ref[at, :] = (back * up * (s + gs * (1.0 - s))).astype(jnp.bfloat16)
        g3_ref[at, :] = (back * gs).astype(jnp.bfloat16)
    load.wait()
    gain = gain_ref[...].reshape(1, width).astype(jnp.float32)
    gain = jnp.where(side == 0, gain[:, :piece_rows], gain[:, piece_rows:])
    piece_ref[...] = (w_ref[...].astype(jnp.float32) * column(gain, columns)).astype(jnp.bfloat16)
    theirs = pl.ds(pl.multiple_of((1 - core) * half, half), half)
    mine = pl.ds(pl.multiple_of(core * half, half), half)
    for j, (left, right) in enumerate([(k_ref, g1_ref), (act_ref, sc_ref), (k_ref, g3_ref)]):
        left = left[...]
        give_ref[j] = dot(left, right[:, theirs], 0, 0).astype(jnp.bfloat16)
        keep_ref[j] = dot(left, right[:, mine], 0, 0)


def pushes(keys, values, rates, w1, w2, w3, gain, weight):
    rows, width = keys.shape
    half = width // 2
    wide = pltpu.VMEM((rows, width), jnp.bfloat16)
    piece = pltpu.VMEM((weight.shape[0] // 2, weight.shape[1] // 2), jnp.bfloat16)
    return pl.pallas_call(
        push_kernel,
        out_shape=(
            pltpu.VMEM((3, width, half), jnp.bfloat16),
            pltpu.VMEM((3, width, half), jnp.float32),
            piece,
        ),
        compiler_params=grant(16),
        in_specs=[VMEM] * 7 + [HBM],
        out_specs=(VMEM,) * 3,
        scratch_shapes=[wide] * 4 + [piece, pltpu.SemaphoreType.DMA],
        name="pushes",
    )(*near_core(keys, values, rates.reshape(1, rows), w1, w2, w3, gain), *far_core(weight))


def add_kernel(keep_ref, got_ref, sum_ref, send_ref):
    total = keep_ref[...] + got_ref[...].astype(jnp.float32)
    sum_ref[...] = total
    send_ref[...] = total.astype(jnp.bfloat16)


def add(keep, got):
    return pl.pallas_call(
        add_kernel,
        out_shape=(pltpu.VMEM(keep.shape, jnp.float32), pltpu.VMEM(keep.shape, jnp.bfloat16)),
        compiler_params=grant(8),
        in_specs=[VMEM] * 2,
        out_specs=(VMEM,) * 2,
        name="add",
    )(*near_core(keep, got))


def renorm_kernel(keep_ref, got_ref, w1_ref, w2_ref, w3_ref, out_ref):
    _, half = got_ref.shape[1:]
    block = 128
    core, _ = place()
    for j, w_ref in enumerate((w1_ref, w2_ref, w3_ref)):
        for first in range(0, half, block):
            at = slice(first, first + block)
            start = pl.multiple_of(core * half + first, block)
            old = w_ref[0, :, pl.ds(start, block)].astype(jnp.float32)
            new = old + (keep_ref[j, :, at] + got_ref[j, :, at].astype(jnp.float32))
            old_norm = jnp.sqrt(jnp.mean(old * old, axis=0, keepdims=True) + EPSILON)
            new_norm = jnp.sqrt(jnp.mean(new * new, axis=0, keepdims=True) + EPSILON)
            out_ref[j, :, at] = (new * (old_norm / new_norm)).astype(jnp.bfloat16)


def renorm(keep, got, w1, w2, w3):
    return pl.pallas_call(
        renorm_kernel,
        out_shape=pltpu.VMEM(keep.shape, jnp.bfloat16),
        compiler_params=grant(8),
        in_specs=[VMEM] * 5,
        out_specs=VMEM,
        name="renorm",
    )(*near_core(keep, got, w1, w2, w3))


def window_kernel(q_hbm, k_hbm, v_hbm, tail_ref, out_ref, q_ref, k_ref, v_ref, sem):
    rows, width = q_ref.shape
    scale = 1.0 / math.sqrt(width)
    query = lax.broadcasted_iota(jnp.int32, (WINDOW, 2 * WINDOW), 0)
    key = lax.broadcasted_iota(jnp.int32, (WINDOW, 2 * WINDOW), 1)
    allowed = (key > query) & (key <= query + WINDOW)
    allowed_first = allowed & ((key >= WINDOW) | (lax.axis_index("ctx") > 0))
    count = rows // WINDOW
    loads = [[
        pltpu.make_async_copy(tail_ref.at[pl.ds(j * WINDOW, WINDOW), :], dst.at[pl.ds(0, WINDOW), :], sem.at[j])
        for j, dst in enumerate((k_ref, v_ref))
    ]]
    for i in range(count):
        at, after = pl.ds(i * WINDOW, WINDOW), pl.ds((i + 1) * WINDOW, WINDOW)
        loads.append([
            pltpu.make_async_copy(q_hbm.at[at, :], q_ref.at[at, :], sem.at[3 * i + 2]),
            pltpu.make_async_copy(k_hbm.at[at, :], k_ref.at[after, :], sem.at[3 * i + 3]),
            pltpu.make_async_copy(v_hbm.at[at, :], v_ref.at[after, :], sem.at[3 * i + 4]),
        ])
    for group in loads:
        for load in group:
            load.start()
    for load in loads[0]:
        load.wait()
    for i in range(count):
        for load in loads[i + 1]:
            load.wait()
        at = slice(i * WINDOW, (i + 1) * WINDOW)
        seen = slice(i * WINDOW, (i + 2) * WINDOW)
        scores = dot(q_ref[at, :], k_ref[seen, :], 1, 1) * scale
        scores = jnp.where(allowed_first if i == 0 else allowed, scores, -jnp.inf)
        peak = jnp.max(scores, axis=1, keepdims=True)
        exponent = jnp.exp(scores - peak)
        weights = exponent / jnp.sum(exponent, axis=1, keepdims=True)
        out_ref[at, :] = dot(weights.astype(jnp.bfloat16), v_ref[seen, :])


def window(queries, keys, values, tail):
    rows, width = queries.shape
    return pl.pallas_call(
        window_kernel,
        out_shape=pltpu.VMEM(queries.shape, jnp.float32),
        compiler_params=grant(24),
        in_specs=[HBM] * 3 + [VMEM],
        out_specs=VMEM,
        scratch_shapes=[pltpu.VMEM((rows, width), jnp.bfloat16)]
        + [pltpu.VMEM((rows + WINDOW, width), jnp.bfloat16)] * 2
        + [pltpu.SemaphoreType.DMA((2 + 3 * (rows // WINDOW),))],
        name="window",
    )(*far_core(queries, keys, values), *near_core(tail))


def apply_kernel(slot, q_ref, seen_ref, mine_ref, other_ref, out_ref):
    rows = out_ref.shape[0]
    half = mine_ref.shape[2]
    core, _ = place()
    own = pl.ds(pl.multiple_of(core * half, half), half)
    rest = pl.ds(pl.multiple_of((1 - core) * half, half), half)
    here = pl.ds(pl.multiple_of((lax.axis_index("head").astype(jnp.int32) ^ slot) * rows, rows), rows)
    q = q_ref[here, :]

    mixed = []
    for ref in (mine_ref, other_ref):
        gate = dot(q, ref[0])
        up = dot(q, ref[2])
        mixed.append((gate * jax.nn.sigmoid(gate) * up).astype(jnp.bfloat16))
    mixed = jnp.concatenate(mixed, axis=1)
    for ref, at in ((mine_ref, own), (other_ref, rest)):
        down = jnp.concatenate([ref[1, own, :], ref[1, rest, :]], axis=0)
        out_ref[:, at] = (dot(mixed, down) + seen_ref[here, at]).astype(jnp.bfloat16)


def apply_fast(slot, queries, seen, mine, other, rows):
    return pl.pallas_call(
        functools.partial(apply_kernel, slot),
        out_shape=pltpu.VMEM((rows, queries.shape[1]), jnp.bfloat16),
        compiler_params=grant(16),
        in_specs=[VMEM] * 4,
        out_specs=VMEM,
        name="apply",
    )(*near_core(queries, seen, mine, other))


def own_project_kernel(x_ref, gain_ref, w_ref, out_ref, squares_ref):
    wide = x_ref[...].astype(jnp.float32)
    squares_ref[...] = jnp.sum(wide * wide, axis=1, keepdims=True)
    gain = gain_ref[...].reshape(1, wide.shape[1]).astype(jnp.float32)
    x = (wide * gain).astype(jnp.bfloat16)
    out_ref[...] = dot(x, w_ref[...])


def own_project(x, gain, weight):
    return pl.pallas_call(
        own_project_kernel,
        out_shape=(
            pltpu.VMEM((x.shape[0], weight.shape[1]), jnp.float32),
            pltpu.VMEM((x.shape[0], 1), jnp.float32),
        ),
        compiler_params=grant(16),
        in_specs=[VMEM] * 3,
        out_specs=(VMEM, VMEM),
        name="own_project",
    )(*near_core(x, gain, weight))


def pile_kernel(*refs):
    *ins, out_ref, sem = refs
    copies = [pltpu.make_async_copy(src, out_ref.at[j], sem.at[j]) for j, src in enumerate(ins)]
    for copy in copies:
        copy.start()
    for copy in copies:
        copy.wait()


def pile(*arrays):
    return pl.pallas_call(
        pile_kernel,
        out_shape=pltpu.VMEM((len(arrays),) + arrays[0].shape, arrays[0].dtype),
        compiler_params=grant(4),
        in_specs=[VMEM] * len(arrays),
        out_specs=VMEM,
        scratch_shapes=[pltpu.SemaphoreType.DMA((len(arrays),))],
        name="pile",
    )(*near_core(*arrays))


def project_kernel(index, scale_by, x_ref, base_ref, squares_ref, near, near_c, far, far_c,
                   out_ref, *rest):
    rows, columns = near.shape[1:]
    core, half = place()
    wide = x_ref[...].astype(jnp.float32)
    squares = squares_ref[...] + jnp.sum(wide * wide, axis=1, keepdims=True)
    mine = pl.ds(pl.multiple_of(half * rows, rows), rows)
    theirs = pl.ds(pl.multiple_of((1 - half) * rows, rows), rows)
    x = jnp.concatenate([x_ref[:, mine], x_ref[:, theirs]], axis=1)
    scale = lax.rsqrt(squares * scale_by + EPSILON) if scale_by else None
    block = columns // 2
    stores = []
    for side, (w_near, w_far) in enumerate(((near, far), (near_c, far_c))):
        start = core if side == 0 else 1 - core
        for j in range(2):
            at = pl.ds(pl.multiple_of(start * columns + j * block, block), block)
            here = slice(j * block, (j + 1) * block)
            w = jnp.concatenate([w_near[index, :, here], w_far[index, :, here]], axis=0)
            total = base_ref[:, at] + dot(x, w)
            if scale_by:
                ready_ref, sem = rest
                ready_ref[2 * side + j] = (total * scale).astype(jnp.bfloat16)
                store = pltpu.make_async_copy(ready_ref.at[2 * side + j], out_ref.at[:, at], sem.at[2 * side + j])
                store.start()
                stores.append(store)
            else:
                out_ref[:, at] = total
    if not scale_by:
        rest[0][...] = squares
    for store in stores:
        store.wait()


def project(index, scale_by, x, base, squares, pieces):
    rows, columns = base.shape
    if scale_by:
        shape = jax.ShapeDtypeStruct((rows, columns), jnp.bfloat16)
        scratch = [pltpu.VMEM((4, rows, columns // 4), jnp.bfloat16), pltpu.SemaphoreType.DMA((4,))]
    else:
        shape = (pltpu.VMEM((rows, columns), jnp.float32), pltpu.VMEM((rows, 1), jnp.float32))
        scratch = []
    return pl.pallas_call(
        functools.partial(project_kernel, index, scale_by),
        out_shape=shape,
        in_specs=[VMEM] * 7,
        out_specs=HBM if scale_by else (VMEM, VMEM),
        scratch_shapes=scratch,
        compiler_params=grant(16),
        name="project",
    )(*near_core(x, base, squares, *pieces))


def step(queries, keys, values, rates, fast_w1, fast_w2, fast_w3, norm_gain, out_weight):
    tok_rows, width = queries.shape
    ctx_count = lax.axis_size("ctx")
    heads = lax.axis_size("head")
    bits = ctx_count.bit_length() - 1
    assert ctx_count == 1 << bits and bits >= 3

    tail, *loaded = load(keys, values, fast_w1, fast_w2, fast_w3)
    tail = lax.ppermute(tail, "ctx", [(i, i + 1) for i in range(ctx_count - 1)])
    give, keep, piece = pushes(
        loaded[0], loaded[1], rates, *loaded[2:], norm_gain, out_weight
    )
    got = swap(give, "ctx", 1)

    near = {0: piece}
    for level in reversed(range(heads.bit_length() - 1)):
        for k in sorted(near):
            near[k | 1 << level] = swap(near[k], "head", 1 << level)

    masks = [1 << b for b in range(1, bits)]
    crossing = [
        [(i, i ^ (backward if i & 1 else forward)) for i in range(ctx_count)]
        for forward, backward in zip(masks, masks[::-1])
    ]
    for pairs in crossing:
        keep, send = add(keep, got)
        got = lax.ppermute(send, "ctx", pairs)
    mine = renorm(keep, got, fast_w1, fast_w2, fast_w3)
    other = swap(mine, "ctx", 1)

    seen = window(queries, keys, values, tail)

    early = pile(*(near[k] for k in range(1, heads - 1)))
    late = near[heads - 1].reshape(1, *piece.shape)
    cross = [(i, i ^ (4 if i & 1 else 2)) for i in range(ctx_count)]
    pieces = []
    for group in (early, late):
        far = lax.ppermute(group, "ctx", cross)
        near_c = swap(group, "ctx", 1)
        far_c = swap(far, "ctx", 1)
        pieces.append((group, near_c, far, far_c))

    rows = tok_rows // heads
    blocks = {}
    for k in send_order(heads) + [0]:
        combined = apply_fast(k, queries, seen, mine, other, rows)
        blocks[k] = swap(combined, "head", k) if k else combined
    base, squares = own_project(blocks[0], norm_gain, out_weight)
    for k in send_order(heads):
        late_one = k == heads - 1
        index, which = (0, pieces[1]) if late_one else (k - 1, pieces[0])
        scale_by = 1.0 / (heads * width) if k == send_order(heads)[-1] else None
        result = project(index, scale_by, blocks[k], base, squares, which)
        if scale_by is None:
            base, squares = result
    return result


def send_order(heads):
    return [heads - 1] + list(range(1, heads - 1))


def solution(mesh):
    placed = (
        P("ctx", "head"),
        P("ctx", "head"),
        P("ctx", "head"),
        P("ctx", "head"),
        P("head", None, None),
        P("head", None, None),
        P("head", None, None),
        P("head"),
        P("head", None),
    )
    return jax.shard_map(
        step, mesh=mesh, in_specs=placed, out_specs=P(("ctx", "head"), None), check_vma=False
    )
```

```python
import functools
import math

import jax
import jax.numpy as jnp
from jax import lax
from jax.experimental import pallas as pl
from jax.experimental.pallas import tpu as pltpu
from jax.sharding import PartitionSpec as P


WINDOW = 256
EPSILON = 1e-06

VMEM = pl.BlockSpec(memory_space=pltpu.VMEM)
HBM = pl.BlockSpec(memory_space=pltpu.HBM)


def near_core(*arrays):
    return [pltpu.with_memory_space_constraint(a, pltpu.VMEM) for a in arrays]


def far_core(*arrays):
    return [pltpu.with_memory_space_constraint(a, pltpu.HBM) for a in arrays]


def grant(mib):
    return pltpu.CompilerParams(vmem_limit_bytes=mib << 20)


def swap(value, axis, mask):
    return lax.ppermute(value, axis, [(i, i ^ mask) for i in range(lax.axis_size(axis))])


def dot(left, right, left_dim=1, right_dim=0):
    return lax.dot_general(
        left, right, (((left_dim,), (right_dim,)), ((), ())), preferred_element_type=jnp.float32
    )


def place():
    me = lax.axis_index("ctx").astype(jnp.int32)
    return me & 1, ((me >> 1) ^ (me >> 2)) & 1


def column(row, width):
    tall = jnp.transpose(jnp.broadcast_to(row, (128, row.shape[1])))
    return jnp.concatenate([tall] * (width // 128), axis=1)


def load_kernel(k_hbm, v_hbm, w1_hbm, w2_hbm, w3_hbm, gain_hbm, w_hbm,
                tail_ref, piece_ref, k_ref, v_ref, w1_ref, w2_ref, w3_ref, w_ref, gain_ref, sem):
    rows, columns = piece_ref.shape
    core, side = place()
    first = pl.multiple_of(side * rows, rows)
    left = pl.multiple_of(core * columns, columns)
    last = pl.ds(k_hbm.shape[0] - WINDOW, WINDOW)
    moves = [(gain_hbm, gain_ref), (w_hbm.at[pl.ds(first, rows), pl.ds(left, columns)], w_ref)]
    moves += [(k_hbm.at[last, :], tail_ref.at[pl.ds(0, WINDOW), :])]
    moves += [(v_hbm.at[last, :], tail_ref.at[pl.ds(WINDOW, WINDOW), :])]
    moves += [(w1_hbm, w1_ref), (w3_hbm, w3_ref), (k_hbm, k_ref), (v_hbm, v_ref), (w2_hbm, w2_ref)]
    copies = [pltpu.make_async_copy(src, dst, sem.at[j]) for j, (src, dst) in enumerate(moves)]
    for copy in copies:
        copy.start()
    copies[0].wait()
    gain = gain_ref[...].reshape(1, 2 * rows).astype(jnp.float32)
    gain = column(jnp.where(side == 0, gain[:, :rows], gain[:, rows:]), columns)
    copies[1].wait()
    piece_ref[...] = (w_ref[...].astype(jnp.float32) * gain).astype(jnp.bfloat16)
    for copy in copies[2:]:
        copy.wait()


def load(keys, values, w1, w2, w3, gain, weight):
    arrays = (keys, values, w1, w2, w3)
    piece = pltpu.VMEM((weight.shape[0] // 2, weight.shape[1] // 2), jnp.bfloat16)
    return pl.pallas_call(
        load_kernel,
        out_shape=[pltpu.VMEM((2 * WINDOW, keys.shape[1]), jnp.bfloat16), piece]
        + [pltpu.VMEM(a.shape, a.dtype) for a in arrays],
        compiler_params=grant(8),
        in_specs=[HBM] * 7,
        out_specs=[VMEM] * 7,
        scratch_shapes=[piece, pltpu.VMEM(gain.shape, gain.dtype), pltpu.SemaphoreType.DMA((9,))],
        name="load",
    )(*far_core(*arrays, gain, weight))


def halves(width):
    core, _ = place()
    half = width // 2
    mine = pl.ds(pl.multiple_of(core * half, half), half)
    theirs = pl.ds(pl.multiple_of((1 - core) * half, half), half)
    return mine, theirs


def push_kernel(k_ref, v_ref, r_ref, w1_ref, w2_ref, w3_ref, give_ref, act_ref, sc_ref, g1_ref, g3_ref):
    rows, width = k_ref.shape
    steps = 4
    block = rows // steps
    for i in range(steps):
        at = slice(i * block, (i + 1) * block)
        k = k_ref[at, :]
        gate = dot(k, w1_ref[0])
        up = dot(k, w3_ref[0])
        rate = column(r_ref[:, at], width)
        scaled = (v_ref[at, :].astype(jnp.float32) * rate).astype(jnp.bfloat16)
        back = dot(scaled, w2_ref[0], 1, 1)
        s = jax.nn.sigmoid(gate)
        gs = gate * s
        act_ref[at, :] = (gs * up).astype(jnp.bfloat16)
        sc_ref[at, :] = scaled
        g1_ref[at, :] = (back * up * (s + gs * (1.0 - s))).astype(jnp.bfloat16)
        g3_ref[at, :] = (back * gs).astype(jnp.bfloat16)
    _, theirs = halves(width)
    for j, (left, right) in enumerate([(k_ref, g1_ref), (act_ref, sc_ref), (k_ref, g3_ref)]):
        give_ref[j] = dot(left[...], right[:, theirs], 0, 0).astype(jnp.bfloat16)


def pushes(keys, values, rates, w1, w2, w3):
    rows, width = keys.shape
    wide = pltpu.VMEM((rows, width), jnp.bfloat16)
    return pl.pallas_call(
        push_kernel,
        out_shape=[pltpu.VMEM((3, width, width // 2), jnp.bfloat16)] + [wide] * 4,
        compiler_params=grant(16),
        in_specs=[VMEM] * 6,
        out_specs=[VMEM] * 5,
        name="pushes",
    )(*near_core(keys, values, rates.reshape(1, rows), w1, w2, w3))


def keep_kernel(k_ref, act_ref, sc_ref, g1_ref, g3_ref, keep_ref):
    mine, _ = halves(k_ref.shape[1])
    for j, (left, right) in enumerate([(k_ref, g1_ref), (act_ref, sc_ref), (k_ref, g3_ref)]):
        keep_ref[j] = dot(left[...], right[:, mine], 0, 0)


def kept(*arrays):
    width = arrays[0].shape[1]
    return pl.pallas_call(
        keep_kernel,
        out_shape=pltpu.VMEM((3, width, width // 2), jnp.float32),
        compiler_params=grant(16),
        in_specs=[VMEM] * 5,
        out_specs=VMEM,
        name="kept",
    )(*near_core(*arrays))


def first_add_kernel(keep_ref, got_ref, sum_ref, a_ref, b_ref):
    quarter = a_ref.shape[2]
    total = keep_ref[...] + got_ref[...].astype(jnp.float32)
    sum_ref[...] = total
    a_ref[...] = total[:, :, :quarter].astype(jnp.bfloat16)
    b_ref[...] = total[:, :, quarter:].astype(jnp.bfloat16)


def later_add_kernel(keep_ref, got_a_ref, got_b_ref, sum_ref, a_ref, b_ref):
    quarter = a_ref.shape[2]
    first = keep_ref[:, :, :quarter] + got_a_ref[...].astype(jnp.float32)
    second = keep_ref[:, :, quarter:] + got_b_ref[...].astype(jnp.float32)
    sum_ref[:, :, :quarter] = first
    sum_ref[:, :, quarter:] = second
    a_ref[...] = first.astype(jnp.bfloat16)
    b_ref[...] = second.astype(jnp.bfloat16)


def add(keep, *got):
    stream = pltpu.VMEM(keep.shape[:2] + (keep.shape[2] // 2,), jnp.bfloat16)
    return pl.pallas_call(
        first_add_kernel if len(got) == 1 else later_add_kernel,
        out_shape=(pltpu.VMEM(keep.shape, jnp.float32), stream, stream),
        compiler_params=grant(8),
        in_specs=[VMEM] * (1 + len(got)),
        out_specs=(VMEM,) * 3,
        name="add",
    )(*near_core(keep, *got))


def renorm_kernel(keep_ref, got_a_ref, got_b_ref, w1_ref, w2_ref, w3_ref, out_ref):
    half = keep_ref.shape[2]
    block = got_a_ref.shape[2]
    core, _ = place()
    for j, w_ref in enumerate((w1_ref, w2_ref, w3_ref)):
        for first, got_ref in ((0, got_a_ref), (block, got_b_ref)):
            at = slice(first, first + block)
            start = pl.multiple_of(core * half + first, block)
            old = w_ref[0, :, pl.ds(start, block)].astype(jnp.float32)
            new = old + (keep_ref[j, :, at] + got_ref[j].astype(jnp.float32))
            old_norm = jnp.sqrt(jnp.mean(old * old, axis=0, keepdims=True) + EPSILON)
            new_norm = jnp.sqrt(jnp.mean(new * new, axis=0, keepdims=True) + EPSILON)
            out_ref[j, :, at] = (new * (old_norm / new_norm)).astype(jnp.bfloat16)


def renorm(keep, *others):
    return pl.pallas_call(
        renorm_kernel,
        out_shape=pltpu.VMEM(keep.shape, jnp.bfloat16),
        compiler_params=grant(8),
        in_specs=[VMEM] * 6,
        out_specs=VMEM,
        name="renorm",
    )(*near_core(keep, *others))


def window_kernel(q_hbm, k_hbm, v_hbm, tail_ref, out_ref, q_ref, k_ref, v_ref, sem):
    rows, width = q_ref.shape
    scale = 1.0 / math.sqrt(width)
    query = lax.broadcasted_iota(jnp.int32, (WINDOW, 2 * WINDOW), 0)
    key = lax.broadcasted_iota(jnp.int32, (WINDOW, 2 * WINDOW), 1)
    allowed = (key > query) & (key <= query + WINDOW)
    allowed_first = allowed & ((key >= WINDOW) | (lax.axis_index("ctx") > 0))
    count = rows // WINDOW
    loads = [[
        pltpu.make_async_copy(tail_ref.at[pl.ds(j * WINDOW, WINDOW), :], dst.at[pl.ds(0, WINDOW), :], sem.at[j])
        for j, dst in enumerate((k_ref, v_ref))
    ]]
    for i in range(count):
        at, after = pl.ds(i * WINDOW, WINDOW), pl.ds((i + 1) * WINDOW, WINDOW)
        loads.append([
            pltpu.make_async_copy(q_hbm.at[at, :], q_ref.at[at, :], sem.at[3 * i + 2]),
            pltpu.make_async_copy(k_hbm.at[at, :], k_ref.at[after, :], sem.at[3 * i + 3]),
            pltpu.make_async_copy(v_hbm.at[at, :], v_ref.at[after, :], sem.at[3 * i + 4]),
        ])
    for group in loads:
        for load in group:
            load.start()
    for load in loads[0]:
        load.wait()
    for i in range(count):
        for load in loads[i + 1]:
            load.wait()
        at = slice(i * WINDOW, (i + 1) * WINDOW)
        seen = slice(i * WINDOW, (i + 2) * WINDOW)
        scores = dot(q_ref[at, :], k_ref[seen, :], 1, 1) * scale
        scores = jnp.where(allowed_first if i == 0 else allowed, scores, -jnp.inf)
        peak = jnp.max(scores, axis=1, keepdims=True)
        exponent = jnp.exp(scores - peak)
        weights = exponent / jnp.sum(exponent, axis=1, keepdims=True)
        out_ref[at, :] = dot(weights.astype(jnp.bfloat16), v_ref[seen, :])


def window(queries, keys, values, tail):
    rows, width = queries.shape
    return pl.pallas_call(
        window_kernel,
        out_shape=pltpu.VMEM(queries.shape, jnp.float32),
        compiler_params=grant(24),
        in_specs=[HBM] * 3 + [VMEM],
        out_specs=VMEM,
        scratch_shapes=[pltpu.VMEM((rows, width), jnp.bfloat16)]
        + [pltpu.VMEM((rows + WINDOW, width), jnp.bfloat16)] * 2
        + [pltpu.SemaphoreType.DMA((2 + 3 * (rows // WINDOW),))],
        name="window",
    )(*far_core(queries, keys, values), *near_core(tail))


def apply_kernel(slot, q_ref, seen_ref, mine_ref, other_ref, out_ref):
    rows = out_ref.shape[0]
    half = mine_ref.shape[2]
    core, _ = place()
    own = pl.ds(pl.multiple_of(core * half, half), half)
    rest = pl.ds(pl.multiple_of((1 - core) * half, half), half)
    here = pl.ds(pl.multiple_of((lax.axis_index("head").astype(jnp.int32) ^ slot) * rows, rows), rows)
    q = q_ref[here, :]

    mixed = []
    for ref in (mine_ref, other_ref):
        gate = dot(q, ref[0])
        up = dot(q, ref[2])
        mixed.append((gate * jax.nn.sigmoid(gate) * up).astype(jnp.bfloat16))
    mixed = jnp.concatenate(mixed, axis=1)
    for ref, at in ((mine_ref, own), (other_ref, rest)):
        down = jnp.concatenate([ref[1, own, :], ref[1, rest, :]], axis=0)
        out_ref[:, at] = (dot(mixed, down) + seen_ref[here, at]).astype(jnp.bfloat16)


def apply_fast(slot, queries, seen, mine, other, rows):
    return pl.pallas_call(
        functools.partial(apply_kernel, slot),
        out_shape=pltpu.VMEM((rows, queries.shape[1]), jnp.bfloat16),
        compiler_params=grant(16),
        in_specs=[VMEM] * 4,
        out_specs=VMEM,
        name="apply",
    )(*near_core(queries, seen, mine, other))


def own_project_kernel(x_ref, gain_ref, w_ref, out_ref, squares_ref):
    wide = x_ref[...].astype(jnp.float32)
    squares_ref[...] = jnp.sum(wide * wide, axis=1, keepdims=True)
    gain = gain_ref[...].reshape(1, wide.shape[1]).astype(jnp.float32)
    x = (wide * gain).astype(jnp.bfloat16)
    out_ref[...] = dot(x, w_ref[...])


def own_project(x, gain, weight):
    return pl.pallas_call(
        own_project_kernel,
        out_shape=(
            pltpu.VMEM((x.shape[0], weight.shape[1]), jnp.float32),
            pltpu.VMEM((x.shape[0], 1), jnp.float32),
        ),
        compiler_params=grant(16),
        in_specs=[VMEM] * 3,
        out_specs=(VMEM, VMEM),
        name="own_project",
    )(*near_core(x, gain, weight))


def pile_kernel(*refs):
    *ins, out_ref, sem = refs
    copies = [pltpu.make_async_copy(src, out_ref.at[j], sem.at[j]) for j, src in enumerate(ins)]
    for copy in copies:
        copy.start()
    for copy in copies:
        copy.wait()


def pile(*arrays):
    return pl.pallas_call(
        pile_kernel,
        out_shape=pltpu.VMEM((len(arrays),) + arrays[0].shape, arrays[0].dtype),
        compiler_params=grant(4),
        in_specs=[VMEM] * len(arrays),
        out_specs=VMEM,
        scratch_shapes=[pltpu.SemaphoreType.DMA((len(arrays),))],
        name="pile",
    )(*near_core(*arrays))


def project_kernel(index, scale_by, x_ref, base_ref, squares_ref, near, near_c, far, far_c,
                   out_ref, *rest):
    rows, columns = near.shape[1:]
    core, half = place()
    wide = x_ref[...].astype(jnp.float32)
    squares = squares_ref[...] + jnp.sum(wide * wide, axis=1, keepdims=True)
    mine = pl.ds(pl.multiple_of(half * rows, rows), rows)
    theirs = pl.ds(pl.multiple_of((1 - half) * rows, rows), rows)
    x = jnp.concatenate([x_ref[:, mine], x_ref[:, theirs]], axis=1)
    scale = lax.rsqrt(squares * scale_by + EPSILON) if scale_by else None
    block = columns // 2
    stores = []
    for side, (w_near, w_far) in enumerate(((near, far), (near_c, far_c))):
        start = core if side == 0 else 1 - core
        for j in range(2):
            at = pl.ds(pl.multiple_of(start * columns + j * block, block), block)
            here = slice(j * block, (j + 1) * block)
            w = jnp.concatenate([w_near[index, :, here], w_far[index, :, here]], axis=0)
            total = base_ref[:, at] + dot(x, w)
            if scale_by:
                ready_ref, sem = rest
                ready_ref[2 * side + j] = (total * scale).astype(jnp.bfloat16)
                store = pltpu.make_async_copy(ready_ref.at[2 * side + j], out_ref.at[:, at], sem.at[2 * side + j])
                store.start()
                stores.append(store)
            else:
                out_ref[:, at] = total
    if not scale_by:
        rest[0][...] = squares
    for store in stores:
        store.wait()


def project(index, scale_by, x, base, squares, pieces):
    rows, columns = base.shape
    if scale_by:
        shape = jax.ShapeDtypeStruct((rows, columns), jnp.bfloat16)
        scratch = [pltpu.VMEM((4, rows, columns // 4), jnp.bfloat16), pltpu.SemaphoreType.DMA((4,))]
    else:
        shape = (pltpu.VMEM((rows, columns), jnp.float32), pltpu.VMEM((rows, 1), jnp.float32))
        scratch = []
    return pl.pallas_call(
        functools.partial(project_kernel, index, scale_by),
        out_shape=shape,
        in_specs=[VMEM] * 7,
        out_specs=HBM if scale_by else (VMEM, VMEM),
        scratch_shapes=scratch,
        compiler_params=grant(16),
        name="project",
    )(*near_core(x, base, squares, *pieces))


def step(queries, keys, values, rates, fast_w1, fast_w2, fast_w3, norm_gain, out_weight):
    tok_rows, width = queries.shape
    ctx_count = lax.axis_size("ctx")
    heads = lax.axis_size("head")
    bits = ctx_count.bit_length() - 1
    assert ctx_count == 1 << bits and bits >= 3

    tail, piece, k_near, *loaded = load(
        keys, values, fast_w1, fast_w2, fast_w3, norm_gain, out_weight
    )
    tail = lax.ppermute(tail, "ctx", [(i, i + 1) for i in range(ctx_count - 1)])

    near = {0: piece}
    for level in reversed(range(heads.bit_length() - 1)):
        for k in sorted(near):
            near[k | 1 << level] = swap(near[k], "head", 1 << level)

    give, *factors = pushes(k_near, loaded[0], rates, *loaded[1:])
    got = [swap(give, "ctx", 1)]
    keep = kept(k_near, *factors)

    masks = [1 << b for b in range(1, bits)]
    for forward, backward in zip(masks, masks[::-1]):
        keep, first, second = add(keep, *got)
        got = [swap(first, "ctx", forward)]
        got.append(swap(second, "ctx", backward))
    mine = renorm(keep, *got, fast_w1, fast_w2, fast_w3)
    other = swap(mine, "ctx", 1)

    seen = window(queries, keys, values, tail)

    early = pile(*(near[k] for k in range(1, heads - 1)))
    late = near[heads - 1].reshape(1, *piece.shape)
    cross = [(i, i ^ (4 if i & 1 else 2)) for i in range(ctx_count)]
    pieces = []
    for group in (early, late):
        far = lax.ppermute(group, "ctx", cross)
        near_c = swap(group, "ctx", 1)
        far_c = swap(far, "ctx", 1)
        pieces.append((group, near_c, far, far_c))

    rows = tok_rows // heads
    blocks = {}
    for k in send_order(heads) + [0]:
        combined = apply_fast(k, queries, seen, mine, other, rows)
        blocks[k] = swap(combined, "head", k) if k else combined
    base, squares = own_project(blocks[0], norm_gain, out_weight)
    for k in send_order(heads):
        late_one = k == heads - 1
        index, which = (0, pieces[1]) if late_one else (k - 1, pieces[0])
        scale_by = 1.0 / (heads * width) if k == send_order(heads)[-1] else None
        result = project(index, scale_by, blocks[k], base, squares, which)
        if scale_by is None:
            base, squares = result
    return result


def send_order(heads):
    return [heads - 1] + list(range(1, heads - 1))


def solution(mesh):
    placed = (
        P("ctx", "head"),
        P("ctx", "head"),
        P("ctx", "head"),
        P("ctx", "head"),
        P("head", None, None),
        P("head", None, None),
        P("head", None, None),
        P("head"),
        P("head", None),
    )
    return jax.shard_map(
        step, mesh=mesh, in_specs=placed, out_specs=P(("ctx", "head"), None), check_vma=False
    )
```

```python
import functools
import math

import jax
import jax.numpy as jnp
from jax import lax
from jax.experimental import pallas as pl
from jax.experimental.pallas import tpu as pltpu
from jax.sharding import PartitionSpec as P


WINDOW = 256
EPSILON = 1e-06

VMEM = pl.BlockSpec(memory_space=pltpu.VMEM)
HBM = pl.BlockSpec(memory_space=pltpu.HBM)


def near_core(*arrays):
    return [pltpu.with_memory_space_constraint(a, pltpu.VMEM) for a in arrays]


def far_core(*arrays):
    return [pltpu.with_memory_space_constraint(a, pltpu.HBM) for a in arrays]


def grant(mib):
    return pltpu.CompilerParams(vmem_limit_bytes=mib << 20)


def swap(value, axis, mask):
    return lax.ppermute(value, axis, [(i, i ^ mask) for i in range(lax.axis_size(axis))])


def dot(left, right, left_dim=1, right_dim=0):
    return lax.dot_general(
        left, right, (((left_dim,), (right_dim,)), ((), ())), preferred_element_type=jnp.float32
    )


def place():
    me = lax.axis_index("ctx").astype(jnp.int32)
    return me & 1, ((me >> 1) ^ (me >> 2)) & 1


def column(row, width):
    tall = jnp.transpose(jnp.broadcast_to(row, (128, row.shape[1])))
    return jnp.concatenate([tall] * (width // 128), axis=1)


def load_kernel(k_hbm, v_hbm, gain_hbm, w_hbm, tail_ref, piece_ref, w_ref, gain_ref, sem):
    rows, columns = piece_ref.shape
    _, side = place()
    first = pl.multiple_of(side * rows, rows)
    last = pl.ds(k_hbm.shape[0] - WINDOW, WINDOW)
    steps = 4
    block = rows // steps
    moves = [(gain_hbm, gain_ref)]
    for i in range(steps):
        at = pl.ds(i * block, block)
        moves.append((w_hbm.at[pl.ds(first + i * block, block), :], w_ref.at[at, :]))
    moves += [(k_hbm.at[last, :], tail_ref.at[pl.ds(0, WINDOW), :])]
    moves += [(v_hbm.at[last, :], tail_ref.at[pl.ds(WINDOW, WINDOW), :])]
    copies = [pltpu.make_async_copy(src, dst, sem.at[j]) for j, (src, dst) in enumerate(moves)]
    for copy in copies:
        copy.start()
    copies[0].wait()
    gain = gain_ref[...].reshape(1, 2 * rows).astype(jnp.float32)
    gain = jnp.transpose(jnp.broadcast_to(jnp.where(side == 0, gain[:, :rows], gain[:, rows:]), (128, rows)))
    for i in range(steps):
        at = slice(i * block, (i + 1) * block)
        copies[1 + i].wait()
        for left in range(0, columns, 128):
            here = slice(left, left + 128)
            piece_ref[at, here] = (w_ref[at, here].astype(jnp.float32) * gain[at, :]).astype(jnp.bfloat16)
    for copy in copies[1 + steps :]:
        copy.wait()


def load(keys, values, gain, weight):
    piece = pltpu.VMEM((weight.shape[0] // 2, weight.shape[1]), jnp.bfloat16)
    return pl.pallas_call(
        load_kernel,
        out_shape=[pltpu.VMEM((2 * WINDOW, keys.shape[1]), jnp.bfloat16), piece],
        compiler_params=grant(8),
        in_specs=[HBM] * 4,
        out_specs=[VMEM] * 2,
        scratch_shapes=[piece, pltpu.VMEM(gain.shape, gain.dtype), pltpu.SemaphoreType.DMA((7,))],
        name="load",
    )(*far_core(keys, values, gain, weight))


def halves(width):
    core, _ = place()
    half = width // 2
    mine = pl.ds(pl.multiple_of(core * half, half), half)
    theirs = pl.ds(pl.multiple_of((1 - core) * half, half), half)
    return mine, theirs


def push_kernel(k_ref, v_ref, r_ref, w1_ref, w2_ref, w3_ref, give_ref, act_ref, sc_ref, g1_ref, g3_ref):
    rows, width = k_ref.shape
    steps = 4
    block = rows // steps
    for i in range(steps):
        at = slice(i * block, (i + 1) * block)
        k = k_ref[at, :]
        gate = dot(k, w1_ref[0])
        up = dot(k, w3_ref[0])
        rate = column(r_ref[:, at], width)
        scaled = (v_ref[at, :].astype(jnp.float32) * rate).astype(jnp.bfloat16)
        back = dot(scaled, w2_ref[0], 1, 1)
        s = jax.nn.sigmoid(gate)
        gs = gate * s
        act_ref[at, :] = (gs * up).astype(jnp.bfloat16)
        sc_ref[at, :] = scaled
        g1_ref[at, :] = (back * up * (s + gs * (1.0 - s))).astype(jnp.bfloat16)
        g3_ref[at, :] = (back * gs).astype(jnp.bfloat16)
    _, theirs = halves(width)
    for j, (left, right) in enumerate([(k_ref, g1_ref), (act_ref, sc_ref), (k_ref, g3_ref)]):
        give_ref[j] = dot(left[...], right[:, theirs], 0, 0).astype(jnp.bfloat16)


def pushes(keys, values, rates, w1, w2, w3):
    rows, width = keys.shape
    wide = pltpu.VMEM((rows, width), jnp.bfloat16)
    return pl.pallas_call(
        push_kernel,
        out_shape=[pltpu.VMEM((3, width, width // 2), jnp.bfloat16)] + [wide] * 4,
        compiler_params=grant(16),
        in_specs=[VMEM] * 6,
        out_specs=[VMEM] * 5,
        name="pushes",
    )(*near_core(keys, values, rates.reshape(1, rows), w1, w2, w3))


def keep_kernel(k_ref, act_ref, sc_ref, g1_ref, g3_ref, keep_ref):
    mine, _ = halves(k_ref.shape[1])
    for j, (left, right) in enumerate([(k_ref, g1_ref), (act_ref, sc_ref), (k_ref, g3_ref)]):
        keep_ref[j] = dot(left[...], right[:, mine], 0, 0)


def kept(*arrays):
    width = arrays[0].shape[1]
    return pl.pallas_call(
        keep_kernel,
        out_shape=pltpu.VMEM((3, width, width // 2), jnp.float32),
        compiler_params=grant(16),
        in_specs=[VMEM] * 5,
        out_specs=VMEM,
        name="kept",
    )(*near_core(*arrays))


def first_add_kernel(keep_ref, got_ref, sum_ref, a_ref, b_ref):
    quarter = a_ref.shape[2]
    total = keep_ref[...] + got_ref[...].astype(jnp.float32)
    sum_ref[...] = total
    a_ref[...] = total[:, :, :quarter].astype(jnp.bfloat16)
    b_ref[...] = total[:, :, quarter:].astype(jnp.bfloat16)


def later_add_kernel(keep_ref, got_a_ref, got_b_ref, sum_ref, a_ref, b_ref):
    quarter = a_ref.shape[2]
    first = keep_ref[:, :, :quarter] + got_a_ref[...].astype(jnp.float32)
    second = keep_ref[:, :, quarter:] + got_b_ref[...].astype(jnp.float32)
    sum_ref[:, :, :quarter] = first
    sum_ref[:, :, quarter:] = second
    a_ref[...] = first.astype(jnp.bfloat16)
    b_ref[...] = second.astype(jnp.bfloat16)


def add(keep, *got):
    stream = pltpu.VMEM(keep.shape[:2] + (keep.shape[2] // 2,), jnp.bfloat16)
    return pl.pallas_call(
        first_add_kernel if len(got) == 1 else later_add_kernel,
        out_shape=(pltpu.VMEM(keep.shape, jnp.float32), stream, stream),
        compiler_params=grant(8),
        in_specs=[VMEM] * (1 + len(got)),
        out_specs=(VMEM,) * 3,
        name="add",
    )(*near_core(keep, *got))


def renorm_kernel(keep_ref, got_a_ref, got_b_ref, w1_ref, w2_ref, w3_ref, out_ref):
    half = keep_ref.shape[2]
    block = got_a_ref.shape[2]
    core, _ = place()
    for j, w_ref in enumerate((w1_ref, w2_ref, w3_ref)):
        for first, got_ref in ((0, got_a_ref), (block, got_b_ref)):
            at = slice(first, first + block)
            start = pl.multiple_of(core * half + first, block)
            old = w_ref[0, :, pl.ds(start, block)].astype(jnp.float32)
            new = old + (keep_ref[j, :, at] + got_ref[j].astype(jnp.float32))
            old_norm = jnp.sqrt(jnp.mean(old * old, axis=0, keepdims=True) + EPSILON)
            new_norm = jnp.sqrt(jnp.mean(new * new, axis=0, keepdims=True) + EPSILON)
            out_ref[j, :, at] = (new * (old_norm / new_norm)).astype(jnp.bfloat16)


def renorm(keep, *others):
    return pl.pallas_call(
        renorm_kernel,
        out_shape=pltpu.VMEM(keep.shape, jnp.bfloat16),
        compiler_params=grant(8),
        in_specs=[VMEM] * 6,
        out_specs=VMEM,
        name="renorm",
    )(*near_core(keep, *others))


def window_kernel(q_hbm, k_hbm, v_hbm, tail_ref, out_ref, q_ref, k_ref, v_ref, sem):
    rows, width = q_ref.shape
    scale = 1.0 / math.sqrt(width)
    query = lax.broadcasted_iota(jnp.int32, (WINDOW, 2 * WINDOW), 0)
    key = lax.broadcasted_iota(jnp.int32, (WINDOW, 2 * WINDOW), 1)
    allowed = (key > query) & (key <= query + WINDOW)
    allowed_first = allowed & ((key >= WINDOW) | (lax.axis_index("ctx") > 0))
    count = rows // WINDOW
    loads = [[
        pltpu.make_async_copy(tail_ref.at[pl.ds(j * WINDOW, WINDOW), :], dst.at[pl.ds(0, WINDOW), :], sem.at[j])
        for j, dst in enumerate((k_ref, v_ref))
    ]]
    for i in range(count):
        at, after = pl.ds(i * WINDOW, WINDOW), pl.ds((i + 1) * WINDOW, WINDOW)
        loads.append([
            pltpu.make_async_copy(q_hbm.at[at, :], q_ref.at[at, :], sem.at[3 * i + 2]),
            pltpu.make_async_copy(k_hbm.at[at, :], k_ref.at[after, :], sem.at[3 * i + 3]),
            pltpu.make_async_copy(v_hbm.at[at, :], v_ref.at[after, :], sem.at[3 * i + 4]),
        ])
    for group in loads:
        for load in group:
            load.start()
    for load in loads[0]:
        load.wait()
    for i in range(count):
        for load in loads[i + 1]:
            load.wait()
        at = slice(i * WINDOW, (i + 1) * WINDOW)
        seen = slice(i * WINDOW, (i + 2) * WINDOW)
        scores = dot(q_ref[at, :], k_ref[seen, :], 1, 1) * scale
        scores = jnp.where(allowed_first if i == 0 else allowed, scores, -jnp.inf)
        peak = jnp.max(scores, axis=1, keepdims=True)
        exponent = jnp.exp(scores - peak)
        weights = exponent / jnp.sum(exponent, axis=1, keepdims=True)
        out_ref[at, :] = dot(weights.astype(jnp.bfloat16), v_ref[seen, :])


def window(queries, keys, values, tail):
    rows, width = queries.shape
    return pl.pallas_call(
        window_kernel,
        out_shape=pltpu.VMEM(queries.shape, jnp.float32),
        compiler_params=grant(24),
        in_specs=[HBM] * 3 + [VMEM],
        out_specs=VMEM,
        scratch_shapes=[pltpu.VMEM((rows, width), jnp.bfloat16)]
        + [pltpu.VMEM((rows + WINDOW, width), jnp.bfloat16)] * 2
        + [pltpu.SemaphoreType.DMA((2 + 3 * (rows // WINDOW),))],
        name="window",
    )(*far_core(queries, keys, values), *near_core(tail))


def apply_kernel(slot, q_ref, seen_ref, mine_ref, other_ref, out_ref):
    rows = out_ref.shape[0]
    half = mine_ref.shape[2]
    core, _ = place()
    own = pl.ds(pl.multiple_of(core * half, half), half)
    rest = pl.ds(pl.multiple_of((1 - core) * half, half), half)
    here = pl.ds(pl.multiple_of((lax.axis_index("head").astype(jnp.int32) ^ slot) * rows, rows), rows)
    q = q_ref[here, :]

    mixed = []
    for ref in (mine_ref, other_ref):
        gate = dot(q, ref[0])
        up = dot(q, ref[2])
        mixed.append((gate * jax.nn.sigmoid(gate) * up).astype(jnp.bfloat16))
    mixed = jnp.concatenate(mixed, axis=1)
    for ref, at in ((mine_ref, own), (other_ref, rest)):
        down = jnp.concatenate([ref[1, own, :], ref[1, rest, :]], axis=0)
        out_ref[:, at] = (dot(mixed, down) + seen_ref[here, at]).astype(jnp.bfloat16)


def apply_fast(slot, queries, seen, mine, other, rows):
    return pl.pallas_call(
        functools.partial(apply_kernel, slot),
        out_shape=pltpu.VMEM((rows, queries.shape[1]), jnp.bfloat16),
        compiler_params=grant(16),
        in_specs=[VMEM] * 4,
        out_specs=VMEM,
        name="apply",
    )(*near_core(queries, seen, mine, other))


def own_project_kernel(x_ref, gain_ref, w_ref, out_ref, squares_ref):
    wide = x_ref[...].astype(jnp.float32)
    squares_ref[...] = jnp.sum(wide * wide, axis=1, keepdims=True)
    gain = gain_ref[...].reshape(1, wide.shape[1]).astype(jnp.float32)
    x = (wide * gain).astype(jnp.bfloat16)
    out_ref[...] = dot(x, w_ref[...])


def own_project(x, gain, weight):
    return pl.pallas_call(
        own_project_kernel,
        out_shape=(
            pltpu.VMEM((x.shape[0], weight.shape[1]), jnp.float32),
            pltpu.VMEM((x.shape[0], 1), jnp.float32),
        ),
        compiler_params=grant(16),
        in_specs=[VMEM] * 3,
        out_specs=(VMEM, VMEM),
        name="own_project",
    )(*near_core(x, gain, weight))


def pick_kernel(early_ref, early_c_ref, out_ref, sem):
    columns = out_ref.shape[1]
    core, _ = place()
    here = pl.ds(pl.multiple_of(core * columns, columns), columns)

    @pl.when(core == 1)
    def _():
        copy = pltpu.make_async_copy(early_ref.at[:, here], out_ref, sem)
        copy.start()
        copy.wait()

    @pl.when(core == 0)
    def _():
        copy = pltpu.make_async_copy(early_c_ref.at[:, here], out_ref, sem)
        copy.start()
        copy.wait()


def pick(early, early_c):
    return pl.pallas_call(
        pick_kernel,
        out_shape=pltpu.VMEM((early.shape[0], early.shape[1] // 2), early.dtype),
        compiler_params=grant(4),
        in_specs=[VMEM] * 2,
        out_specs=VMEM,
        scratch_shapes=[pltpu.SemaphoreType.DMA],
        name="pick",
    )(*near_core(early, early_c))


def project_kernel(holder, scale_by, x_ref, base_ref, squares_ref, near, near_c, far, far_c,
                   out_ref, *rest):
    rows = near.shape[0]
    columns = out_ref.shape[1] // 2
    core, half = place()
    wide = x_ref[...].astype(jnp.float32)
    squares = squares_ref[...] + jnp.sum(wide * wide, axis=1, keepdims=True)
    mine = pl.ds(pl.multiple_of(half * rows, rows), rows)
    theirs = pl.ds(pl.multiple_of((1 - half) * rows, rows), rows)
    x = jnp.concatenate([x_ref[:, mine], x_ref[:, theirs]], axis=1)
    scale = lax.rsqrt(squares * scale_by + EPSILON) if scale_by else None
    block = columns // 2
    stores = []
    for side in range(2):
        for j in range(2):
            if holder is None:
                w_near, w_far = ((near, far), (near_c, far_c))[side]
                start = core if side == 0 else 1 - core
                here = slice(j * block, (j + 1) * block)
                w = jnp.concatenate([w_near[:, here], w_far[:, here]], axis=0)
                at = pl.ds(pl.multiple_of(start * columns + j * block, block), block)
            else:
                at = slice(side * columns + j * block, side * columns + (j + 1) * block)
                w = [jnp.where(core == holder, a[:, at], b[:, at]) for a, b in ((near, near_c), (far, far_c))]
                w = jnp.concatenate(w, axis=0)
            total = base_ref[:, at] + dot(x, w)
            if scale_by:
                ready_ref, sem = rest
                ready_ref[2 * side + j] = (total * scale).astype(jnp.bfloat16)
                store = pltpu.make_async_copy(ready_ref.at[2 * side + j], out_ref.at[:, at], sem.at[2 * side + j])
                store.start()
                stores.append(store)
            else:
                out_ref[:, at] = total
    if not scale_by:
        rest[0][...] = squares
    for store in stores:
        store.wait()


def project(holder, scale_by, x, base, squares, pieces):
    rows, columns = base.shape
    if scale_by:
        shape = jax.ShapeDtypeStruct((rows, columns), jnp.bfloat16)
        scratch = [pltpu.VMEM((4, rows, columns // 4), jnp.bfloat16), pltpu.SemaphoreType.DMA((4,))]
    else:
        shape = (pltpu.VMEM((rows, columns), jnp.float32), pltpu.VMEM((rows, 1), jnp.float32))
        scratch = []
    return pl.pallas_call(
        functools.partial(project_kernel, holder, scale_by),
        out_shape=shape,
        in_specs=[VMEM] * 7,
        out_specs=HBM if scale_by else (VMEM, VMEM),
        scratch_shapes=scratch,
        compiler_params=grant(16),
        name="project",
    )(*near_core(x, base, squares, *pieces))


def step(queries, keys, values, rates, fast_w1, fast_w2, fast_w3, norm_gain, out_weight):
    tok_rows, width = queries.shape
    ctx_count = lax.axis_size("ctx")
    heads = lax.axis_size("head")
    bits = ctx_count.bit_length() - 1
    assert ctx_count == 1 << bits and bits >= 3 and heads == 4

    tail, piece = load(keys, values, norm_gain, out_weight)
    tail = lax.ppermute(tail, "ctx", [(i, i + 1) for i in range(ctx_count - 1)])

    over = [(i, i ^ (2 if i // heads & 1 else 1)) for i in range(ctx_count * heads)]
    early = lax.ppermute(piece, ("ctx", "head"), over)
    early_c = swap(early, "ctx", 1)
    late = pick(early, early_c)
    late = swap(late, "head", 1)
    cross = [(i, i ^ (4 if i & 1 else 2)) for i in range(ctx_count)]
    early_far = lax.ppermute(early, "ctx", cross)
    late_far = lax.ppermute(late, "ctx", cross)
    late_c = swap(late, "ctx", 1)
    early_far_c = swap(early_far, "ctx", 1)
    late_far_c = swap(late_far, "ctx", 1)
    early_pieces = (early, early_c, early_far, early_far_c)
    late_pieces = (late, late_c, late_far, late_far_c)

    give, *factors = pushes(keys, values, rates, fast_w1, fast_w2, fast_w3)
    got = [swap(give, "ctx", 1)]
    keep = kept(keys, *factors)

    masks = [1 << b for b in range(1, bits)]
    for forward, backward in zip(masks, masks[::-1]):
        keep, first, second = add(keep, *got)
        got = [swap(first, "ctx", forward)]
        got.append(swap(second, "ctx", backward))
    mine = renorm(keep, *got, fast_w1, fast_w2, fast_w3)
    other = swap(mine, "ctx", 1)

    seen = window(queries, keys, values, tail)

    rows = tok_rows // heads
    blocks = {}
    for k in send_order(heads) + [0]:
        combined = apply_fast(k, queries, seen, mine, other, rows)
        blocks[k] = swap(combined, "head", k) if k else combined
    base, squares = own_project(blocks[0], norm_gain, out_weight)
    for k in send_order(heads):
        holder, pieces = (None, late_pieces) if k == heads - 1 else (k - 1, early_pieces)
        scale_by = 1.0 / (heads * width) if k == send_order(heads)[-1] else None
        result = project(holder, scale_by, blocks[k], base, squares, pieces)
        if scale_by is None:
            base, squares = result
    return result


def send_order(heads):
    return [heads - 1] + list(range(1, heads - 1))


def solution(mesh):
    placed = (
        P("ctx", "head"),
        P("ctx", "head"),
        P("ctx", "head"),
        P("ctx", "head"),
        P("head", None, None),
        P("head", None, None),
        P("head", None, None),
        P("head"),
        P("head", None),
    )
    return jax.shard_map(step, mesh=mesh, in_specs=placed, out_specs=P(("ctx", "head"), None), check_vma=False)
```

```python
import functools
import math

import jax
import jax.numpy as jnp
from jax import lax
from jax.experimental import pallas as pl
from jax.experimental.pallas import tpu as pltpu
from jax.sharding import PartitionSpec as P


WINDOW = 256
EPSILON = 1e-06

VMEM = pl.BlockSpec(memory_space=pltpu.VMEM)
HBM = pl.BlockSpec(memory_space=pltpu.HBM)


def near_core(*arrays):
    return [pltpu.with_memory_space_constraint(a, pltpu.VMEM) for a in arrays]


def far_core(*arrays):
    return [pltpu.with_memory_space_constraint(a, pltpu.HBM) for a in arrays]


def grant(mib):
    return pltpu.CompilerParams(vmem_limit_bytes=mib << 20)


def swap(value, axis, mask):
    return lax.ppermute(value, axis, [(i, i ^ mask) for i in range(lax.axis_size(axis))])


def dot(left, right, left_dim=1, right_dim=0):
    return lax.dot_general(
        left, right, (((left_dim,), (right_dim,)), ((), ())), preferred_element_type=jnp.float32
    )


def place():
    me = lax.axis_index("ctx").astype(jnp.int32)
    return me & 1, ((me >> 1) ^ (me >> 2)) & 1


def column(row, width):
    tall = jnp.transpose(jnp.broadcast_to(row, (128, row.shape[1])))
    return jnp.concatenate([tall] * (width // 128), axis=1)


def load_kernel(k_hbm, v_hbm, gain_hbm, w_hbm, tail_ref, piece_ref, w_ref, gain_ref, sem):
    rows, columns = piece_ref.shape
    _, side = place()
    first = pl.multiple_of(side * rows, rows)
    last = pl.ds(k_hbm.shape[0] - WINDOW, WINDOW)
    steps = 4
    block = rows // steps
    moves = [(gain_hbm, gain_ref)]
    for i in range(steps):
        at = pl.ds(i * block, block)
        moves.append((w_hbm.at[pl.ds(first + i * block, block), :], w_ref.at[at, :]))
    moves += [(k_hbm.at[last, :], tail_ref.at[pl.ds(0, WINDOW), :])]
    moves += [(v_hbm.at[last, :], tail_ref.at[pl.ds(WINDOW, WINDOW), :])]
    copies = [pltpu.make_async_copy(src, dst, sem.at[j]) for j, (src, dst) in enumerate(moves)]
    for copy in copies:
        copy.start()
    copies[0].wait()
    gain = gain_ref[...].reshape(1, 2 * rows).astype(jnp.float32)
    gain = jnp.transpose(jnp.broadcast_to(jnp.where(side == 0, gain[:, :rows], gain[:, rows:]), (128, rows)))
    for i in range(steps):
        at = slice(i * block, (i + 1) * block)
        copies[1 + i].wait()
        for left in range(0, columns, 128):
            here = slice(left, left + 128)
            piece_ref[at, here] = (w_ref[at, here].astype(jnp.float32) * gain[at, :]).astype(jnp.bfloat16)
    for copy in copies[1 + steps :]:
        copy.wait()


def load(keys, values, gain, weight):
    piece = pltpu.VMEM((weight.shape[0] // 2, weight.shape[1]), jnp.bfloat16)
    return pl.pallas_call(
        load_kernel,
        out_shape=[pltpu.VMEM((2 * WINDOW, keys.shape[1]), jnp.bfloat16), piece],
        compiler_params=grant(8),
        in_specs=[HBM] * 4,
        out_specs=[VMEM] * 2,
        scratch_shapes=[piece, pltpu.VMEM(gain.shape, gain.dtype), pltpu.SemaphoreType.DMA((7,))],
        name="load",
    )(*far_core(keys, values, gain, weight))


def halves(width):
    core, _ = place()
    half = width // 2
    mine = pl.ds(pl.multiple_of(core * half, half), half)
    theirs = pl.ds(pl.multiple_of((1 - core) * half, half), half)
    return mine, theirs


def forward_kernel(k_ref, v_ref, r_ref, w1_ref, w3_ref, give_ref, act_ref, sc_ref, gs_ref, slope_ref):
    rows, width = k_ref.shape
    steps = 4
    block = rows // steps
    for i in range(steps):
        at = slice(i * block, (i + 1) * block)
        k = k_ref[at, :]
        gate = dot(k, w1_ref[0])
        up = dot(k, w3_ref[0])
        rate = column(r_ref[:, at], width)
        s = jax.nn.sigmoid(gate)
        gs = gate * s
        act_ref[at, :] = (gs * up).astype(jnp.bfloat16)
        sc_ref[at, :] = (v_ref[at, :].astype(jnp.float32) * rate).astype(jnp.bfloat16)
        gs_ref[at, :] = gs
        slope_ref[at, :] = up * (s + gs * (1.0 - s))
    _, theirs = halves(width)
    give_ref[0] = dot(act_ref[...], sc_ref[:, theirs], 0, 0).astype(jnp.bfloat16)


def push_forward(keys, values, rates, w1, w3):
    rows, width = keys.shape
    return pl.pallas_call(
        forward_kernel,
        out_shape=[pltpu.VMEM((1, width, width // 2), jnp.bfloat16)]
        + [pltpu.VMEM((rows, width), jnp.bfloat16)] * 2
        + [pltpu.VMEM((rows, width), jnp.float32)] * 2,
        compiler_params=grant(12),
        in_specs=[VMEM] * 5,
        out_specs=[VMEM] * 5,
        name="push_forward",
    )(*near_core(keys, values, rates.reshape(1, rows), w1, w3))


def backward_kernel(k_ref, act_ref, sc_ref, gs_ref, slope_ref, w2_ref, give_ref, keep_ref, g1_ref, g3_ref):
    rows, width = k_ref.shape
    steps = 4
    block = rows // steps
    for i in range(steps):
        at = slice(i * block, (i + 1) * block)
        back = dot(sc_ref[at, :], w2_ref[0], 1, 1)
        g1_ref[at, :] = (back * slope_ref[at, :]).astype(jnp.bfloat16)
        g3_ref[at, :] = (back * gs_ref[at, :]).astype(jnp.bfloat16)
    mine, theirs = halves(width)
    give_ref[0] = dot(k_ref[...], g1_ref[:, theirs], 0, 0).astype(jnp.bfloat16)
    give_ref[1] = dot(k_ref[...], g3_ref[:, theirs], 0, 0).astype(jnp.bfloat16)
    keep_ref[0] = dot(act_ref[...], sc_ref[:, mine], 0, 0)


def push_backward(keys, act, scaled, gs, slope, w2):
    rows, width = keys.shape
    return pl.pallas_call(
        backward_kernel,
        out_shape=[
            pltpu.VMEM((2, width, width // 2), jnp.bfloat16),
            pltpu.VMEM((1, width, width // 2), jnp.float32),
        ]
        + [pltpu.VMEM((rows, width), jnp.bfloat16)] * 2,
        compiler_params=grant(12),
        in_specs=[VMEM] * 6,
        out_specs=[VMEM] * 4,
        name="push_backward",
    )(*near_core(keys, act, scaled, gs, slope, w2))


def keep_kernel(k_ref, g1_ref, g3_ref, keep_ref):
    mine, _ = halves(k_ref.shape[1])
    for j, ref in enumerate((g1_ref, g3_ref)):
        keep_ref[j] = dot(k_ref[...], ref[:, mine], 0, 0)


def kept(keys, g1, g3):
    width = keys.shape[1]
    return pl.pallas_call(
        keep_kernel,
        out_shape=pltpu.VMEM((2, width, width // 2), jnp.float32),
        compiler_params=grant(12),
        in_specs=[VMEM] * 3,
        out_specs=VMEM,
        name="kept",
    )(*near_core(keys, g1, g3))


def add_kernel(keep_ref, got_ref, sum_ref, send_ref):
    total = keep_ref[...] + got_ref[...].astype(jnp.float32)
    sum_ref[...] = total
    send_ref[...] = total.astype(jnp.bfloat16)


def add(keep, got):
    return pl.pallas_call(
        add_kernel,
        out_shape=(pltpu.VMEM(keep.shape, jnp.float32), pltpu.VMEM(keep.shape, jnp.bfloat16)),
        compiler_params=grant(8),
        in_specs=[VMEM] * 2,
        out_specs=(VMEM,) * 2,
        name="add",
    )(*near_core(keep, got))


def renorm_kernel(keep_ref, got_ref, *refs):
    *weights, out_ref = refs
    half = keep_ref.shape[2]
    block = half // 2
    core, _ = place()
    for j, w_ref in enumerate(weights):
        for first in (0, block):
            at = slice(first, first + block)
            start = pl.multiple_of(core * half + first, block)
            old = w_ref[0, :, pl.ds(start, block)].astype(jnp.float32)
            new = old + (keep_ref[j, :, at] + got_ref[j, :, at].astype(jnp.float32))
            old_norm = jnp.sqrt(jnp.mean(old * old, axis=0, keepdims=True) + EPSILON)
            new_norm = jnp.sqrt(jnp.mean(new * new, axis=0, keepdims=True) + EPSILON)
            out_ref[j, :, at] = (new * (old_norm / new_norm)).astype(jnp.bfloat16)


def renorm(keep, got, *weights):
    return pl.pallas_call(
        renorm_kernel,
        out_shape=pltpu.VMEM(keep.shape, jnp.bfloat16),
        compiler_params=grant(8),
        in_specs=[VMEM] * (2 + len(weights)),
        out_specs=VMEM,
        name="renorm",
    )(*near_core(keep, got, *weights))


def window_kernel(q_hbm, k_hbm, v_hbm, tail_ref, out_ref, q_ref, k_ref, v_ref, sem):
    rows, width = q_ref.shape
    scale = 1.0 / math.sqrt(width)
    query = lax.broadcasted_iota(jnp.int32, (WINDOW, 2 * WINDOW), 0)
    key = lax.broadcasted_iota(jnp.int32, (WINDOW, 2 * WINDOW), 1)
    allowed = (key > query) & (key <= query + WINDOW)
    allowed_first = allowed & ((key >= WINDOW) | (lax.axis_index("ctx") > 0))
    count = rows // WINDOW
    loads = [[
        pltpu.make_async_copy(tail_ref.at[pl.ds(j * WINDOW, WINDOW), :], dst.at[pl.ds(0, WINDOW), :], sem.at[j])
        for j, dst in enumerate((k_ref, v_ref))
    ]]
    for i in range(count):
        at, after = pl.ds(i * WINDOW, WINDOW), pl.ds((i + 1) * WINDOW, WINDOW)
        loads.append([
            pltpu.make_async_copy(q_hbm.at[at, :], q_ref.at[at, :], sem.at[3 * i + 2]),
            pltpu.make_async_copy(k_hbm.at[at, :], k_ref.at[after, :], sem.at[3 * i + 3]),
            pltpu.make_async_copy(v_hbm.at[at, :], v_ref.at[after, :], sem.at[3 * i + 4]),
        ])
    for group in loads:
        for load in group:
            load.start()
    for load in loads[0]:
        load.wait()
    for i in range(count):
        for load in loads[i + 1]:
            load.wait()
        at = slice(i * WINDOW, (i + 1) * WINDOW)
        seen = slice(i * WINDOW, (i + 2) * WINDOW)
        scores = dot(q_ref[at, :], k_ref[seen, :], 1, 1) * scale
        scores = jnp.where(allowed_first if i == 0 else allowed, scores, -jnp.inf)
        peak = jnp.max(scores, axis=1, keepdims=True)
        exponent = jnp.exp(scores - peak)
        weights = exponent / jnp.sum(exponent, axis=1, keepdims=True)
        out_ref[at, :] = dot(weights.astype(jnp.bfloat16), v_ref[seen, :])


def window(queries, keys, values, tail):
    rows, width = queries.shape
    return pl.pallas_call(
        window_kernel,
        out_shape=pltpu.VMEM(queries.shape, jnp.float32),
        compiler_params=grant(24),
        in_specs=[HBM] * 3 + [VMEM],
        out_specs=VMEM,
        scratch_shapes=[pltpu.VMEM((rows, width), jnp.bfloat16)]
        + [pltpu.VMEM((rows + WINDOW, width), jnp.bfloat16)] * 2
        + [pltpu.SemaphoreType.DMA((2 + 3 * (rows // WINDOW),))],
        name="window",
    )(*far_core(queries, keys, values), *near_core(tail))


def apply_kernel(slot, q_ref, seen_ref, down_ref, up_ref, down_c_ref, up_c_ref, out_ref):
    rows, width = out_ref.shape
    own, rest = halves(width)
    here = pl.ds(pl.multiple_of((lax.axis_index("head").astype(jnp.int32) ^ slot) * rows, rows), rows)
    q = q_ref[here, :]
    mixed = []
    for ref in (up_ref, up_c_ref):
        gate = dot(q, ref[0])
        up = dot(q, ref[1])
        mixed.append((gate * jax.nn.sigmoid(gate) * up).astype(jnp.bfloat16))
    mixed = jnp.concatenate(mixed, axis=1)
    for ref, at in ((down_ref, own), (down_c_ref, rest)):
        down = jnp.concatenate([ref[0, own, :], ref[0, rest, :]], axis=0)
        out_ref[:, at] = (dot(mixed, down) + seen_ref[here, at]).astype(jnp.bfloat16)


def apply_fast(slot, queries, seen, weights, rows):
    return pl.pallas_call(
        functools.partial(apply_kernel, slot),
        out_shape=pltpu.VMEM((rows, queries.shape[1]), jnp.bfloat16),
        compiler_params=grant(16),
        in_specs=[VMEM] * 6,
        out_specs=VMEM,
        name="apply",
    )(*near_core(queries, seen, *weights))


def own_project_kernel(x_ref, gain_ref, w_ref, out_ref, squares_ref):
    wide = x_ref[...].astype(jnp.float32)
    squares_ref[...] = jnp.sum(wide * wide, axis=1, keepdims=True)
    gain = gain_ref[...].reshape(1, wide.shape[1]).astype(jnp.float32)
    x = (wide * gain).astype(jnp.bfloat16)
    out_ref[...] = dot(x, w_ref[...])


def own_project(x, gain, weight):
    return pl.pallas_call(
        own_project_kernel,
        out_shape=(
            pltpu.VMEM((x.shape[0], weight.shape[1]), jnp.float32),
            pltpu.VMEM((x.shape[0], 1), jnp.float32),
        ),
        compiler_params=grant(16),
        in_specs=[VMEM] * 3,
        out_specs=(VMEM, VMEM),
        name="own_project",
    )(*near_core(x, gain, weight))


def pick_kernel(early_ref, early_c_ref, out_ref, sem):
    columns = out_ref.shape[1]
    core, _ = place()
    here = pl.ds(pl.multiple_of(core * columns, columns), columns)

    @pl.when(core == 1)
    def _():
        copy = pltpu.make_async_copy(early_ref.at[:, here], out_ref, sem)
        copy.start()
        copy.wait()

    @pl.when(core == 0)
    def _():
        copy = pltpu.make_async_copy(early_c_ref.at[:, here], out_ref, sem)
        copy.start()
        copy.wait()


def pick(early, early_c):
    return pl.pallas_call(
        pick_kernel,
        out_shape=pltpu.VMEM((early.shape[0], early.shape[1] // 2), early.dtype),
        compiler_params=grant(4),
        in_specs=[VMEM] * 2,
        out_specs=VMEM,
        scratch_shapes=[pltpu.SemaphoreType.DMA],
        name="pick",
    )(*near_core(early, early_c))


def project_kernel(holder, scale_by, x_ref, base_ref, squares_ref, near, near_c, far, far_c,
                   out_ref, *rest):
    rows = near.shape[0]
    columns = out_ref.shape[1] // 2
    core, half = place()
    wide = x_ref[...].astype(jnp.float32)
    squares = squares_ref[...] + jnp.sum(wide * wide, axis=1, keepdims=True)
    mine = pl.ds(pl.multiple_of(half * rows, rows), rows)
    theirs = pl.ds(pl.multiple_of((1 - half) * rows, rows), rows)
    x = jnp.concatenate([x_ref[:, mine], x_ref[:, theirs]], axis=1)
    scale = lax.rsqrt(squares * scale_by + EPSILON) if scale_by else None
    block = columns // 2
    stores = []
    for side in range(2):
        for j in range(2):
            if holder is None:
                w_near, w_far = ((near, far), (near_c, far_c))[side]
                start = core if side == 0 else 1 - core
                here = slice(j * block, (j + 1) * block)
                w = jnp.concatenate([w_near[:, here], w_far[:, here]], axis=0)
                at = pl.ds(pl.multiple_of(start * columns + j * block, block), block)
            else:
                at = slice(side * columns + j * block, side * columns + (j + 1) * block)
                w = [jnp.where(core == holder, a[:, at], b[:, at]) for a, b in ((near, near_c), (far, far_c))]
                w = jnp.concatenate(w, axis=0)
            total = base_ref[:, at] + dot(x, w)
            if scale_by:
                ready_ref, sem = rest
                ready_ref[2 * side + j] = (total * scale).astype(jnp.bfloat16)
                store = pltpu.make_async_copy(ready_ref.at[2 * side + j], out_ref.at[:, at], sem.at[2 * side + j])
                store.start()
                stores.append(store)
            else:
                out_ref[:, at] = total
    if not scale_by:
        rest[0][...] = squares
    for store in stores:
        store.wait()


def project(holder, scale_by, x, base, squares, pieces):
    rows, columns = base.shape
    if scale_by:
        shape = jax.ShapeDtypeStruct((rows, columns), jnp.bfloat16)
        scratch = [pltpu.VMEM((4, rows, columns // 4), jnp.bfloat16), pltpu.SemaphoreType.DMA((4,))]
    else:
        shape = (pltpu.VMEM((rows, columns), jnp.float32), pltpu.VMEM((rows, 1), jnp.float32))
        scratch = []
    return pl.pallas_call(
        functools.partial(project_kernel, holder, scale_by),
        out_shape=shape,
        in_specs=[VMEM] * 7,
        out_specs=HBM if scale_by else (VMEM, VMEM),
        scratch_shapes=scratch,
        compiler_params=grant(16),
        name="project",
    )(*near_core(x, base, squares, *pieces))


def step(queries, keys, values, rates, fast_w1, fast_w2, fast_w3, norm_gain, out_weight):
    tok_rows, width = queries.shape
    ctx_count = lax.axis_size("ctx")
    heads = lax.axis_size("head")
    bits = ctx_count.bit_length() - 1
    assert ctx_count == 1 << bits and bits >= 3 and heads == 4

    tail, piece = load(keys, values, norm_gain, out_weight)
    tail = lax.ppermute(tail, "ctx", [(i, i + 1) for i in range(ctx_count - 1)])

    over = [(i, i ^ (2 if i // heads & 1 else 1)) for i in range(ctx_count * heads)]
    early = lax.ppermute(piece, ("ctx", "head"), over)
    early_c = swap(early, "ctx", 1)
    late = pick(early, early_c)
    late = swap(late, "head", 1)
    cross = [(i, i ^ (2 if i & 1 else 4)) for i in range(ctx_count)]
    early_far = lax.ppermute(early, "ctx", cross)
    late_far = lax.ppermute(late, "ctx", cross)
    late_c = swap(late, "ctx", 1)
    early_far_c = swap(early_far, "ctx", 1)
    late_far_c = swap(late_far, "ctx", 1)
    early_pieces = (early, early_c, early_far, early_far_c)
    late_pieces = (late, late_c, late_far, late_far_c)

    give_a, act, scaled, gs, slope = push_forward(keys, values, rates, fast_w1, fast_w3)
    give_b, keep_a, g1, g3 = push_backward(keys, act, scaled, gs, slope, fast_w2)
    keep_b = kept(keys, g1, g3)

    masks = [1 << b for b in range(1, bits)]
    crossing = [
        [(i, i ^ (backward if i & 1 else forward)) for i in range(ctx_count)]
        for forward, backward in zip(masks, masks[::-1])
    ]
    weights = []
    for give, keep, olds in ((give_a, keep_a, (fast_w2,)), (give_b, keep_b, (fast_w1, fast_w3))):
        got = swap(give, "ctx", 1)
        for pairs in crossing:
            keep, send = add(keep, got)
            got = lax.ppermute(send, "ctx", pairs)
        mine = renorm(keep, got, *olds)
        other = swap(mine, "ctx", 1)
        weights.append((mine, other))
    weights = (weights[0][0], weights[1][0], weights[0][1], weights[1][1])

    seen = window(queries, keys, values, tail)

    rows = tok_rows // heads
    blocks = {}
    for k in send_order(heads) + [0]:
        combined = apply_fast(k, queries, seen, weights, rows)
        blocks[k] = swap(combined, "head", k) if k else combined
    base, squares = own_project(blocks[0], norm_gain, out_weight)
    for k in send_order(heads):
        holder, pieces = (None, late_pieces) if k == heads - 1 else (k - 1, early_pieces)
        scale_by = 1.0 / (heads * width) if k == send_order(heads)[-1] else None
        result = project(holder, scale_by, blocks[k], base, squares, pieces)
        if scale_by is None:
            base, squares = result
    return result


def send_order(heads):
    return [heads - 1] + list(range(1, heads - 1))


def solution(mesh):
    placed = (
        P("ctx", "head"),
        P("ctx", "head"),
        P("ctx", "head"),
        P("ctx", "head"),
        P("head", None, None),
        P("head", None, None),
        P("head", None, None),
        P("head"),
        P("head", None),
    )
    return jax.shard_map(step, mesh=mesh, in_specs=placed, out_specs=P(("ctx", "head"), None), check_vma=False)
```

```python
import functools
import math

import jax
import jax.numpy as jnp
from jax import lax
from jax.experimental import pallas as pl
from jax.experimental.pallas import tpu as pltpu
from jax.sharding import PartitionSpec as P


WINDOW = 256
EPSILON = 1e-06

VMEM = pl.BlockSpec(memory_space=pltpu.VMEM)
HBM = pl.BlockSpec(memory_space=pltpu.HBM)


def near_core(*arrays):
    return [pltpu.with_memory_space_constraint(a, pltpu.VMEM) for a in arrays]


def far_core(*arrays):
    return [pltpu.with_memory_space_constraint(a, pltpu.HBM) for a in arrays]


def grant(mib):
    return pltpu.CompilerParams(vmem_limit_bytes=mib << 20)


def swap(value, axis, mask):
    return lax.ppermute(value, axis, [(i, i ^ mask) for i in range(lax.axis_size(axis))])


def dot(left, right, left_dim=1, right_dim=0):
    return lax.dot_general(
        left, right, (((left_dim,), (right_dim,)), ((), ())), preferred_element_type=jnp.float32
    )


def place():
    me = lax.axis_index("ctx").astype(jnp.int32)
    return me & 1, ((me >> 1) ^ (me >> 2)) & 1


def column(row, width):
    tall = jnp.transpose(jnp.broadcast_to(row, (128, row.shape[1])))
    return jnp.concatenate([tall] * (width // 128), axis=1)


def load_kernel(k_hbm, v_hbm, gain_hbm, w_hbm, tail_ref, piece_ref, w_ref, gain_ref, sem):
    rows, columns = piece_ref.shape
    _, side = place()
    first = pl.multiple_of(side * rows, rows)
    last = pl.ds(k_hbm.shape[0] - WINDOW, WINDOW)
    steps = 4
    block = rows // steps
    moves = [(gain_hbm, gain_ref)]
    for i in range(steps):
        at = pl.ds(i * block, block)
        moves.append((w_hbm.at[pl.ds(first + i * block, block), :], w_ref.at[at, :]))
    moves += [(k_hbm.at[last, :], tail_ref.at[pl.ds(0, WINDOW), :])]
    moves += [(v_hbm.at[last, :], tail_ref.at[pl.ds(WINDOW, WINDOW), :])]
    copies = [pltpu.make_async_copy(src, dst, sem.at[j]) for j, (src, dst) in enumerate(moves)]
    for copy in copies:
        copy.start()
    copies[0].wait()
    gain = gain_ref[...].reshape(1, 2 * rows).astype(jnp.float32)
    gain = jnp.transpose(jnp.broadcast_to(jnp.where(side == 0, gain[:, :rows], gain[:, rows:]), (128, rows)))
    for i in range(steps):
        at = slice(i * block, (i + 1) * block)
        copies[1 + i].wait()
        for left in range(0, columns, 128):
            here = slice(left, left + 128)
            piece_ref[at, here] = (w_ref[at, here].astype(jnp.float32) * gain[at, :]).astype(jnp.bfloat16)
    for copy in copies[1 + steps :]:
        copy.wait()


def load(keys, values, gain, weight):
    piece = pltpu.VMEM((weight.shape[0] // 2, weight.shape[1]), jnp.bfloat16)
    return pl.pallas_call(
        load_kernel,
        out_shape=[pltpu.VMEM((2 * WINDOW, keys.shape[1]), jnp.bfloat16), piece],
        compiler_params=grant(8),
        in_specs=[HBM] * 4,
        out_specs=[VMEM] * 2,
        scratch_shapes=[piece, pltpu.VMEM(gain.shape, gain.dtype), pltpu.SemaphoreType.DMA((7,))],
        name="load",
    )(*far_core(keys, values, gain, weight))


def halves(width):
    core, _ = place()
    half = width // 2
    mine = pl.ds(pl.multiple_of(core * half, half), half)
    theirs = pl.ds(pl.multiple_of((1 - core) * half, half), half)
    return mine, theirs


def push_kernel(k_ref, v_ref, r_ref, w1_ref, w2_ref, w3_ref, give_ref, act_ref, sc_ref, g1_ref, g3_ref):
    rows, width = k_ref.shape
    steps = 4
    block = rows // steps
    for i in range(steps):
        at = slice(i * block, (i + 1) * block)
        k = k_ref[at, :]
        gate = dot(k, w1_ref[0])
        up = dot(k, w3_ref[0])
        rate = column(r_ref[:, at], width)
        scaled = (v_ref[at, :].astype(jnp.float32) * rate).astype(jnp.bfloat16)
        back = dot(scaled, w2_ref[0], 1, 1)
        s = jax.nn.sigmoid(gate)
        gs = gate * s
        act_ref[at, :] = (gs * up).astype(jnp.bfloat16)
        sc_ref[at, :] = scaled
        g1_ref[at, :] = (back * up * (s + gs * (1.0 - s))).astype(jnp.bfloat16)
        g3_ref[at, :] = (back * gs).astype(jnp.bfloat16)
    _, theirs = halves(width)
    for j, ref in enumerate((g1_ref, g3_ref)):
        give_ref[j] = dot(k_ref[...], ref[:, theirs], 0, 0).astype(jnp.bfloat16)


def pushes(keys, values, rates, w1, w2, w3):
    rows, width = keys.shape
    wide = pltpu.VMEM((rows, width), jnp.bfloat16)
    return pl.pallas_call(
        push_kernel,
        out_shape=[pltpu.VMEM((2, width, width // 2), jnp.bfloat16)] + [wide] * 4,
        compiler_params=grant(16),
        in_specs=[VMEM] * 6,
        out_specs=[VMEM] * 5,
        name="pushes",
    )(*near_core(keys, values, rates.reshape(1, rows), w1, w2, w3))


def contract_kernel(kept, left_ref, *refs):
    *rights, out_ref = refs
    mine, theirs = halves(left_ref.shape[1])
    for j, ref in enumerate(rights):
        out_ref[j] = dot(left_ref[...], ref[:, mine if kept else theirs], 0, 0).astype(out_ref.dtype)


def contract(kept, left, *rights):
    width = left.shape[1]
    dtype = jnp.float32 if kept else jnp.bfloat16
    return pl.pallas_call(
        functools.partial(contract_kernel, kept),
        out_shape=pltpu.VMEM((len(rights), width, width // 2), dtype),
        compiler_params=grant(12),
        in_specs=[VMEM] * (1 + len(rights)),
        out_specs=VMEM,
        name="contract",
    )(*near_core(left, *rights))


def add_kernel(keep_ref, got_ref, sum_ref, send_ref):
    total = keep_ref[...] + got_ref[...].astype(jnp.float32)
    sum_ref[...] = total
    send_ref[...] = total.astype(jnp.bfloat16)


def add(keep, got):
    return pl.pallas_call(
        add_kernel,
        out_shape=(pltpu.VMEM(keep.shape, jnp.float32), pltpu.VMEM(keep.shape, jnp.bfloat16)),
        compiler_params=grant(8),
        in_specs=[VMEM] * 2,
        out_specs=(VMEM,) * 2,
        name="add",
    )(*near_core(keep, got))


def renorm_kernel(keep_ref, got_ref, *refs):
    *weights, out_ref = refs
    half = keep_ref.shape[2]
    block = half // 2
    core, _ = place()
    for j, w_ref in enumerate(weights):
        for first in (0, block):
            at = slice(first, first + block)
            start = pl.multiple_of(core * half + first, block)
            old = w_ref[0, :, pl.ds(start, block)].astype(jnp.float32)
            new = old + (keep_ref[j, :, at] + got_ref[j, :, at].astype(jnp.float32))
            old_norm = jnp.sqrt(jnp.mean(old * old, axis=0, keepdims=True) + EPSILON)
            new_norm = jnp.sqrt(jnp.mean(new * new, axis=0, keepdims=True) + EPSILON)
            out_ref[j, :, at] = (new * (old_norm / new_norm)).astype(jnp.bfloat16)


def renorm(keep, got, *weights):
    return pl.pallas_call(
        renorm_kernel,
        out_shape=pltpu.VMEM(keep.shape, jnp.bfloat16),
        compiler_params=grant(8),
        in_specs=[VMEM] * (2 + len(weights)),
        out_specs=VMEM,
        name="renorm",
    )(*near_core(keep, got, *weights))


def window_kernel(q_hbm, k_hbm, v_hbm, tail_ref, out_ref, q_ref, k_ref, v_ref, sem):
    rows, width = q_ref.shape
    scale = 1.0 / math.sqrt(width)
    query = lax.broadcasted_iota(jnp.int32, (WINDOW, 2 * WINDOW), 0)
    key = lax.broadcasted_iota(jnp.int32, (WINDOW, 2 * WINDOW), 1)
    allowed = (key > query) & (key <= query + WINDOW)
    allowed_first = allowed & ((key >= WINDOW) | (lax.axis_index("ctx") > 0))
    count = rows // WINDOW
    loads = [[
        pltpu.make_async_copy(tail_ref.at[pl.ds(j * WINDOW, WINDOW), :], dst.at[pl.ds(0, WINDOW), :], sem.at[j])
        for j, dst in enumerate((k_ref, v_ref))
    ]]
    for i in range(count):
        at, after = pl.ds(i * WINDOW, WINDOW), pl.ds((i + 1) * WINDOW, WINDOW)
        loads.append([
            pltpu.make_async_copy(q_hbm.at[at, :], q_ref.at[at, :], sem.at[3 * i + 2]),
            pltpu.make_async_copy(k_hbm.at[at, :], k_ref.at[after, :], sem.at[3 * i + 3]),
            pltpu.make_async_copy(v_hbm.at[at, :], v_ref.at[after, :], sem.at[3 * i + 4]),
        ])
    for group in loads:
        for load in group:
            load.start()
    for load in loads[0]:
        load.wait()
    for i in range(count):
        for load in loads[i + 1]:
            load.wait()
        at = slice(i * WINDOW, (i + 1) * WINDOW)
        seen = slice(i * WINDOW, (i + 2) * WINDOW)
        scores = dot(q_ref[at, :], k_ref[seen, :], 1, 1) * scale
        scores = jnp.where(allowed_first if i == 0 else allowed, scores, -jnp.inf)
        peak = jnp.max(scores, axis=1, keepdims=True)
        exponent = jnp.exp(scores - peak)
        weights = exponent / jnp.sum(exponent, axis=1, keepdims=True)
        out_ref[at, :] = dot(weights.astype(jnp.bfloat16), v_ref[seen, :])


def window(queries, keys, values, tail):
    rows, width = queries.shape
    return pl.pallas_call(
        window_kernel,
        out_shape=pltpu.VMEM(queries.shape, jnp.float32),
        compiler_params=grant(24),
        in_specs=[HBM] * 3 + [VMEM],
        out_specs=VMEM,
        scratch_shapes=[pltpu.VMEM((rows, width), jnp.bfloat16)]
        + [pltpu.VMEM((rows + WINDOW, width), jnp.bfloat16)] * 2
        + [pltpu.SemaphoreType.DMA((2 + 3 * (rows // WINDOW),))],
        name="window",
    )(*far_core(queries, keys, values), *near_core(tail))


def apply_kernel(slot, q_ref, seen_ref, down_ref, up_ref, down_c_ref, up_c_ref, out_ref):
    rows, width = out_ref.shape
    own, rest = halves(width)
    here = pl.ds(pl.multiple_of((lax.axis_index("head").astype(jnp.int32) ^ slot) * rows, rows), rows)
    q = q_ref[here, :]
    mixed = []
    for ref in (up_ref, up_c_ref):
        gate = dot(q, ref[0])
        up = dot(q, ref[1])
        mixed.append((gate * jax.nn.sigmoid(gate) * up).astype(jnp.bfloat16))
    mixed = jnp.concatenate(mixed, axis=1)
    for ref, at in ((down_ref, own), (down_c_ref, rest)):
        down = jnp.concatenate([ref[0, own, :], ref[0, rest, :]], axis=0)
        out_ref[:, at] = (dot(mixed, down) + seen_ref[here, at]).astype(jnp.bfloat16)


def apply_fast(slot, queries, seen, weights, rows):
    return pl.pallas_call(
        functools.partial(apply_kernel, slot),
        out_shape=pltpu.VMEM((rows, queries.shape[1]), jnp.bfloat16),
        compiler_params=grant(16),
        in_specs=[VMEM] * 6,
        out_specs=VMEM,
        name="apply",
    )(*near_core(queries, seen, *weights))


def own_project_kernel(x_ref, gain_ref, w_ref, out_ref, squares_ref):
    wide = x_ref[...].astype(jnp.float32)
    squares_ref[...] = jnp.sum(wide * wide, axis=1, keepdims=True)
    gain = gain_ref[...].reshape(1, wide.shape[1]).astype(jnp.float32)
    x = (wide * gain).astype(jnp.bfloat16)
    out_ref[...] = dot(x, w_ref[...])


def own_project(x, gain, weight):
    return pl.pallas_call(
        own_project_kernel,
        out_shape=(
            pltpu.VMEM((x.shape[0], weight.shape[1]), jnp.float32),
            pltpu.VMEM((x.shape[0], 1), jnp.float32),
        ),
        compiler_params=grant(16),
        in_specs=[VMEM] * 3,
        out_specs=(VMEM, VMEM),
        name="own_project",
    )(*near_core(x, gain, weight))


def pick_kernel(early_ref, early_c_ref, out_ref, sem):
    columns = out_ref.shape[1]
    core, _ = place()
    here = pl.ds(pl.multiple_of(core * columns, columns), columns)

    @pl.when(core == 1)
    def _():
        copy = pltpu.make_async_copy(early_ref.at[:, here], out_ref, sem)
        copy.start()
        copy.wait()

    @pl.when(core == 0)
    def _():
        copy = pltpu.make_async_copy(early_c_ref.at[:, here], out_ref, sem)
        copy.start()
        copy.wait()


def pick(early, early_c):
    return pl.pallas_call(
        pick_kernel,
        out_shape=pltpu.VMEM((early.shape[0], early.shape[1] // 2), early.dtype),
        compiler_params=grant(4),
        in_specs=[VMEM] * 2,
        out_specs=VMEM,
        scratch_shapes=[pltpu.SemaphoreType.DMA],
        name="pick",
    )(*near_core(early, early_c))


def project_kernel(holder, scale_by, x_ref, base_ref, squares_ref, near, near_c, far, far_c,
                   out_ref, *rest):
    rows = near.shape[0]
    columns = out_ref.shape[1] // 2
    core, half = place()
    wide = x_ref[...].astype(jnp.float32)
    squares = squares_ref[...] + jnp.sum(wide * wide, axis=1, keepdims=True)
    mine = pl.ds(pl.multiple_of(half * rows, rows), rows)
    theirs = pl.ds(pl.multiple_of((1 - half) * rows, rows), rows)
    x = jnp.concatenate([x_ref[:, mine], x_ref[:, theirs]], axis=1)
    scale = lax.rsqrt(squares * scale_by + EPSILON) if scale_by else None
    block = columns // 2
    stores = []
    for side in range(2):
        for j in range(2):
            if holder is None:
                w_near, w_far = ((near, far), (near_c, far_c))[side]
                start = core if side == 0 else 1 - core
                here = slice(j * block, (j + 1) * block)
                w = jnp.concatenate([w_near[:, here], w_far[:, here]], axis=0)
                at = pl.ds(pl.multiple_of(start * columns + j * block, block), block)
            else:
                at = slice(side * columns + j * block, side * columns + (j + 1) * block)
                w = [jnp.where(core == holder, a[:, at], b[:, at]) for a, b in ((near, near_c), (far, far_c))]
                w = jnp.concatenate(w, axis=0)
            total = base_ref[:, at] + dot(x, w)
            if scale_by:
                ready_ref, sem = rest
                ready_ref[2 * side + j] = (total * scale).astype(jnp.bfloat16)
                store = pltpu.make_async_copy(ready_ref.at[2 * side + j], out_ref.at[:, at], sem.at[2 * side + j])
                store.start()
                stores.append(store)
            else:
                out_ref[:, at] = total
    if not scale_by:
        rest[0][...] = squares
    for store in stores:
        store.wait()


def project(holder, scale_by, x, base, squares, pieces):
    rows, columns = base.shape
    if scale_by:
        shape = jax.ShapeDtypeStruct((rows, columns), jnp.bfloat16)
        scratch = [pltpu.VMEM((4, rows, columns // 4), jnp.bfloat16), pltpu.SemaphoreType.DMA((4,))]
    else:
        shape = (pltpu.VMEM((rows, columns), jnp.float32), pltpu.VMEM((rows, 1), jnp.float32))
        scratch = []
    return pl.pallas_call(
        functools.partial(project_kernel, holder, scale_by),
        out_shape=shape,
        in_specs=[VMEM] * 7,
        out_specs=HBM if scale_by else (VMEM, VMEM),
        scratch_shapes=scratch,
        compiler_params=grant(16),
        name="project",
    )(*near_core(x, base, squares, *pieces))


def step(queries, keys, values, rates, fast_w1, fast_w2, fast_w3, norm_gain, out_weight):
    tok_rows, width = queries.shape
    ctx_count = lax.axis_size("ctx")
    heads = lax.axis_size("head")
    bits = ctx_count.bit_length() - 1
    assert ctx_count == 1 << bits and bits >= 3 and heads == 4

    tail, piece = load(keys, values, norm_gain, out_weight)
    tail = lax.ppermute(tail, "ctx", [(i, i + 1) for i in range(ctx_count - 1)])

    over = [(i, i ^ (2 if i // heads & 1 else 1)) for i in range(ctx_count * heads)]
    early = lax.ppermute(piece, ("ctx", "head"), over)
    early_c = swap(early, "ctx", 1)
    late = pick(early, early_c)
    late = swap(late, "head", 1)
    cross = [(i, i ^ (2 if i & 1 else 4)) for i in range(ctx_count)]
    early_far = lax.ppermute(early, "ctx", cross)
    late_far = lax.ppermute(late, "ctx", cross)
    late_c = swap(late, "ctx", 1)
    early_far_c = swap(early_far, "ctx", 1)
    late_far_c = swap(late_far, "ctx", 1)
    early_pieces = (early, early_c, early_far, early_far_c)
    late_pieces = (late, late_c, late_far, late_far_c)

    give_a, act, scaled, g1, g3 = pushes(keys, values, rates, fast_w1, fast_w2, fast_w3)
    give_b = contract(False, act, scaled)
    keep_a = contract(True, keys, g1, g3)
    keep_b = contract(True, act, scaled)

    masks = [1 << b for b in range(1, bits)]
    crossing = [
        [(i, i ^ (backward if i & 1 else forward)) for i in range(ctx_count)]
        for forward, backward in zip(masks, masks[::-1])
    ]
    weights = []
    for give, keep, olds in ((give_a, keep_a, (fast_w1, fast_w3)), (give_b, keep_b, (fast_w2,))):
        got = swap(give, "ctx", 1)
        for pairs in crossing:
            keep, send = add(keep, got)
            got = lax.ppermute(send, "ctx", pairs)
        mine = renorm(keep, got, *olds)
        other = swap(mine, "ctx", 1)
        weights.append((mine, other))
    weights = (weights[1][0], weights[0][0], weights[1][1], weights[0][1])

    seen = window(queries, keys, values, tail)

    rows = tok_rows // heads
    blocks = {}
    for k in send_order(heads) + [0]:
        combined = apply_fast(k, queries, seen, weights, rows)
        blocks[k] = swap(combined, "head", k) if k else combined
    base, squares = own_project(blocks[0], norm_gain, out_weight)
    for k in send_order(heads):
        holder, pieces = (None, late_pieces) if k == heads - 1 else (k - 1, early_pieces)
        scale_by = 1.0 / (heads * width) if k == send_order(heads)[-1] else None
        result = project(holder, scale_by, blocks[k], base, squares, pieces)
        if scale_by is None:
            base, squares = result
    return result


def send_order(heads):
    return [heads - 1] + list(range(1, heads - 1))


def solution(mesh):
    placed = (
        P("ctx", "head"),
        P("ctx", "head"),
        P("ctx", "head"),
        P("ctx", "head"),
        P("head", None, None),
        P("head", None, None),
        P("head", None, None),
        P("head"),
        P("head", None),
    )
    return jax.shard_map(step, mesh=mesh, in_specs=placed, out_specs=P(("ctx", "head"), None), check_vma=False)
```

```python
import functools
import math

import jax
import jax.numpy as jnp
from jax import lax
from jax.experimental import pallas as pl
from jax.experimental.pallas import tpu as pltpu
from jax.sharding import PartitionSpec as P


WINDOW = 256
EPSILON = 1e-06

VMEM = pl.BlockSpec(memory_space=pltpu.VMEM)
HBM = pl.BlockSpec(memory_space=pltpu.HBM)


def near_core(*arrays):
    return [pltpu.with_memory_space_constraint(a, pltpu.VMEM) for a in arrays]


def far_core(*arrays):
    return [pltpu.with_memory_space_constraint(a, pltpu.HBM) for a in arrays]


def grant(mib):
    return pltpu.CompilerParams(vmem_limit_bytes=mib << 20)


def swap(value, axis, mask):
    return lax.ppermute(value, axis, [(i, i ^ mask) for i in range(lax.axis_size(axis))])


def dot(left, right, left_dim=1, right_dim=0):
    return lax.dot_general(
        left, right, (((left_dim,), (right_dim,)), ((), ())), preferred_element_type=jnp.float32
    )


def place():
    me = lax.axis_index("ctx").astype(jnp.int32)
    return me & 1, ((me >> 1) ^ (me >> 2)) & 1


def column(row, width):
    tall = jnp.transpose(jnp.broadcast_to(row, (128, row.shape[1])))
    return jnp.concatenate([tall] * (width // 128), axis=1)


def load_kernel(k_hbm, v_hbm, gain_hbm, w_hbm, tail_ref, piece_ref, w_ref, gain_ref, sem):
    rows, columns = piece_ref.shape
    _, side = place()
    first = pl.multiple_of(side * rows, rows)
    last = pl.ds(k_hbm.shape[0] - WINDOW, WINDOW)
    steps = 4
    block = rows // steps
    moves = [(gain_hbm, gain_ref)]
    for i in range(steps):
        at = pl.ds(i * block, block)
        moves.append((w_hbm.at[pl.ds(first + i * block, block), :], w_ref.at[at, :]))
    moves += [(k_hbm.at[last, :], tail_ref.at[pl.ds(0, WINDOW), :])]
    moves += [(v_hbm.at[last, :], tail_ref.at[pl.ds(WINDOW, WINDOW), :])]
    copies = [pltpu.make_async_copy(src, dst, sem.at[j]) for j, (src, dst) in enumerate(moves)]
    for copy in copies:
        copy.start()
    copies[0].wait()
    gain = gain_ref[...].reshape(1, 2 * rows).astype(jnp.float32)
    gain = jnp.transpose(jnp.broadcast_to(jnp.where(side == 0, gain[:, :rows], gain[:, rows:]), (128, rows)))
    for i in range(steps):
        at = slice(i * block, (i + 1) * block)
        copies[1 + i].wait()
        for left in range(0, columns, 128):
            here = slice(left, left + 128)
            piece_ref[at, here] = (w_ref[at, here].astype(jnp.float32) * gain[at, :]).astype(jnp.bfloat16)
    for copy in copies[1 + steps :]:
        copy.wait()


def load(keys, values, gain, weight):
    piece = pltpu.VMEM((weight.shape[0] // 2, weight.shape[1]), jnp.bfloat16)
    return pl.pallas_call(
        load_kernel,
        out_shape=[pltpu.VMEM((2 * WINDOW, keys.shape[1]), jnp.bfloat16), piece],
        compiler_params=grant(8),
        in_specs=[HBM] * 4,
        out_specs=[VMEM] * 2,
        scratch_shapes=[piece, pltpu.VMEM(gain.shape, gain.dtype), pltpu.SemaphoreType.DMA((7,))],
        name="load",
    )(*far_core(keys, values, gain, weight))


def halves(width):
    core, _ = place()
    half = width // 2
    mine = pl.ds(pl.multiple_of(core * half, half), half)
    theirs = pl.ds(pl.multiple_of((1 - core) * half, half), half)
    return mine, theirs


def push_kernel(k_ref, v_ref, r_ref, w1_ref, w2_ref, w3_ref, give_ref, act_ref, sc_ref, g1_ref, g3_ref):
    rows, width = k_ref.shape
    steps = 4
    block = rows // steps
    for i in range(steps):
        at = slice(i * block, (i + 1) * block)
        k = k_ref[at, :]
        gate = dot(k, w1_ref[0])
        up = dot(k, w3_ref[0])
        rate = column(r_ref[:, at], width)
        scaled = (v_ref[at, :].astype(jnp.float32) * rate).astype(jnp.bfloat16)
        back = dot(scaled, w2_ref[0], 1, 1)
        s = jax.nn.sigmoid(gate)
        gs = gate * s
        act_ref[at, :] = (gs * up).astype(jnp.bfloat16)
        sc_ref[at, :] = scaled
        g1_ref[at, :] = (back * up * (s + gs * (1.0 - s))).astype(jnp.bfloat16)
        g3_ref[at, :] = (back * gs).astype(jnp.bfloat16)
    _, theirs = halves(width)
    for j, ref in enumerate((g1_ref, g3_ref)):
        give_ref[j] = dot(k_ref[...], ref[:, theirs], 0, 0).astype(jnp.bfloat16)


def pushes(keys, values, rates, w1, w2, w3):
    rows, width = keys.shape
    wide = pltpu.VMEM((rows, width), jnp.bfloat16)
    return pl.pallas_call(
        push_kernel,
        out_shape=[pltpu.VMEM((2, width, width // 2), jnp.bfloat16)] + [wide] * 4,
        compiler_params=grant(16),
        in_specs=[VMEM] * 6,
        out_specs=[VMEM] * 5,
        name="pushes",
    )(*near_core(keys, values, rates.reshape(1, rows), w1, w2, w3))


def contract_kernel(kept, left_ref, *refs):
    *rights, out_ref = refs
    mine, theirs = halves(left_ref.shape[1])
    for j, ref in enumerate(rights):
        out_ref[j] = dot(left_ref[...], ref[:, mine if kept else theirs], 0, 0).astype(out_ref.dtype)


def contract(kept, left, *rights):
    width = left.shape[1]
    dtype = jnp.float32 if kept else jnp.bfloat16
    return pl.pallas_call(
        functools.partial(contract_kernel, kept),
        out_shape=pltpu.VMEM((len(rights), width, width // 2), dtype),
        compiler_params=grant(12),
        in_specs=[VMEM] * (1 + len(rights)),
        out_specs=VMEM,
        name="contract",
    )(*near_core(left, *rights))


def add_kernel(keep_ref, got_ref, sum_ref, send_ref):
    total = keep_ref[...] + got_ref[...].astype(jnp.float32)
    sum_ref[...] = total
    send_ref[...] = total.astype(jnp.bfloat16)


def add(keep, got):
    return pl.pallas_call(
        add_kernel,
        out_shape=(pltpu.VMEM(keep.shape, jnp.float32), pltpu.VMEM(keep.shape, jnp.bfloat16)),
        compiler_params=grant(8),
        in_specs=[VMEM] * 2,
        out_specs=(VMEM,) * 2,
        name="add",
    )(*near_core(keep, got))


def renorm_kernel(keep_ref, got_ref, *refs):
    *weights, out_ref = refs
    half = keep_ref.shape[2]
    block = half // 2
    core, _ = place()
    for j, w_ref in enumerate(weights):
        for first in (0, block):
            at = slice(first, first + block)
            start = pl.multiple_of(core * half + first, block)
            old = w_ref[0, :, pl.ds(start, block)].astype(jnp.float32)
            new = old + (keep_ref[j, :, at] + got_ref[j, :, at].astype(jnp.float32))
            old_norm = jnp.sqrt(jnp.mean(old * old, axis=0, keepdims=True) + EPSILON)
            new_norm = jnp.sqrt(jnp.mean(new * new, axis=0, keepdims=True) + EPSILON)
            out_ref[j, :, at] = (new * (old_norm / new_norm)).astype(jnp.bfloat16)


def renorm(keep, got, *weights):
    return pl.pallas_call(
        renorm_kernel,
        out_shape=pltpu.VMEM(keep.shape, jnp.bfloat16),
        compiler_params=grant(8),
        in_specs=[VMEM] * (2 + len(weights)),
        out_specs=VMEM,
        name="renorm",
    )(*near_core(keep, got, *weights))


def window_kernel(q_hbm, k_hbm, v_hbm, tail_ref, out_ref, q_ref, k_ref, v_ref, sem):
    rows, width = q_ref.shape
    scale = 1.0 / math.sqrt(width)
    query = lax.broadcasted_iota(jnp.int32, (WINDOW, 2 * WINDOW), 0)
    key = lax.broadcasted_iota(jnp.int32, (WINDOW, 2 * WINDOW), 1)
    allowed = (key > query) & (key <= query + WINDOW)
    allowed_first = allowed & ((key >= WINDOW) | (lax.axis_index("ctx") > 0))
    count = rows // WINDOW
    loads = [[
        pltpu.make_async_copy(tail_ref.at[pl.ds(j * WINDOW, WINDOW), :], dst.at[pl.ds(0, WINDOW), :], sem.at[j])
        for j, dst in enumerate((k_ref, v_ref))
    ]]
    for i in range(count):
        at, after = pl.ds(i * WINDOW, WINDOW), pl.ds((i + 1) * WINDOW, WINDOW)
        loads.append([
            pltpu.make_async_copy(q_hbm.at[at, :], q_ref.at[at, :], sem.at[3 * i + 2]),
            pltpu.make_async_copy(k_hbm.at[at, :], k_ref.at[after, :], sem.at[3 * i + 3]),
            pltpu.make_async_copy(v_hbm.at[at, :], v_ref.at[after, :], sem.at[3 * i + 4]),
        ])
    for group in loads:
        for load in group:
            load.start()
    for load in loads[0]:
        load.wait()
    for i in range(count):
        for load in loads[i + 1]:
            load.wait()
        at = slice(i * WINDOW, (i + 1) * WINDOW)
        seen = slice(i * WINDOW, (i + 2) * WINDOW)
        scores = dot(q_ref[at, :], k_ref[seen, :], 1, 1) * scale
        scores = jnp.where(allowed_first if i == 0 else allowed, scores, -jnp.inf)
        peak = jnp.max(scores, axis=1, keepdims=True)
        exponent = jnp.exp(scores - peak)
        weights = exponent / jnp.sum(exponent, axis=1, keepdims=True)
        out_ref[at, :] = dot(weights.astype(jnp.bfloat16), v_ref[seen, :])


def window(queries, keys, values, tail):
    rows, width = queries.shape
    return pl.pallas_call(
        window_kernel,
        out_shape=pltpu.VMEM(queries.shape, jnp.float32),
        compiler_params=grant(24),
        in_specs=[HBM] * 3 + [VMEM],
        out_specs=VMEM,
        scratch_shapes=[pltpu.VMEM((rows, width), jnp.bfloat16)]
        + [pltpu.VMEM((rows + WINDOW, width), jnp.bfloat16)] * 2
        + [pltpu.SemaphoreType.DMA((2 + 3 * (rows // WINDOW),))],
        name="window",
    )(*far_core(queries, keys, values), *near_core(tail))


def apply_kernel(slot, q_ref, seen_ref, down_ref, up_ref, down_c_ref, up_c_ref, out_ref):
    rows, width = out_ref.shape
    own, rest = halves(width)
    here = pl.ds(pl.multiple_of((lax.axis_index("head").astype(jnp.int32) ^ slot) * rows, rows), rows)
    q = q_ref[here, :]
    mixed = []
    for ref in (up_ref, up_c_ref):
        gate = dot(q, ref[0])
        up = dot(q, ref[1])
        mixed.append((gate * jax.nn.sigmoid(gate) * up).astype(jnp.bfloat16))
    mixed = jnp.concatenate(mixed, axis=1)
    for ref, at in ((down_ref, own), (down_c_ref, rest)):
        down = jnp.concatenate([ref[0, own, :], ref[0, rest, :]], axis=0)
        out_ref[:, at] = (dot(mixed, down) + seen_ref[here, at]).astype(jnp.bfloat16)


def apply_fast(slot, queries, seen, weights, rows):
    return pl.pallas_call(
        functools.partial(apply_kernel, slot),
        out_shape=pltpu.VMEM((rows, queries.shape[1]), jnp.bfloat16),
        compiler_params=grant(16),
        in_specs=[VMEM] * 6,
        out_specs=VMEM,
        name="apply",
    )(*near_core(queries, seen, *weights))


def own_project_kernel(x_ref, gain_ref, w_ref, out_ref, squares_ref):
    wide = x_ref[...].astype(jnp.float32)
    squares_ref[...] = jnp.sum(wide * wide, axis=1, keepdims=True)
    gain = gain_ref[...].reshape(1, wide.shape[1]).astype(jnp.float32)
    x = (wide * gain).astype(jnp.bfloat16)
    out_ref[...] = dot(x, w_ref[...])


def own_project(x, gain, weight):
    return pl.pallas_call(
        own_project_kernel,
        out_shape=(
            pltpu.VMEM((x.shape[0], weight.shape[1]), jnp.float32),
            pltpu.VMEM((x.shape[0], 1), jnp.float32),
        ),
        compiler_params=grant(16),
        in_specs=[VMEM] * 3,
        out_specs=(VMEM, VMEM),
        name="own_project",
    )(*near_core(x, gain, weight))


def pick_kernel(early_ref, early_c_ref, out_ref, sem):
    columns = out_ref.shape[1]
    core, _ = place()
    here = pl.ds(pl.multiple_of(core * columns, columns), columns)

    @pl.when(core == 1)
    def _():
        copy = pltpu.make_async_copy(early_ref.at[:, here], out_ref, sem)
        copy.start()
        copy.wait()

    @pl.when(core == 0)
    def _():
        copy = pltpu.make_async_copy(early_c_ref.at[:, here], out_ref, sem)
        copy.start()
        copy.wait()


def pick(early, early_c):
    return pl.pallas_call(
        pick_kernel,
        out_shape=pltpu.VMEM((early.shape[0], early.shape[1] // 2), early.dtype),
        compiler_params=grant(4),
        in_specs=[VMEM] * 2,
        out_specs=VMEM,
        scratch_shapes=[pltpu.SemaphoreType.DMA],
        name="pick",
    )(*near_core(early, early_c))


def project_kernel(holder, scale_by, x_ref, base_ref, squares_ref, near, near_c, far, far_c, out_ref, *rest):
    rows = near.shape[0]
    columns = out_ref.shape[1] // 2
    core, half = place()
    wide = x_ref[...].astype(jnp.float32)
    squares = squares_ref[...] + jnp.sum(wide * wide, axis=1, keepdims=True)
    mine = pl.ds(pl.multiple_of(half * rows, rows), rows)
    theirs = pl.ds(pl.multiple_of((1 - half) * rows, rows), rows)
    x = jnp.concatenate([x_ref[:, mine], x_ref[:, theirs]], axis=1)
    scale = lax.rsqrt(squares * scale_by + EPSILON) if scale_by else None
    block = columns // 2
    split = far.shape[1] == columns
    stores = []
    for side in range(2):
        for j in range(2):
            here = slice(j * block, (j + 1) * block)
            start = (core if side == 0 else 1 - core) if split else side
            at = pl.ds(pl.multiple_of(start * columns + j * block, block), block)
            if split:
                w_far = (far, far_c)[side][:, here]
            else:
                w_far = jnp.where(core == holder, far[:, at], far_c[:, at])
            w = jnp.concatenate([jnp.where(core == holder, near[:, at], near_c[:, at]), w_far], axis=0)
            total = base_ref[:, at] + dot(x, w)
            if scale_by:
                ready_ref, sem = rest
                ready_ref[2 * side + j] = (total * scale).astype(jnp.bfloat16)
                store = pltpu.make_async_copy(ready_ref.at[2 * side + j], out_ref.at[:, at], sem.at[2 * side + j])
                store.start()
                stores.append(store)
            else:
                out_ref[:, at] = total
    if not scale_by:
        rest[0][...] = squares
    for store in stores:
        store.wait()


def project(holder, scale_by, x, base, squares, pieces):
    rows, columns = base.shape
    if scale_by:
        shape = jax.ShapeDtypeStruct((rows, columns), jnp.bfloat16)
        scratch = [pltpu.VMEM((4, rows, columns // 4), jnp.bfloat16), pltpu.SemaphoreType.DMA((4,))]
    else:
        shape = (pltpu.VMEM((rows, columns), jnp.float32), pltpu.VMEM((rows, 1), jnp.float32))
        scratch = []
    return pl.pallas_call(
        functools.partial(project_kernel, holder, scale_by),
        out_shape=shape,
        in_specs=[VMEM] * 7,
        out_specs=HBM if scale_by else (VMEM, VMEM),
        scratch_shapes=scratch,
        compiler_params=grant(16),
        name="project",
    )(*near_core(x, base, squares, *pieces))


def step(queries, keys, values, rates, fast_w1, fast_w2, fast_w3, norm_gain, out_weight):
    tok_rows, width = queries.shape
    ctx_count = lax.axis_size("ctx")
    heads = lax.axis_size("head")
    bits = ctx_count.bit_length() - 1
    assert ctx_count == 1 << bits and bits >= 3 and heads == 4

    tail, piece = load(keys, values, norm_gain, out_weight)
    tail = lax.ppermute(tail, "ctx", [(i, i + 1) for i in range(ctx_count - 1)])

    every = range(ctx_count * heads)
    over = [(i, i ^ (2 if i // heads & 1 else 1)) for i in every]
    early = lax.ppermute(piece, ("ctx", "head"), over)
    over = [(i, i ^ (1 if i // heads & 1 else 4 * heads)) for i in every]
    relay = lax.ppermute(early, ("ctx", "head"), over)
    early_far = lax.ppermute(early, "ctx", [(i, i ^ 2) for i in range(1, ctx_count, 2)])
    early_c = swap(early, "ctx", 1)
    relay_c = swap(relay, "ctx", 1)
    late = pick(relay, relay_c)
    late_far = lax.ppermute(late, "ctx", [(i, i ^ (2 if i & 1 else 4)) for i in range(ctx_count)])
    early_far_c = swap(early_far, "ctx", 1)
    late_far_c = swap(late_far, "ctx", 1)
    pieces = {
        1: (0, (early, early_c, relay, relay_c)),
        2: (1, (early, early_c, early_far, early_far_c)),
        3: (1, (relay, relay_c, late_far, late_far_c)),
    }

    give_a, act, scaled, g1, g3 = pushes(keys, values, rates, fast_w1, fast_w2, fast_w3)
    give_b = contract(False, act, scaled)
    keep_a = contract(True, keys, g1, g3)
    keep_b = contract(True, act, scaled)

    masks = [1 << b for b in range(1, bits)]
    crossing = [
        [(i, i ^ (backward if i & 1 else forward)) for i in range(ctx_count)]
        for forward, backward in zip(masks, masks[::-1])
    ]
    weights = []
    for give, keep, olds in ((give_a, keep_a, (fast_w1, fast_w3)), (give_b, keep_b, (fast_w2,))):
        got = swap(give, "ctx", 1)
        for pairs in crossing:
            keep, send = add(keep, got)
            got = lax.ppermute(send, "ctx", pairs)
        mine = renorm(keep, got, *olds)
        other = swap(mine, "ctx", 1)
        weights.append((mine, other))
    weights = (weights[1][0], weights[0][0], weights[1][1], weights[0][1])

    seen = window(queries, keys, values, tail)

    rows = tok_rows // heads
    blocks = {}
    for k in send_order(heads) + [0]:
        combined = apply_fast(k, queries, seen, weights, rows)
        blocks[k] = swap(combined, "head", k) if k else combined
    base, squares = own_project(blocks[0], norm_gain, out_weight)
    for k in send_order(heads):
        scale_by = 1.0 / (heads * width) if k == send_order(heads)[-1] else None
        holder, brought = pieces[k]
        result = project(holder, scale_by, blocks[k], base, squares, brought)
        if scale_by is None:
            base, squares = result
    return result


def send_order(heads):
    return [heads - 1] + list(range(1, heads - 1))


def solution(mesh):
    placed = (
        P("ctx", "head"),
        P("ctx", "head"),
        P("ctx", "head"),
        P("ctx", "head"),
        P("head", None, None),
        P("head", None, None),
        P("head", None, None),
        P("head"),
        P("head", None),
    )
    return jax.shard_map(step, mesh=mesh, in_specs=placed, out_specs=P(("ctx", "head"), None), check_vma=False)
```

```python
import functools
import math

import jax
import jax.numpy as jnp
from jax import lax
from jax.experimental import pallas as pl
from jax.experimental.pallas import tpu as pltpu
from jax.sharding import PartitionSpec as P


WINDOW = 256
EPSILON = 1e-06

VMEM = pl.BlockSpec(memory_space=pltpu.VMEM)
HBM = pl.BlockSpec(memory_space=pltpu.HBM)


def near_core(*arrays):
    return [pltpu.with_memory_space_constraint(a, pltpu.VMEM) for a in arrays]


def far_core(*arrays):
    return [pltpu.with_memory_space_constraint(a, pltpu.HBM) for a in arrays]


def grant(mib):
    return pltpu.CompilerParams(vmem_limit_bytes=mib << 20)


def swap(value, axis, mask):
    return lax.ppermute(value, axis, [(i, i ^ mask) for i in range(lax.axis_size(axis))])


def dot(left, right, left_dim=1, right_dim=0):
    return lax.dot_general(
        left, right, (((left_dim,), (right_dim,)), ((), ())), preferred_element_type=jnp.float32
    )


def place():
    me = lax.axis_index("ctx").astype(jnp.int32)
    return me & 1, ((me >> 1) ^ (me >> 2)) & 1


def column(row, width):
    tall = jnp.transpose(jnp.broadcast_to(row, (128, row.shape[1])))
    return jnp.concatenate([tall] * (width // 128), axis=1)


def load_kernel(k_hbm, v_hbm, gain_hbm, w_hbm, tail_ref, piece_ref, w_ref, gain_ref, sem):
    rows, columns = piece_ref.shape
    _, side = place()
    first = pl.multiple_of(side * rows, rows)
    last = pl.ds(k_hbm.shape[0] - WINDOW, WINDOW)
    steps = 4
    block = rows // steps
    moves = [(gain_hbm, gain_ref)]
    for i in range(steps):
        at = pl.ds(i * block, block)
        moves.append((w_hbm.at[pl.ds(first + i * block, block), :], w_ref.at[at, :]))
    moves += [(k_hbm.at[last, :], tail_ref.at[pl.ds(0, WINDOW), :])]
    moves += [(v_hbm.at[last, :], tail_ref.at[pl.ds(WINDOW, WINDOW), :])]
    copies = [pltpu.make_async_copy(src, dst, sem.at[j]) for j, (src, dst) in enumerate(moves)]
    for copy in copies:
        copy.start()
    copies[0].wait()
    gain = gain_ref[...].reshape(1, 2 * rows).astype(jnp.float32)
    gain = jnp.transpose(jnp.broadcast_to(jnp.where(side == 0, gain[:, :rows], gain[:, rows:]), (128, rows)))
    for i in range(steps):
        at = slice(i * block, (i + 1) * block)
        copies[1 + i].wait()
        for left in range(0, columns, 128):
            here = slice(left, left + 128)
            piece_ref[at, here] = (w_ref[at, here].astype(jnp.float32) * gain[at, :]).astype(jnp.bfloat16)
    for copy in copies[1 + steps :]:
        copy.wait()


def load(keys, values, gain, weight):
    piece = pltpu.VMEM((weight.shape[0] // 2, weight.shape[1]), jnp.bfloat16)
    return pl.pallas_call(
        load_kernel,
        out_shape=[pltpu.VMEM((2 * WINDOW, keys.shape[1]), jnp.bfloat16), piece],
        compiler_params=grant(8),
        in_specs=[HBM] * 4,
        out_specs=[VMEM] * 2,
        scratch_shapes=[piece, pltpu.VMEM(gain.shape, gain.dtype), pltpu.SemaphoreType.DMA((7,))],
        name="load",
    )(*far_core(keys, values, gain, weight))


def halves(width):
    core, _ = place()
    half = width // 2
    mine = pl.ds(pl.multiple_of(core * half, half), half)
    theirs = pl.ds(pl.multiple_of((1 - core) * half, half), half)
    return mine, theirs


def push_kernel(k_ref, v_ref, r_ref, w1_ref, w2_ref, w3_ref, give_ref, act_ref, sc_ref, g1_ref, g3_ref):
    rows, width = k_ref.shape
    steps = 4
    block = rows // steps
    for i in range(steps):
        at = slice(i * block, (i + 1) * block)
        k = k_ref[at, :]
        gate = dot(k, w1_ref[0])
        up = dot(k, w3_ref[0])
        rate = column(r_ref[:, at], width)
        scaled = (v_ref[at, :].astype(jnp.float32) * rate).astype(jnp.bfloat16)
        back = dot(scaled, w2_ref[0], 1, 1)
        s = jax.nn.sigmoid(gate)
        gs = gate * s
        act_ref[at, :] = (gs * up).astype(jnp.bfloat16)
        sc_ref[at, :] = scaled
        g1_ref[at, :] = (back * up * (s + gs * (1.0 - s))).astype(jnp.bfloat16)
        g3_ref[at, :] = (back * gs).astype(jnp.bfloat16)
    _, theirs = halves(width)
    for j, ref in enumerate((g1_ref, g3_ref)):
        give_ref[j] = dot(k_ref[...], ref[:, theirs], 0, 0).astype(jnp.bfloat16)


def pushes(keys, values, rates, w1, w2, w3):
    rows, width = keys.shape
    wide = pltpu.VMEM((rows, width), jnp.bfloat16)
    return pl.pallas_call(
        push_kernel,
        out_shape=[pltpu.VMEM((2, width, width // 2), jnp.bfloat16)] + [wide] * 4,
        compiler_params=grant(16),
        in_specs=[VMEM] * 6,
        out_specs=[VMEM] * 5,
        name="pushes",
    )(*near_core(keys, values, rates.reshape(1, rows), w1, w2, w3))


def contract_kernel(kept, left_ref, *refs):
    *rights, out_ref = refs
    mine, theirs = halves(left_ref.shape[1])
    for j, ref in enumerate(rights):
        out_ref[j] = dot(left_ref[...], ref[:, mine if kept else theirs], 0, 0).astype(out_ref.dtype)


def contract(kept, left, *rights):
    width = left.shape[1]
    dtype = jnp.float32 if kept else jnp.bfloat16
    return pl.pallas_call(
        functools.partial(contract_kernel, kept),
        out_shape=pltpu.VMEM((len(rights), width, width // 2), dtype),
        compiler_params=grant(12),
        in_specs=[VMEM] * (1 + len(rights)),
        out_specs=VMEM,
        name="contract",
    )(*near_core(left, *rights))


def add_kernel(keep_ref, got_ref, sum_ref, send_ref):
    total = keep_ref[...] + got_ref[...].astype(jnp.float32)
    sum_ref[...] = total
    send_ref[...] = total.astype(jnp.bfloat16)


def add(keep, got):
    return pl.pallas_call(
        add_kernel,
        out_shape=(pltpu.VMEM(keep.shape, jnp.float32), pltpu.VMEM(keep.shape, jnp.bfloat16)),
        compiler_params=grant(8),
        in_specs=[VMEM] * 2,
        out_specs=(VMEM,) * 2,
        name="add",
    )(*near_core(keep, got))


def renorm_kernel(keep_ref, got_ref, *refs):
    *weights, out_ref = refs
    half = keep_ref.shape[2]
    block = half // 2
    core, _ = place()
    for j, w_ref in enumerate(weights):
        for first in (0, block):
            at = slice(first, first + block)
            start = pl.multiple_of(core * half + first, block)
            old = w_ref[0, :, pl.ds(start, block)].astype(jnp.float32)
            new = old + (keep_ref[j, :, at] + got_ref[j, :, at].astype(jnp.float32))
            old_norm = jnp.sqrt(jnp.mean(old * old, axis=0, keepdims=True) + EPSILON)
            new_norm = jnp.sqrt(jnp.mean(new * new, axis=0, keepdims=True) + EPSILON)
            out_ref[j, :, at] = (new * (old_norm / new_norm)).astype(jnp.bfloat16)


def renorm(keep, got, *weights):
    return pl.pallas_call(
        renorm_kernel,
        out_shape=pltpu.VMEM(keep.shape, jnp.bfloat16),
        compiler_params=grant(8),
        in_specs=[VMEM] * (2 + len(weights)),
        out_specs=VMEM,
        name="renorm",
    )(*near_core(keep, got, *weights))


def window_kernel(q_hbm, k_hbm, v_hbm, tail_ref, out_ref, q_ref, k_ref, v_ref, sem):
    rows, width = q_ref.shape
    scale = 1.0 / math.sqrt(width)
    query = lax.broadcasted_iota(jnp.int32, (WINDOW, 2 * WINDOW), 0)
    key = lax.broadcasted_iota(jnp.int32, (WINDOW, 2 * WINDOW), 1)
    allowed = (key > query) & (key <= query + WINDOW)
    allowed_first = allowed & ((key >= WINDOW) | (lax.axis_index("ctx") > 0))
    count = rows // WINDOW
    loads = [[
        pltpu.make_async_copy(tail_ref.at[pl.ds(j * WINDOW, WINDOW), :], dst.at[pl.ds(0, WINDOW), :], sem.at[j])
        for j, dst in enumerate((k_ref, v_ref))
    ]]
    for i in range(count):
        at, after = pl.ds(i * WINDOW, WINDOW), pl.ds((i + 1) * WINDOW, WINDOW)
        loads.append([
            pltpu.make_async_copy(q_hbm.at[at, :], q_ref.at[at, :], sem.at[3 * i + 2]),
            pltpu.make_async_copy(k_hbm.at[at, :], k_ref.at[after, :], sem.at[3 * i + 3]),
            pltpu.make_async_copy(v_hbm.at[at, :], v_ref.at[after, :], sem.at[3 * i + 4]),
        ])
    for group in loads:
        for load in group:
            load.start()
    for load in loads[0]:
        load.wait()
    for i in range(count):
        for load in loads[i + 1]:
            load.wait()
        at = slice(i * WINDOW, (i + 1) * WINDOW)
        seen = slice(i * WINDOW, (i + 2) * WINDOW)
        scores = dot(q_ref[at, :], k_ref[seen, :], 1, 1) * scale
        scores = jnp.where(allowed_first if i == 0 else allowed, scores, -jnp.inf)
        peak = jnp.max(scores, axis=1, keepdims=True)
        exponent = jnp.exp(scores - peak)
        weights = exponent / jnp.sum(exponent, axis=1, keepdims=True)
        out_ref[at, :] = dot(weights.astype(jnp.bfloat16), v_ref[seen, :])


def window(queries, keys, values, tail):
    rows, width = queries.shape
    return pl.pallas_call(
        window_kernel,
        out_shape=pltpu.VMEM(queries.shape, jnp.float32),
        compiler_params=grant(24),
        in_specs=[HBM] * 3 + [VMEM],
        out_specs=VMEM,
        scratch_shapes=[pltpu.VMEM((rows, width), jnp.bfloat16)]
        + [pltpu.VMEM((rows + WINDOW, width), jnp.bfloat16)] * 2
        + [pltpu.SemaphoreType.DMA((2 + 3 * (rows // WINDOW),))],
        name="window",
    )(*far_core(queries, keys, values), *near_core(tail))


def apply_kernel(slot, q_ref, seen_ref, down_ref, up_ref, down_c_ref, up_c_ref, out_ref):
    rows, width = out_ref.shape
    own, rest = halves(width)
    here = pl.ds(pl.multiple_of((lax.axis_index("head").astype(jnp.int32) ^ slot) * rows, rows), rows)
    q = q_ref[here, :]
    mixed = []
    for ref in (up_ref, up_c_ref):
        gate = dot(q, ref[0])
        up = dot(q, ref[1])
        mixed.append((gate * jax.nn.sigmoid(gate) * up).astype(jnp.bfloat16))
    mixed = jnp.concatenate(mixed, axis=1)
    for ref, at in ((down_ref, own), (down_c_ref, rest)):
        down = jnp.concatenate([ref[0, own, :], ref[0, rest, :]], axis=0)
        out_ref[:, at] = (dot(mixed, down) + seen_ref[here, at]).astype(jnp.bfloat16)


def apply_fast(slot, queries, seen, weights, rows):
    return pl.pallas_call(
        functools.partial(apply_kernel, slot),
        out_shape=pltpu.VMEM((rows, queries.shape[1]), jnp.bfloat16),
        compiler_params=grant(16),
        in_specs=[VMEM] * 6,
        out_specs=VMEM,
        name="apply",
    )(*near_core(queries, seen, *weights))


def own_project_kernel(x_ref, gain_ref, w_ref, out_ref, squares_ref):
    wide = x_ref[...].astype(jnp.float32)
    squares_ref[...] = jnp.sum(wide * wide, axis=1, keepdims=True)
    gain = gain_ref[...].reshape(1, wide.shape[1]).astype(jnp.float32)
    x = (wide * gain).astype(jnp.bfloat16)
    out_ref[...] = dot(x, w_ref[...])


def own_project(x, gain, weight):
    return pl.pallas_call(
        own_project_kernel,
        out_shape=(
            pltpu.VMEM((x.shape[0], weight.shape[1]), jnp.float32),
            pltpu.VMEM((x.shape[0], 1), jnp.float32),
        ),
        compiler_params=grant(16),
        in_specs=[VMEM] * 3,
        out_specs=(VMEM, VMEM),
        name="own_project",
    )(*near_core(x, gain, weight))


def split_kernel(whole_ref, left_ref, right_ref, sem):
    columns = left_ref.shape[1]
    copies = [
        pltpu.make_async_copy(whole_ref.at[:, pl.ds(j * columns, columns)], out, sem.at[j])
        for j, out in enumerate((left_ref, right_ref))
    ]
    for copy in copies:
        copy.start()
    for copy in copies:
        copy.wait()


def split(whole):
    half = pltpu.VMEM((whole.shape[0], whole.shape[1] // 2), whole.dtype)
    return pl.pallas_call(
        split_kernel,
        out_shape=(half, half),
        compiler_params=grant(4),
        in_specs=[VMEM],
        out_specs=(VMEM, VMEM),
        scratch_shapes=[pltpu.SemaphoreType.DMA((2,))],
        name="split",
    )(*near_core(whole))


def project_kernel(holder, scale_by, x_ref, base_ref, squares_ref, *refs):
    count = (len(refs) - (3 if scale_by else 2)) // 2
    brought, copied = refs[:count], refs[count : 2 * count]
    out_ref, *rest = refs[2 * count :]
    rows, columns = brought[0].shape
    core, half = place()
    wide = x_ref[...].astype(jnp.float32)
    squares = squares_ref[...] + jnp.sum(wide * wide, axis=1, keepdims=True)
    mine = pl.ds(pl.multiple_of(half * rows, rows), rows)
    theirs = pl.ds(pl.multiple_of((1 - half) * rows, rows), rows)
    x = jnp.concatenate([x_ref[:, mine], x_ref[:, theirs]], axis=1)
    scale = lax.rsqrt(squares * scale_by + EPSILON) if scale_by else None
    block = columns // 4
    stores = []
    for j in range(4):
        at = slice(j * block, (j + 1) * block)
        far, here = (1, at) if count == 2 else (1 + j // 2, slice(j % 2 * block, (j % 2 + 1) * block))
        w_near = jnp.where(core == holder, brought[0][:, at], copied[0][:, at])
        w_far = jnp.where(core == holder, brought[far][:, here], copied[far][:, here])
        total = base_ref[:, at] + dot(x, jnp.concatenate([w_near, w_far], axis=0))
        if scale_by:
            ready_ref, sem = rest
            ready_ref[j] = (total * scale).astype(jnp.bfloat16)
            store = pltpu.make_async_copy(ready_ref.at[j], out_ref.at[:, pl.ds(j * block, block)], sem.at[j])
            store.start()
            stores.append(store)
        else:
            out_ref[:, at] = total
    if not scale_by:
        rest[0][...] = squares
    for store in stores:
        store.wait()


def project(holder, scale_by, x, base, squares, pieces):
    rows, columns = base.shape
    if scale_by:
        shape = jax.ShapeDtypeStruct((rows, columns), jnp.bfloat16)
        scratch = [pltpu.VMEM((4, rows, columns // 4), jnp.bfloat16), pltpu.SemaphoreType.DMA((4,))]
    else:
        shape = (pltpu.VMEM((rows, columns), jnp.float32), pltpu.VMEM((rows, 1), jnp.float32))
        scratch = []
    return pl.pallas_call(
        functools.partial(project_kernel, holder, scale_by),
        out_shape=shape,
        in_specs=[VMEM] * (3 + len(pieces)),
        out_specs=HBM if scale_by else (VMEM, VMEM),
        scratch_shapes=scratch,
        compiler_params=grant(16),
        name="project",
    )(*near_core(x, base, squares, *pieces))


def step(queries, keys, values, rates, fast_w1, fast_w2, fast_w3, norm_gain, out_weight):
    tok_rows, width = queries.shape
    ctx_count = lax.axis_size("ctx")
    heads = lax.axis_size("head")
    bits = ctx_count.bit_length() - 1
    assert ctx_count == 1 << bits and bits >= 3 and heads == 4

    tail, piece = load(keys, values, norm_gain, out_weight)
    tail = lax.ppermute(tail, "ctx", [(i, i + 1) for i in range(ctx_count - 1)])

    every = range(ctx_count * heads)
    over = [(i, i ^ (2 if i // heads & 1 else 1)) for i in every]
    early = lax.ppermute(piece, ("ctx", "head"), over)
    over = [(i, i ^ (1 if i // heads & 1 else 4 * heads)) for i in every]
    relay = lax.ppermute(early, ("ctx", "head"), over)
    early_far = lax.ppermute(early, "ctx", [(i, i ^ 2) for i in range(1, ctx_count, 2)])
    early_c = swap(early, "ctx", 1)
    relay_c = swap(relay, "ctx", 1)
    left, right = split(relay)
    late_x = lax.ppermute(left, "ctx", [(i, i ^ 2) for i in range(1, ctx_count, 2)])
    late_y = lax.ppermute(right, "ctx", [(i, i ^ 4) for i in range(1, ctx_count, 2)])
    early_far_c = swap(early_far, "ctx", 1)
    late_x_c = swap(late_x, "ctx", 1)
    late_y_c = swap(late_y, "ctx", 1)
    pieces = {
        1: (0, (early, relay, early_c, relay_c)),
        2: (1, (early, early_far, early_c, early_far_c)),
        3: (1, (relay, late_x, late_y, relay_c, late_x_c, late_y_c)),
    }

    give_a, act, scaled, g1, g3 = pushes(keys, values, rates, fast_w1, fast_w2, fast_w3)
    give_b = contract(False, act, scaled)
    keep_a = contract(True, keys, g1, g3)
    keep_b = contract(True, act, scaled)

    masks = [1 << b for b in range(1, bits)]
    crossing = [
        [(i, i ^ (backward if i & 1 else forward)) for i in range(ctx_count)]
        for forward, backward in zip(masks, masks[::-1])
    ]
    weights = []
    for give, keep, olds in ((give_a, keep_a, (fast_w1, fast_w3)), (give_b, keep_b, (fast_w2,))):
        got = swap(give, "ctx", 1)
        for pairs in crossing:
            keep, send = add(keep, got)
            got = lax.ppermute(send, "ctx", pairs)
        mine = renorm(keep, got, *olds)
        other = swap(mine, "ctx", 1)
        weights.append((mine, other))
    weights = (weights[1][0], weights[0][0], weights[1][1], weights[0][1])

    seen = window(queries, keys, values, tail)

    rows = tok_rows // heads
    blocks = {}
    for k in send_order(heads) + [0]:
        combined = apply_fast(k, queries, seen, weights, rows)
        blocks[k] = swap(combined, "head", k) if k else combined
    base, squares = own_project(blocks[0], norm_gain, out_weight)
    for k in (1, 3, 2):
        scale_by = 1.0 / (heads * width) if k == 2 else None
        holder, brought = pieces[k]
        result = project(holder, scale_by, blocks[k], base, squares, brought)
        if scale_by is None:
            base, squares = result
    return result


def send_order(heads):
    return [heads - 1] + list(range(1, heads - 1))


def solution(mesh):
    placed = (
        P("ctx", "head"),
        P("ctx", "head"),
        P("ctx", "head"),
        P("ctx", "head"),
        P("head", None, None),
        P("head", None, None),
        P("head", None, None),
        P("head"),
        P("head", None),
    )
    return jax.shard_map(step, mesh=mesh, in_specs=placed, out_specs=P(("ctx", "head"), None), check_vma=False)
```

```python
import functools
import math

import jax
import jax.numpy as jnp
from jax import lax
from jax.experimental import pallas as pl
from jax.experimental.pallas import tpu as pltpu
from jax.sharding import PartitionSpec as P


WINDOW = 256
EPSILON = 1e-06

VMEM = pl.BlockSpec(memory_space=pltpu.VMEM)
HBM = pl.BlockSpec(memory_space=pltpu.HBM)


def near_core(*arrays):
    return [pltpu.with_memory_space_constraint(a, pltpu.VMEM) for a in arrays]


def far_core(*arrays):
    return [pltpu.with_memory_space_constraint(a, pltpu.HBM) for a in arrays]


def grant(mib):
    return pltpu.CompilerParams(vmem_limit_bytes=mib << 20)


def swap(value, axis, mask):
    return lax.ppermute(value, axis, [(i, i ^ mask) for i in range(lax.axis_size(axis))])


def dot(left, right, left_dim=1, right_dim=0):
    return lax.dot_general(
        left, right, (((left_dim,), (right_dim,)), ((), ())), preferred_element_type=jnp.float32
    )


def place():
    me = lax.axis_index("ctx").astype(jnp.int32)
    return me & 1, ((me >> 1) ^ (me >> 2)) & 1


def column(row, width):
    tall = jnp.transpose(jnp.broadcast_to(row, (128, row.shape[1])))
    return jnp.concatenate([tall] * (width // 128), axis=1)


def load_kernel(k_hbm, v_hbm, gain_hbm, w_hbm, tail_ref, low_ref, high_ref, w_ref, gain_ref, sem):
    rows, columns = w_ref.shape
    _, side = place()
    first = pl.multiple_of(side * rows, rows)
    last = pl.ds(k_hbm.shape[0] - WINDOW, WINDOW)
    steps = 4
    block = rows // steps
    moves = [(gain_hbm, gain_ref)]
    for i in range(steps):
        at = pl.ds(i * block, block)
        moves.append((w_hbm.at[pl.ds(first + i * block, block), :], w_ref.at[at, :]))
    moves += [(k_hbm.at[last, :], tail_ref.at[pl.ds(0, WINDOW), :])]
    moves += [(v_hbm.at[last, :], tail_ref.at[pl.ds(WINDOW, WINDOW), :])]
    copies = [pltpu.make_async_copy(src, dst, sem.at[j]) for j, (src, dst) in enumerate(moves)]
    for copy in copies:
        copy.start()
    copies[0].wait()
    gain = gain_ref[...].reshape(1, 2 * rows).astype(jnp.float32)
    gain = jnp.transpose(jnp.broadcast_to(jnp.where(side == 0, gain[:, :rows], gain[:, rows:]), (128, rows)))
    for i in range(steps):
        at = slice(i * block, (i + 1) * block)
        copies[1 + i].wait()
        to_ref, to = (low_ref, at) if i < steps // 2 else (high_ref, slice((i - 2) * block, (i - 1) * block))
        for left in range(0, columns, 128):
            here = slice(left, left + 128)
            to_ref[to, here] = (w_ref[at, here].astype(jnp.float32) * gain[at, :]).astype(jnp.bfloat16)
    for copy in copies[1 + steps :]:
        copy.wait()


def load(keys, values, gain, weight):
    piece = pltpu.VMEM((weight.shape[0] // 2, weight.shape[1]), jnp.bfloat16)
    chunk = pltpu.VMEM((weight.shape[0] // 4, weight.shape[1]), jnp.bfloat16)
    return pl.pallas_call(
        load_kernel,
        out_shape=[pltpu.VMEM((2 * WINDOW, keys.shape[1]), jnp.bfloat16), chunk, chunk],
        compiler_params=grant(8),
        in_specs=[HBM] * 4,
        out_specs=[VMEM] * 3,
        scratch_shapes=[piece, pltpu.VMEM(gain.shape, gain.dtype), pltpu.SemaphoreType.DMA((7,))],
        name="load",
    )(*far_core(keys, values, gain, weight))


def halves(width):
    core, _ = place()
    half = width // 2
    mine = pl.ds(pl.multiple_of(core * half, half), half)
    theirs = pl.ds(pl.multiple_of((1 - core) * half, half), half)
    return mine, theirs


def push_kernel(k_ref, v_ref, r_ref, w1_ref, w2_ref, w3_ref, give_ref, act_ref, sc_ref, g1_ref, g3_ref):
    rows, width = k_ref.shape
    steps = 4
    block = rows // steps
    for i in range(steps):
        at = slice(i * block, (i + 1) * block)
        k = k_ref[at, :]
        gate = dot(k, w1_ref[0])
        up = dot(k, w3_ref[0])
        rate = column(r_ref[:, at], width)
        scaled = (v_ref[at, :].astype(jnp.float32) * rate).astype(jnp.bfloat16)
        back = dot(scaled, w2_ref[0], 1, 1)
        s = jax.nn.sigmoid(gate)
        gs = gate * s
        act_ref[at, :] = (gs * up).astype(jnp.bfloat16)
        sc_ref[at, :] = scaled
        g1_ref[at, :] = (back * up * (s + gs * (1.0 - s))).astype(jnp.bfloat16)
        g3_ref[at, :] = (back * gs).astype(jnp.bfloat16)
    _, theirs = halves(width)
    for j, ref in enumerate((g1_ref, g3_ref)):
        give_ref[j] = dot(k_ref[...], ref[:, theirs], 0, 0).astype(jnp.bfloat16)


def pushes(keys, values, rates, w1, w2, w3):
    rows, width = keys.shape
    wide = pltpu.VMEM((rows, width), jnp.bfloat16)
    return pl.pallas_call(
        push_kernel,
        out_shape=[pltpu.VMEM((2, width, width // 2), jnp.bfloat16)] + [wide] * 4,
        compiler_params=grant(16),
        in_specs=[VMEM] * 6,
        out_specs=[VMEM] * 5,
        name="pushes",
    )(*near_core(keys, values, rates.reshape(1, rows), w1, w2, w3))


def contract_kernel(kept, left_ref, *refs):
    *rights, out_ref = refs
    mine, theirs = halves(left_ref.shape[1])
    for j, ref in enumerate(rights):
        out_ref[j] = dot(left_ref[...], ref[:, mine if kept else theirs], 0, 0).astype(out_ref.dtype)


def contract(kept, left, *rights):
    width = left.shape[1]
    dtype = jnp.float32 if kept else jnp.bfloat16
    return pl.pallas_call(
        functools.partial(contract_kernel, kept),
        out_shape=pltpu.VMEM((len(rights), width, width // 2), dtype),
        compiler_params=grant(12),
        in_specs=[VMEM] * (1 + len(rights)),
        out_specs=VMEM,
        name="contract",
    )(*near_core(left, *rights))


def add_kernel(keep_ref, got_ref, sum_ref, send_ref):
    total = keep_ref[...] + got_ref[...].astype(jnp.float32)
    sum_ref[...] = total
    send_ref[...] = total.astype(jnp.bfloat16)


def add(keep, got):
    return pl.pallas_call(
        add_kernel,
        out_shape=(pltpu.VMEM(keep.shape, jnp.float32), pltpu.VMEM(keep.shape, jnp.bfloat16)),
        compiler_params=grant(8),
        in_specs=[VMEM] * 2,
        out_specs=(VMEM,) * 2,
        name="add",
    )(*near_core(keep, got))


def renorm_kernel(keep_ref, got_ref, *refs):
    *weights, out_ref = refs
    half = keep_ref.shape[2]
    block = half // 2
    core, _ = place()
    for j, w_ref in enumerate(weights):
        for first in (0, block):
            at = slice(first, first + block)
            start = pl.multiple_of(core * half + first, block)
            old = w_ref[0, :, pl.ds(start, block)].astype(jnp.float32)
            new = old + (keep_ref[j, :, at] + got_ref[j, :, at].astype(jnp.float32))
            old_norm = jnp.sqrt(jnp.mean(old * old, axis=0, keepdims=True) + EPSILON)
            new_norm = jnp.sqrt(jnp.mean(new * new, axis=0, keepdims=True) + EPSILON)
            out_ref[j, :, at] = (new * (old_norm / new_norm)).astype(jnp.bfloat16)


def renorm(keep, got, *weights):
    return pl.pallas_call(
        renorm_kernel,
        out_shape=pltpu.VMEM(keep.shape, jnp.bfloat16),
        compiler_params=grant(8),
        in_specs=[VMEM] * (2 + len(weights)),
        out_specs=VMEM,
        name="renorm",
    )(*near_core(keep, got, *weights))


def window_kernel(q_hbm, k_hbm, v_hbm, tail_ref, out_ref, q_ref, k_ref, v_ref, sem):
    rows, width = q_ref.shape
    scale = 1.0 / math.sqrt(width)
    query = lax.broadcasted_iota(jnp.int32, (WINDOW, 2 * WINDOW), 0)
    key = lax.broadcasted_iota(jnp.int32, (WINDOW, 2 * WINDOW), 1)
    allowed = (key > query) & (key <= query + WINDOW)
    allowed_first = allowed & ((key >= WINDOW) | (lax.axis_index("ctx") > 0))
    count = rows // WINDOW
    loads = [[
        pltpu.make_async_copy(tail_ref.at[pl.ds(j * WINDOW, WINDOW), :], dst.at[pl.ds(0, WINDOW), :], sem.at[j])
        for j, dst in enumerate((k_ref, v_ref))
    ]]
    for i in range(count):
        at, after = pl.ds(i * WINDOW, WINDOW), pl.ds((i + 1) * WINDOW, WINDOW)
        loads.append([
            pltpu.make_async_copy(q_hbm.at[at, :], q_ref.at[at, :], sem.at[3 * i + 2]),
            pltpu.make_async_copy(k_hbm.at[at, :], k_ref.at[after, :], sem.at[3 * i + 3]),
            pltpu.make_async_copy(v_hbm.at[at, :], v_ref.at[after, :], sem.at[3 * i + 4]),
        ])
    for group in loads:
        for load in group:
            load.start()
    for load in loads[0]:
        load.wait()
    for i in range(count):
        for load in loads[i + 1]:
            load.wait()
        at = slice(i * WINDOW, (i + 1) * WINDOW)
        seen = slice(i * WINDOW, (i + 2) * WINDOW)
        scores = dot(q_ref[at, :], k_ref[seen, :], 1, 1) * scale
        scores = jnp.where(allowed_first if i == 0 else allowed, scores, -jnp.inf)
        peak = jnp.max(scores, axis=1, keepdims=True)
        exponent = jnp.exp(scores - peak)
        weights = exponent / jnp.sum(exponent, axis=1, keepdims=True)
        out_ref[at, :] = dot(weights.astype(jnp.bfloat16), v_ref[seen, :])


def window(queries, keys, values, tail):
    rows, width = queries.shape
    return pl.pallas_call(
        window_kernel,
        out_shape=pltpu.VMEM(queries.shape, jnp.float32),
        compiler_params=grant(24),
        in_specs=[HBM] * 3 + [VMEM],
        out_specs=VMEM,
        scratch_shapes=[pltpu.VMEM((rows, width), jnp.bfloat16)]
        + [pltpu.VMEM((rows + WINDOW, width), jnp.bfloat16)] * 2
        + [pltpu.SemaphoreType.DMA((2 + 3 * (rows // WINDOW),))],
        name="window",
    )(*far_core(queries, keys, values), *near_core(tail))


def apply_kernel(slot, q_ref, seen_ref, down_ref, up_ref, down_c_ref, up_c_ref, out_ref):
    rows, width = out_ref.shape
    own, rest = halves(width)
    here = pl.ds(pl.multiple_of((lax.axis_index("head").astype(jnp.int32) ^ slot) * rows, rows), rows)
    q = q_ref[here, :]
    mixed = []
    for ref in (up_ref, up_c_ref):
        gate = dot(q, ref[0])
        up = dot(q, ref[1])
        mixed.append((gate * jax.nn.sigmoid(gate) * up).astype(jnp.bfloat16))
    mixed = jnp.concatenate(mixed, axis=1)
    for ref, at in ((down_ref, own), (down_c_ref, rest)):
        down = jnp.concatenate([ref[0, own, :], ref[0, rest, :]], axis=0)
        out_ref[:, at] = (dot(mixed, down) + seen_ref[here, at]).astype(jnp.bfloat16)


def apply_fast(slot, queries, seen, weights, rows):
    return pl.pallas_call(
        functools.partial(apply_kernel, slot),
        out_shape=pltpu.VMEM((rows, queries.shape[1]), jnp.bfloat16),
        compiler_params=grant(16),
        in_specs=[VMEM] * 6,
        out_specs=VMEM,
        name="apply",
    )(*near_core(queries, seen, *weights))


def own_project_kernel(x_ref, gain_ref, w_ref, out_ref, squares_ref):
    wide = x_ref[...].astype(jnp.float32)
    squares_ref[...] = jnp.sum(wide * wide, axis=1, keepdims=True)
    gain = gain_ref[...].reshape(1, wide.shape[1]).astype(jnp.float32)
    x = (wide * gain).astype(jnp.bfloat16)
    out_ref[...] = dot(x, w_ref[...])


def own_project(x, gain, weight):
    return pl.pallas_call(
        own_project_kernel,
        out_shape=(
            pltpu.VMEM((x.shape[0], weight.shape[1]), jnp.float32),
            pltpu.VMEM((x.shape[0], 1), jnp.float32),
        ),
        compiler_params=grant(16),
        in_specs=[VMEM] * 3,
        out_specs=(VMEM, VMEM),
        name="own_project",
    )(*near_core(x, gain, weight))


def project_kernel(holder, scale_by, x_ref, base_ref, squares_ref, *refs):
    count = (len(refs) - (3 if scale_by else 2)) // 2
    brought, copied = refs[:count], refs[count : 2 * count]
    out_ref, *rest = refs[2 * count :]
    core, half = place()
    wide = x_ref[...].astype(jnp.float32)
    squares = squares_ref[...] + jnp.sum(wide * wide, axis=1, keepdims=True)
    rows = wide.shape[1] // 2
    mine = pl.ds(pl.multiple_of(half * rows, rows), rows)
    theirs = pl.ds(pl.multiple_of((1 - half) * rows, rows), rows)
    x = jnp.concatenate([x_ref[:, mine], x_ref[:, theirs]], axis=1)
    scale = lax.rsqrt(squares * scale_by + EPSILON) if scale_by else None
    block = brought[0].shape[1] // 4
    stores = []
    for j in range(4):
        at = slice(j * block, (j + 1) * block)
        w = [jnp.where(core == holder, a[:, at], b[:, at]) for a, b in zip(brought, copied)]
        total = base_ref[:, at] + dot(x, jnp.concatenate(w, axis=0))
        if scale_by:
            ready_ref, sem = rest
            ready_ref[j] = (total * scale).astype(jnp.bfloat16)
            store = pltpu.make_async_copy(ready_ref.at[j], out_ref.at[:, pl.ds(j * block, block)], sem.at[j])
            store.start()
            stores.append(store)
        else:
            out_ref[:, at] = total
    if not scale_by:
        rest[0][...] = squares
    for store in stores:
        store.wait()


def project(holder, scale_by, x, base, squares, pieces):
    rows, columns = base.shape
    if scale_by:
        shape = jax.ShapeDtypeStruct((rows, columns), jnp.bfloat16)
        scratch = [pltpu.VMEM((4, rows, columns // 4), jnp.bfloat16), pltpu.SemaphoreType.DMA((4,))]
    else:
        shape = (pltpu.VMEM((rows, columns), jnp.float32), pltpu.VMEM((rows, 1), jnp.float32))
        scratch = []
    return pl.pallas_call(
        functools.partial(project_kernel, holder, scale_by),
        out_shape=shape,
        in_specs=[VMEM] * (3 + len(pieces)),
        out_specs=HBM if scale_by else (VMEM, VMEM),
        scratch_shapes=scratch,
        compiler_params=grant(16),
        name="project",
    )(*near_core(x, base, squares, *pieces))


def step(queries, keys, values, rates, fast_w1, fast_w2, fast_w3, norm_gain, out_weight):
    tok_rows, width = queries.shape
    ctx_count = lax.axis_size("ctx")
    heads = lax.axis_size("head")
    bits = ctx_count.bit_length() - 1
    assert ctx_count == 1 << bits and bits >= 3 and heads == 4

    tail, *chunks = load(keys, values, norm_gain, out_weight)
    tail = lax.ppermute(tail, "ctx", [(i, i + 1) for i in range(ctx_count - 1)])

    over = [(i, i ^ (2 if i // heads & 1 else 1)) for i in range(ctx_count * heads)]
    again = [(i, i ^ 1) for i in range(ctx_count * heads) if i // heads & 1]
    cross = [(i, i ^ (2 if i & 1 else 4)) for i in range(ctx_count)]
    early, relay, far, late = [], [], [], []
    for j, chunk in enumerate(chunks):
        early.append(lax.ppermute(chunk, ("ctx", "head"), over))
        relay.append(lax.ppermute(early[j], ("ctx", "head"), again))
        far.append(lax.ppermute(early[j], "ctx", cross))
        late.append(lax.ppermute(relay[j], "ctx", [(i, i ^ (2 << j)) for i in range(1, ctx_count, 2)]))

    def shared(arrays):
        copies = []
        for array in arrays:
            copies.append(swap(array, "ctx", 1))
        return copies

    early_c, relay_c = shared(early), shared(relay)
    far_c, late_c = shared(far), shared(late)
    pieces = {
        1: (0, early + far + early_c + far_c),
        2: (1, early + far + early_c + far_c),
        3: (1, relay + late + relay_c + late_c),
    }

    give_a, act, scaled, g1, g3 = pushes(keys, values, rates, fast_w1, fast_w2, fast_w3)
    give_b = contract(False, act, scaled)
    keep_a = contract(True, keys, g1, g3)
    keep_b = contract(True, act, scaled)

    masks = [1 << b for b in range(1, bits)]
    crossing = [
        [(i, i ^ (backward if i & 1 else forward)) for i in range(ctx_count)]
        for forward, backward in zip(masks, masks[::-1])
    ]
    weights = []
    for give, keep, olds in ((give_a, keep_a, (fast_w1, fast_w3)), (give_b, keep_b, (fast_w2,))):
        got = swap(give, "ctx", 1)
        for pairs in crossing:
            keep, send = add(keep, got)
            got = lax.ppermute(send, "ctx", pairs)
        mine = renorm(keep, got, *olds)
        other = swap(mine, "ctx", 1)
        weights.append((mine, other))
    weights = (weights[1][0], weights[0][0], weights[1][1], weights[0][1])

    seen = window(queries, keys, values, tail)

    rows = tok_rows // heads
    blocks = {}
    for k in send_order(heads) + [0]:
        combined = apply_fast(k, queries, seen, weights, rows)
        blocks[k] = swap(combined, "head", k) if k else combined
    base, squares = own_project(blocks[0], norm_gain, out_weight)
    for k in (1, 3, 2):
        scale_by = 1.0 / (heads * width) if k == 2 else None
        holder, brought = pieces[k]
        result = project(holder, scale_by, blocks[k], base, squares, brought)
        if scale_by is None:
            base, squares = result
    return result


def send_order(heads):
    return [heads - 1] + list(range(1, heads - 1))


def solution(mesh):
    placed = (
        P("ctx", "head"),
        P("ctx", "head"),
        P("ctx", "head"),
        P("ctx", "head"),
        P("head", None, None),
        P("head", None, None),
        P("head", None, None),
        P("head"),
        P("head", None),
    )
    return jax.shard_map(step, mesh=mesh, in_specs=placed, out_specs=P(("ctx", "head"), None), check_vma=False)
```

```python
import functools
import math

import jax
import jax.numpy as jnp
from jax import lax
from jax.experimental import pallas as pl
from jax.experimental.pallas import tpu as pltpu
from jax.sharding import PartitionSpec as P


WINDOW = 256
EPSILON = 1e-06

VMEM = pl.BlockSpec(memory_space=pltpu.VMEM)
HBM = pl.BlockSpec(memory_space=pltpu.HBM)


def near_core(*arrays):
    return [pltpu.with_memory_space_constraint(a, pltpu.VMEM) for a in arrays]


def far_core(*arrays):
    return [pltpu.with_memory_space_constraint(a, pltpu.HBM) for a in arrays]


def grant(mib):
    return pltpu.CompilerParams(vmem_limit_bytes=mib << 20)


def swap(value, axis, mask):
    return lax.ppermute(value, axis, [(i, i ^ mask) for i in range(lax.axis_size(axis))])


def dot(left, right, left_dim=1, right_dim=0):
    return lax.dot_general(
        left, right, (((left_dim,), (right_dim,)), ((), ())), preferred_element_type=jnp.float32
    )


def place():
    me = lax.axis_index("ctx").astype(jnp.int32)
    return me & 1, ((me >> 1) ^ (me >> 2)) & 1


def column(row, width):
    tall = jnp.transpose(jnp.broadcast_to(row, (128, row.shape[1])))
    return jnp.concatenate([tall] * (width // 128), axis=1)


def load_kernel(chunk, k_hbm, v_hbm, gain_hbm, w_hbm, *refs):
    *tail_ref, piece_ref, w_ref, gain_ref, sem = refs
    rows, columns = piece_ref.shape
    _, side = place()
    first = pl.multiple_of((2 * side + chunk) * rows, rows)
    moves = [(gain_hbm, gain_ref), (w_hbm.at[pl.ds(first, rows), :], w_ref)]
    if tail_ref:
        last = pl.ds(k_hbm.shape[0] - WINDOW, WINDOW)
        moves += [
            (src.at[last, :], tail_ref[0].at[pl.ds(j * WINDOW, WINDOW), :])
            for j, src in enumerate((k_hbm, v_hbm))
        ]
    copies = [pltpu.make_async_copy(src, dst, sem.at[j]) for j, (src, dst) in enumerate(moves)]
    for copy in copies:
        copy.start()
    copies[0].wait()
    gain = gain_ref[...].reshape(1, gain_ref.shape[0]).astype(jnp.float32)
    low, high = (gain[:, (2 * j + chunk) * rows : (2 * j + chunk + 1) * rows] for j in range(2))
    gain = jnp.transpose(jnp.broadcast_to(jnp.where(side == 0, low, high), (128, rows)))
    copies[1].wait()
    for left in range(0, columns, 128):
        here = slice(left, left + 128)
        piece_ref[:, here] = (w_ref[:, here].astype(jnp.float32) * gain).astype(jnp.bfloat16)
    for copy in copies[2:]:
        copy.wait()


def load(chunk, keys, values, gain, weight):
    piece = pltpu.VMEM((weight.shape[0] // 4, weight.shape[1]), jnp.bfloat16)
    shapes = [pltpu.VMEM((2 * WINDOW, keys.shape[1]), jnp.bfloat16)] if chunk == 0 else []
    return pl.pallas_call(
        functools.partial(load_kernel, chunk),
        out_shape=shapes + [piece],
        compiler_params=grant(8),
        in_specs=[HBM] * 4,
        out_specs=[VMEM] * (len(shapes) + 1),
        scratch_shapes=[piece, pltpu.VMEM(gain.shape, gain.dtype), pltpu.SemaphoreType.DMA((4,))],
        name="load",
    )(*far_core(keys, values, gain, weight))


def halves(width):
    core, _ = place()
    half = width // 2
    mine = pl.ds(pl.multiple_of(core * half, half), half)
    theirs = pl.ds(pl.multiple_of((1 - core) * half, half), half)
    return mine, theirs


def push_kernel(k_ref, v_ref, r_ref, w1_ref, w2_ref, w3_ref, give_ref, act_ref, sc_ref, g1_ref, g3_ref):
    rows, width = k_ref.shape
    steps = 4
    block = rows // steps
    for i in range(steps):
        at = slice(i * block, (i + 1) * block)
        k = k_ref[at, :]
        gate = dot(k, w1_ref[0])
        up = dot(k, w3_ref[0])
        rate = column(r_ref[:, at], width)
        scaled = (v_ref[at, :].astype(jnp.float32) * rate).astype(jnp.bfloat16)
        back = dot(scaled, w2_ref[0], 1, 1)
        s = jax.nn.sigmoid(gate)
        gs = gate * s
        act_ref[at, :] = (gs * up).astype(jnp.bfloat16)
        sc_ref[at, :] = scaled
        g1_ref[at, :] = (back * up * (s + gs * (1.0 - s))).astype(jnp.bfloat16)
        g3_ref[at, :] = (back * gs).astype(jnp.bfloat16)
    _, theirs = halves(width)
    for j, ref in enumerate((g1_ref, g3_ref)):
        give_ref[j] = dot(k_ref[...], ref[:, theirs], 0, 0).astype(jnp.bfloat16)


def pushes(keys, values, rates, w1, w2, w3):
    rows, width = keys.shape
    wide = pltpu.VMEM((rows, width), jnp.bfloat16)
    return pl.pallas_call(
        push_kernel,
        out_shape=[pltpu.VMEM((2, width, width // 2), jnp.bfloat16)] + [wide] * 4,
        compiler_params=grant(16),
        in_specs=[VMEM] * 6,
        out_specs=[VMEM] * 5,
        name="pushes",
    )(*near_core(keys, values, rates.reshape(1, rows), w1, w2, w3))


def contract_kernel(kept, left_ref, *refs):
    *rights, out_ref = refs
    mine, theirs = halves(left_ref.shape[1])
    for j, ref in enumerate(rights):
        out_ref[j] = dot(left_ref[...], ref[:, mine if kept else theirs], 0, 0).astype(out_ref.dtype)


def contract(kept, left, *rights):
    width = left.shape[1]
    dtype = jnp.float32 if kept else jnp.bfloat16
    return pl.pallas_call(
        functools.partial(contract_kernel, kept),
        out_shape=pltpu.VMEM((len(rights), width, width // 2), dtype),
        compiler_params=grant(12),
        in_specs=[VMEM] * (1 + len(rights)),
        out_specs=VMEM,
        name="contract",
    )(*near_core(left, *rights))


def add_kernel(keep_ref, got_ref, sum_ref, send_ref):
    total = keep_ref[...] + got_ref[...].astype(jnp.float32)
    sum_ref[...] = total
    send_ref[...] = total.astype(jnp.bfloat16)


def add(keep, got):
    return pl.pallas_call(
        add_kernel,
        out_shape=(pltpu.VMEM(keep.shape, jnp.float32), pltpu.VMEM(keep.shape, jnp.bfloat16)),
        compiler_params=grant(8),
        in_specs=[VMEM] * 2,
        out_specs=(VMEM,) * 2,
        name="add",
    )(*near_core(keep, got))


def renorm_kernel(keep_ref, got_ref, *refs):
    *weights, out_ref = refs
    half = keep_ref.shape[2]
    block = half // 2
    core, _ = place()
    for j, w_ref in enumerate(weights):
        for first in (0, block):
            at = slice(first, first + block)
            start = pl.multiple_of(core * half + first, block)
            old = w_ref[0, :, pl.ds(start, block)].astype(jnp.float32)
            new = old + (keep_ref[j, :, at] + got_ref[j, :, at].astype(jnp.float32))
            old_norm = jnp.sqrt(jnp.mean(old * old, axis=0, keepdims=True) + EPSILON)
            new_norm = jnp.sqrt(jnp.mean(new * new, axis=0, keepdims=True) + EPSILON)
            out_ref[j, :, at] = (new * (old_norm / new_norm)).astype(jnp.bfloat16)


def renorm(keep, got, *weights):
    return pl.pallas_call(
        renorm_kernel,
        out_shape=pltpu.VMEM(keep.shape, jnp.bfloat16),
        compiler_params=grant(8),
        in_specs=[VMEM] * (2 + len(weights)),
        out_specs=VMEM,
        name="renorm",
    )(*near_core(keep, got, *weights))


def window_kernel(q_hbm, k_hbm, v_hbm, tail_ref, out_ref, q_ref, k_ref, v_ref, sem):
    rows, width = q_ref.shape
    scale = 1.0 / math.sqrt(width)
    query = lax.broadcasted_iota(jnp.int32, (WINDOW, 2 * WINDOW), 0)
    key = lax.broadcasted_iota(jnp.int32, (WINDOW, 2 * WINDOW), 1)
    allowed = (key > query) & (key <= query + WINDOW)
    allowed_first = allowed & ((key >= WINDOW) | (lax.axis_index("ctx") > 0))
    count = rows // WINDOW
    loads = [[
        pltpu.make_async_copy(tail_ref.at[pl.ds(j * WINDOW, WINDOW), :], dst.at[pl.ds(0, WINDOW), :], sem.at[j])
        for j, dst in enumerate((k_ref, v_ref))
    ]]
    for i in range(count):
        at, after = pl.ds(i * WINDOW, WINDOW), pl.ds((i + 1) * WINDOW, WINDOW)
        loads.append([
            pltpu.make_async_copy(q_hbm.at[at, :], q_ref.at[at, :], sem.at[3 * i + 2]),
            pltpu.make_async_copy(k_hbm.at[at, :], k_ref.at[after, :], sem.at[3 * i + 3]),
            pltpu.make_async_copy(v_hbm.at[at, :], v_ref.at[after, :], sem.at[3 * i + 4]),
        ])
    for group in loads:
        for load in group:
            load.start()
    for load in loads[0]:
        load.wait()
    for i in range(count):
        for load in loads[i + 1]:
            load.wait()
        at = slice(i * WINDOW, (i + 1) * WINDOW)
        seen = slice(i * WINDOW, (i + 2) * WINDOW)
        scores = dot(q_ref[at, :], k_ref[seen, :], 1, 1) * scale
        scores = jnp.where(allowed_first if i == 0 else allowed, scores, -jnp.inf)
        peak = jnp.max(scores, axis=1, keepdims=True)
        exponent = jnp.exp(scores - peak)
        weights = exponent / jnp.sum(exponent, axis=1, keepdims=True)
        out_ref[at, :] = dot(weights.astype(jnp.bfloat16), v_ref[seen, :])


def window(queries, keys, values, tail):
    rows, width = queries.shape
    return pl.pallas_call(
        window_kernel,
        out_shape=pltpu.VMEM(queries.shape, jnp.float32),
        compiler_params=grant(24),
        in_specs=[HBM] * 3 + [VMEM],
        out_specs=VMEM,
        scratch_shapes=[pltpu.VMEM((rows, width), jnp.bfloat16)]
        + [pltpu.VMEM((rows + WINDOW, width), jnp.bfloat16)] * 2
        + [pltpu.SemaphoreType.DMA((2 + 3 * (rows // WINDOW),))],
        name="window",
    )(*far_core(queries, keys, values), *near_core(tail))


def mix_kernel(slot, q_ref, up_ref, up_c_ref, out_ref):
    rows, width = out_ref.shape
    here = pl.ds(pl.multiple_of((lax.axis_index("head").astype(jnp.int32) ^ slot) * rows, rows), rows)
    q = q_ref[here, :]
    half = width // 2
    for j, ref in enumerate((up_ref, up_c_ref)):
        gate = dot(q, ref[0])
        up = dot(q, ref[1])
        out_ref[:, j * half : (j + 1) * half] = (gate * jax.nn.sigmoid(gate) * up).astype(jnp.bfloat16)


def mix(slot, queries, up, up_c, rows):
    return pl.pallas_call(
        functools.partial(mix_kernel, slot),
        out_shape=pltpu.VMEM((rows, queries.shape[1]), jnp.bfloat16),
        compiler_params=grant(8),
        in_specs=[VMEM] * 3,
        out_specs=VMEM,
        name="mix",
    )(*near_core(queries, up, up_c))


def down_kernel(slot, mixed_ref, seen_ref, down_ref, down_c_ref, out_ref):
    rows, width = out_ref.shape
    own, rest = halves(width)
    here = pl.ds(pl.multiple_of((lax.axis_index("head").astype(jnp.int32) ^ slot) * rows, rows), rows)
    for ref, at in ((down_ref, own), (down_c_ref, rest)):
        down = jnp.concatenate([ref[0, own, :], ref[0, rest, :]], axis=0)
        out_ref[:, at] = (dot(mixed_ref[...], down) + seen_ref[here, at]).astype(jnp.bfloat16)


def combine(slot, mixed, seen, down, down_c):
    return pl.pallas_call(
        functools.partial(down_kernel, slot),
        out_shape=pltpu.VMEM(mixed.shape, jnp.bfloat16),
        compiler_params=grant(8),
        in_specs=[VMEM] * 4,
        out_specs=VMEM,
        name="combine",
    )(*near_core(mixed, seen, down, down_c))


def own_project_kernel(x_ref, gain_ref, w_ref, out_ref, squares_ref):
    wide = x_ref[...].astype(jnp.float32)
    squares_ref[...] = jnp.sum(wide * wide, axis=1, keepdims=True)
    gain = gain_ref[...].reshape(1, wide.shape[1]).astype(jnp.float32)
    x = (wide * gain).astype(jnp.bfloat16)
    out_ref[...] = dot(x, w_ref[...])


def own_project(x, gain, weight):
    return pl.pallas_call(
        own_project_kernel,
        out_shape=(
            pltpu.VMEM((x.shape[0], weight.shape[1]), jnp.float32),
            pltpu.VMEM((x.shape[0], 1), jnp.float32),
        ),
        compiler_params=grant(16),
        in_specs=[VMEM] * 3,
        out_specs=(VMEM, VMEM),
        name="own_project",
    )(*near_core(x, gain, weight))


def project_kernel(holder, scale_by, x_ref, base_ref, squares_ref, *refs):
    count = (len(refs) - (3 if scale_by else 2)) // 2
    brought, copied = refs[:count], refs[count : 2 * count]
    out_ref, *rest = refs[2 * count :]
    core, half = place()
    wide = x_ref[...].astype(jnp.float32)
    squares = squares_ref[...] + jnp.sum(wide * wide, axis=1, keepdims=True)
    rows = wide.shape[1] // 2
    mine = pl.ds(pl.multiple_of(half * rows, rows), rows)
    theirs = pl.ds(pl.multiple_of((1 - half) * rows, rows), rows)
    x = jnp.concatenate([x_ref[:, mine], x_ref[:, theirs]], axis=1)
    scale = lax.rsqrt(squares * scale_by + EPSILON) if scale_by else None
    block = brought[0].shape[1] // 4
    stores = []
    for j in range(4):
        at = slice(j * block, (j + 1) * block)
        w = [jnp.where(core == holder, a[:, at], b[:, at]) for a, b in zip(brought, copied)]
        total = base_ref[:, at] + dot(x, jnp.concatenate(w, axis=0))
        if scale_by:
            ready_ref, sem = rest
            ready_ref[j] = (total * scale).astype(jnp.bfloat16)
            store = pltpu.make_async_copy(ready_ref.at[j], out_ref.at[:, pl.ds(j * block, block)], sem.at[j])
            store.start()
            stores.append(store)
        else:
            out_ref[:, at] = total
    if not scale_by:
        rest[0][...] = squares
    for store in stores:
        store.wait()


def project(holder, scale_by, x, base, squares, pieces):
    rows, columns = base.shape
    if scale_by:
        shape = jax.ShapeDtypeStruct((rows, columns), jnp.bfloat16)
        scratch = [pltpu.VMEM((4, rows, columns // 4), jnp.bfloat16), pltpu.SemaphoreType.DMA((4,))]
    else:
        shape = (pltpu.VMEM((rows, columns), jnp.float32), pltpu.VMEM((rows, 1), jnp.float32))
        scratch = []
    return pl.pallas_call(
        functools.partial(project_kernel, holder, scale_by),
        out_shape=shape,
        in_specs=[VMEM] * (3 + len(pieces)),
        out_specs=HBM if scale_by else (VMEM, VMEM),
        scratch_shapes=scratch,
        compiler_params=grant(16),
        name="project",
    )(*near_core(x, base, squares, *pieces))


def step(queries, keys, values, rates, fast_w1, fast_w2, fast_w3, norm_gain, out_weight):
    tok_rows, width = queries.shape
    ctx_count = lax.axis_size("ctx")
    heads = lax.axis_size("head")
    bits = ctx_count.bit_length() - 1
    assert ctx_count == 1 << bits and bits >= 3 and heads == 4

    tail, chunk = load(0, keys, values, norm_gain, out_weight)
    chunks = [chunk, *load(1, keys, values, norm_gain, out_weight)]
    tail = lax.ppermute(tail, "ctx", [(i, i + 1) for i in range(ctx_count - 1)])

    over = [(i, i ^ (2 if i // heads & 1 else 1)) for i in range(ctx_count * heads)]
    again = [(i, i ^ 1) for i in range(ctx_count * heads) if i // heads & 1]
    cross = [(i, i ^ (2 if i & 1 else 4)) for i in range(ctx_count)]
    early, relay, far, late = [], [], [], []
    for j, chunk in enumerate(chunks):
        early.append(lax.ppermute(chunk, ("ctx", "head"), over))
        relay.append(lax.ppermute(early[j], ("ctx", "head"), again))
        far.append(lax.ppermute(early[j], "ctx", cross))
        late.append(lax.ppermute(relay[j], "ctx", [(i, i ^ (2 << j)) for i in range(1, ctx_count, 2)]))

    def shared(arrays):
        copies = []
        for array in arrays:
            copies.append(swap(array, "ctx", 1))
        return copies

    early_c, relay_c = shared(early), shared(relay)
    far_c, late_c = shared(far), shared(late)
    pieces = {
        1: (0, early + far + early_c + far_c),
        2: (1, early + far + early_c + far_c),
        3: (1, relay + late + relay_c + late_c),
    }

    give_a, act, scaled, g1, g3 = pushes(keys, values, rates, fast_w1, fast_w2, fast_w3)
    give_b = contract(False, act, scaled)
    keep_a = contract(True, keys, g1, g3)
    keep_b = contract(True, act, scaled)

    masks = [1 << b for b in range(1, bits)]
    crossing = [
        [(i, i ^ (backward if i & 1 else forward)) for i in range(ctx_count)]
        for forward, backward in zip(masks, masks[::-1])
    ]
    weights = []
    for give, keep, olds in ((give_a, keep_a, (fast_w1, fast_w3)), (give_b, keep_b, (fast_w2,))):
        got = swap(give, "ctx", 1)
        for pairs in crossing:
            keep, send = add(keep, got)
            got = lax.ppermute(send, "ctx", pairs)
        mine = renorm(keep, got, *olds)
        other = swap(mine, "ctx", 1)
        weights.append((mine, other))
    weights = (weights[1][0], weights[0][0], weights[1][1], weights[0][1])

    seen = window(queries, keys, values, tail)

    rows = tok_rows // heads
    blocks = {}
    for k in send_order(heads) + [0]:
        mixed = mix(k, queries, weights[1], weights[3], rows)
        combined = combine(k, mixed, seen, weights[0], weights[2])
        blocks[k] = swap(combined, "head", k) if k else combined
    base, squares = own_project(blocks[0], norm_gain, out_weight)
    for k in (1, 3, 2):
        scale_by = 1.0 / (heads * width) if k == 2 else None
        holder, brought = pieces[k]
        result = project(holder, scale_by, blocks[k], base, squares, brought)
        if scale_by is None:
            base, squares = result
    return result


def send_order(heads):
    return [heads - 1] + list(range(1, heads - 1))


def solution(mesh):
    placed = (
        P("ctx", "head"),
        P("ctx", "head"),
        P("ctx", "head"),
        P("ctx", "head"),
        P("head", None, None),
        P("head", None, None),
        P("head", None, None),
        P("head"),
        P("head", None),
    )
    return jax.shard_map(step, mesh=mesh, in_specs=placed, out_specs=P(("ctx", "head"), None), check_vma=False)
```

```python
import functools
import math

import jax
import jax.numpy as jnp
from jax import lax
from jax.experimental import pallas as pl
from jax.experimental.pallas import tpu as pltpu
from jax.sharding import PartitionSpec as P


WINDOW = 256
EPSILON = 1e-06

VMEM = pl.BlockSpec(memory_space=pltpu.VMEM)
HBM = pl.BlockSpec(memory_space=pltpu.HBM)


def near_core(*arrays):
    return [pltpu.with_memory_space_constraint(a, pltpu.VMEM) for a in arrays]


def far_core(*arrays):
    return [pltpu.with_memory_space_constraint(a, pltpu.HBM) for a in arrays]


def grant(mib):
    return pltpu.CompilerParams(vmem_limit_bytes=mib << 20)


def swap(value, axis, mask):
    return lax.ppermute(value, axis, [(i, i ^ mask) for i in range(lax.axis_size(axis))])


def dot(left, right, left_dim=1, right_dim=0):
    return lax.dot_general(
        left, right, (((left_dim,), (right_dim,)), ((), ())), preferred_element_type=jnp.float32
    )


def place():
    me = lax.axis_index("ctx").astype(jnp.int32)
    return me & 1, ((me >> 1) ^ (me >> 2)) & 1


def column(row, width):
    tall = jnp.transpose(jnp.broadcast_to(row, (128, row.shape[1])))
    return jnp.concatenate([tall] * (width // 128), axis=1)


def load_kernel(k_hbm, v_hbm, gain_hbm, w_hbm, tail_ref, low_ref, high_ref, w_ref, gain_ref, sem):
    rows, columns = w_ref.shape
    _, side = place()
    first = pl.multiple_of(side * rows, rows)
    last = pl.ds(k_hbm.shape[0] - WINDOW, WINDOW)
    steps = 4
    block = rows // steps
    moves = [(gain_hbm, gain_ref)]
    for i in range(steps):
        at = pl.ds(i * block, block)
        moves.append((w_hbm.at[pl.ds(first + i * block, block), :], w_ref.at[at, :]))
    moves += [(k_hbm.at[last, :], tail_ref.at[pl.ds(0, WINDOW), :])]
    moves += [(v_hbm.at[last, :], tail_ref.at[pl.ds(WINDOW, WINDOW), :])]
    copies = [pltpu.make_async_copy(src, dst, sem.at[j]) for j, (src, dst) in enumerate(moves)]
    for copy in copies:
        copy.start()
    copies[0].wait()
    gain = gain_ref[...].reshape(1, 2 * rows).astype(jnp.float32)
    gain = jnp.transpose(jnp.broadcast_to(jnp.where(side == 0, gain[:, :rows], gain[:, rows:]), (128, rows)))
    for i in range(steps):
        at = slice(i * block, (i + 1) * block)
        copies[1 + i].wait()
        to_ref, to = (low_ref, at) if i < steps // 2 else (high_ref, slice((i - 2) * block, (i - 1) * block))
        for left in range(0, columns, 128):
            here = slice(left, left + 128)
            to_ref[to, here] = (w_ref[at, here].astype(jnp.float32) * gain[at, :]).astype(jnp.bfloat16)
    for copy in copies[1 + steps :]:
        copy.wait()


def load(keys, values, gain, weight):
    piece = pltpu.VMEM((weight.shape[0] // 2, weight.shape[1]), jnp.bfloat16)
    chunk = pltpu.VMEM((weight.shape[0] // 4, weight.shape[1]), jnp.bfloat16)
    return pl.pallas_call(
        load_kernel,
        out_shape=[pltpu.VMEM((2 * WINDOW, keys.shape[1]), jnp.bfloat16), chunk, chunk],
        compiler_params=grant(8),
        in_specs=[HBM] * 4,
        out_specs=[VMEM] * 3,
        scratch_shapes=[piece, pltpu.VMEM(gain.shape, gain.dtype), pltpu.SemaphoreType.DMA((7,))],
        name="load",
    )(*far_core(keys, values, gain, weight))


def halves(width):
    core, _ = place()
    half = width // 2
    mine = pl.ds(pl.multiple_of(core * half, half), half)
    theirs = pl.ds(pl.multiple_of((1 - core) * half, half), half)
    return mine, theirs


def push_kernel(k_ref, v_ref, r_ref, w1_ref, w2_ref, w3_ref, give_ref, act_ref, sc_ref, g1_ref, g3_ref):
    rows, width = k_ref.shape
    steps = 4
    block = rows // steps
    for i in range(steps):
        at = slice(i * block, (i + 1) * block)
        k = k_ref[at, :]
        gate = dot(k, w1_ref[0])
        up = dot(k, w3_ref[0])
        rate = column(r_ref[:, at], width)
        scaled = (v_ref[at, :].astype(jnp.float32) * rate).astype(jnp.bfloat16)
        back = dot(scaled, w2_ref[0], 1, 1)
        s = jax.nn.sigmoid(gate)
        gs = gate * s
        act_ref[at, :] = (gs * up).astype(jnp.bfloat16)
        sc_ref[at, :] = scaled
        g1_ref[at, :] = (back * up * (s + gs * (1.0 - s))).astype(jnp.bfloat16)
        g3_ref[at, :] = (back * gs).astype(jnp.bfloat16)
    _, theirs = halves(width)
    for j, ref in enumerate((g1_ref, g3_ref)):
        give_ref[j] = dot(k_ref[...], ref[:, theirs], 0, 0).astype(jnp.bfloat16)


def pushes(keys, values, rates, w1, w2, w3):
    rows, width = keys.shape
    wide = pltpu.VMEM((rows, width), jnp.bfloat16)
    return pl.pallas_call(
        push_kernel,
        out_shape=[pltpu.VMEM((2, width, width // 2), jnp.bfloat16)] + [wide] * 4,
        compiler_params=grant(16),
        in_specs=[VMEM] * 6,
        out_specs=[VMEM] * 5,
        name="pushes",
    )(*near_core(keys, values, rates.reshape(1, rows), w1, w2, w3))


def contract_kernel(kept, left_ref, *refs):
    *rights, out_ref = refs
    mine, theirs = halves(left_ref.shape[1])
    for j, ref in enumerate(rights):
        out_ref[j] = dot(left_ref[...], ref[:, mine if kept else theirs], 0, 0).astype(out_ref.dtype)


def contract(kept, left, *rights):
    width = left.shape[1]
    dtype = jnp.float32 if kept else jnp.bfloat16
    return pl.pallas_call(
        functools.partial(contract_kernel, kept),
        out_shape=pltpu.VMEM((len(rights), width, width // 2), dtype),
        compiler_params=grant(12),
        in_specs=[VMEM] * (1 + len(rights)),
        out_specs=VMEM,
        name="contract",
    )(*near_core(left, *rights))


def add_kernel(keep_ref, got_ref, sum_ref, send_ref):
    total = keep_ref[...] + got_ref[...].astype(jnp.float32)
    sum_ref[...] = total
    send_ref[...] = total.astype(jnp.bfloat16)


def add(keep, got):
    return pl.pallas_call(
        add_kernel,
        out_shape=(pltpu.VMEM(keep.shape, jnp.float32), pltpu.VMEM(keep.shape, jnp.bfloat16)),
        compiler_params=grant(8),
        in_specs=[VMEM] * 2,
        out_specs=(VMEM,) * 2,
        name="add",
    )(*near_core(keep, got))


def renorm_kernel(keep_ref, got_ref, *refs):
    *weights, out_ref = refs
    half = keep_ref.shape[2]
    block = half // 2
    core, _ = place()
    for j, w_ref in enumerate(weights):
        for first in (0, block):
            at = slice(first, first + block)
            start = pl.multiple_of(core * half + first, block)
            old = w_ref[0, :, pl.ds(start, block)].astype(jnp.float32)
            new = old + (keep_ref[j, :, at] + got_ref[j, :, at].astype(jnp.float32))
            old_norm = jnp.sqrt(jnp.mean(old * old, axis=0, keepdims=True) + EPSILON)
            new_norm = jnp.sqrt(jnp.mean(new * new, axis=0, keepdims=True) + EPSILON)
            out_ref[j, :, at] = (new * (old_norm / new_norm)).astype(jnp.bfloat16)


def renorm(keep, got, *weights):
    return pl.pallas_call(
        renorm_kernel,
        out_shape=pltpu.VMEM(keep.shape, jnp.bfloat16),
        compiler_params=grant(8),
        in_specs=[VMEM] * (2 + len(weights)),
        out_specs=VMEM,
        name="renorm",
    )(*near_core(keep, got, *weights))


def window_kernel(q_hbm, k_hbm, v_hbm, tail_ref, out_ref, q_ref, k_ref, v_ref, sem):
    rows, width = q_ref.shape
    scale = 1.0 / math.sqrt(width)
    query = lax.broadcasted_iota(jnp.int32, (WINDOW, 2 * WINDOW), 0)
    key = lax.broadcasted_iota(jnp.int32, (WINDOW, 2 * WINDOW), 1)
    allowed = (key > query) & (key <= query + WINDOW)
    allowed_first = allowed & ((key >= WINDOW) | (lax.axis_index("ctx") > 0))
    count = rows // WINDOW
    loads = [[
        pltpu.make_async_copy(tail_ref.at[pl.ds(j * WINDOW, WINDOW), :], dst.at[pl.ds(0, WINDOW), :], sem.at[j])
        for j, dst in enumerate((k_ref, v_ref))
    ]]
    for i in range(count):
        at, after = pl.ds(i * WINDOW, WINDOW), pl.ds((i + 1) * WINDOW, WINDOW)
        loads.append([
            pltpu.make_async_copy(q_hbm.at[at, :], q_ref.at[at, :], sem.at[3 * i + 2]),
            pltpu.make_async_copy(k_hbm.at[at, :], k_ref.at[after, :], sem.at[3 * i + 3]),
            pltpu.make_async_copy(v_hbm.at[at, :], v_ref.at[after, :], sem.at[3 * i + 4]),
        ])
    for group in loads:
        for load in group:
            load.start()
    for load in loads[0]:
        load.wait()
    for i in range(count):
        for load in loads[i + 1]:
            load.wait()
        at = slice(i * WINDOW, (i + 1) * WINDOW)
        seen = slice(i * WINDOW, (i + 2) * WINDOW)
        scores = dot(q_ref[at, :], k_ref[seen, :], 1, 1) * scale
        scores = jnp.where(allowed_first if i == 0 else allowed, scores, -jnp.inf)
        peak = jnp.max(scores, axis=1, keepdims=True)
        exponent = jnp.exp(scores - peak)
        weights = exponent / jnp.sum(exponent, axis=1, keepdims=True)
        out_ref[at, :] = dot(weights.astype(jnp.bfloat16), v_ref[seen, :])


def window(queries, keys, values, tail):
    rows, width = queries.shape
    return pl.pallas_call(
        window_kernel,
        out_shape=pltpu.VMEM(queries.shape, jnp.float32),
        compiler_params=grant(24),
        in_specs=[HBM] * 3 + [VMEM],
        out_specs=VMEM,
        scratch_shapes=[pltpu.VMEM((rows, width), jnp.bfloat16)]
        + [pltpu.VMEM((rows + WINDOW, width), jnp.bfloat16)] * 2
        + [pltpu.SemaphoreType.DMA((2 + 3 * (rows // WINDOW),))],
        name="window",
    )(*far_core(queries, keys, values), *near_core(tail))


def mix_kernel(slot, q_ref, up_ref, up_c_ref, out_ref):
    rows, width = out_ref.shape
    here = pl.ds(pl.multiple_of((lax.axis_index("head").astype(jnp.int32) ^ slot) * rows, rows), rows)
    q = q_ref[here, :]
    half = width // 2
    for j, ref in enumerate((up_ref, up_c_ref)):
        gate = dot(q, ref[0])
        up = dot(q, ref[1])
        out_ref[:, j * half : (j + 1) * half] = (gate * jax.nn.sigmoid(gate) * up).astype(jnp.bfloat16)


def mix(slot, queries, up, up_c, rows):
    return pl.pallas_call(
        functools.partial(mix_kernel, slot),
        out_shape=pltpu.VMEM((rows, queries.shape[1]), jnp.bfloat16),
        compiler_params=grant(8),
        in_specs=[VMEM] * 3,
        out_specs=VMEM,
        name="mix",
    )(*near_core(queries, up, up_c))


def down_kernel(slot, mixed_ref, seen_ref, down_ref, down_c_ref, out_ref):
    rows, width = out_ref.shape
    own, rest = halves(width)
    here = pl.ds(pl.multiple_of((lax.axis_index("head").astype(jnp.int32) ^ slot) * rows, rows), rows)
    for ref, at in ((down_ref, own), (down_c_ref, rest)):
        down = jnp.concatenate([ref[0, own, :], ref[0, rest, :]], axis=0)
        out_ref[:, at] = (dot(mixed_ref[...], down) + seen_ref[here, at]).astype(jnp.bfloat16)


def combine(slot, mixed, seen, down, down_c):
    return pl.pallas_call(
        functools.partial(down_kernel, slot),
        out_shape=pltpu.VMEM(mixed.shape, jnp.bfloat16),
        compiler_params=grant(8),
        in_specs=[VMEM] * 4,
        out_specs=VMEM,
        name="combine",
    )(*near_core(mixed, seen, down, down_c))


def own_project_kernel(x_ref, gain_ref, w_ref, out_ref, squares_ref):
    wide = x_ref[...].astype(jnp.float32)
    squares_ref[...] = jnp.sum(wide * wide, axis=1, keepdims=True)
    gain = gain_ref[...].reshape(1, wide.shape[1]).astype(jnp.float32)
    x = (wide * gain).astype(jnp.bfloat16)
    out_ref[...] = dot(x, w_ref[...])


def own_project(x, gain, weight):
    return pl.pallas_call(
        own_project_kernel,
        out_shape=(
            pltpu.VMEM((x.shape[0], weight.shape[1]), jnp.float32),
            pltpu.VMEM((x.shape[0], 1), jnp.float32),
        ),
        compiler_params=grant(16),
        in_specs=[VMEM] * 3,
        out_specs=(VMEM, VMEM),
        name="own_project",
    )(*near_core(x, gain, weight))


def project_kernel(holder, scale_by, x_ref, base_ref, squares_ref, *refs):
    count = (len(refs) - (3 if scale_by else 2)) // 2
    brought, copied = refs[:count], refs[count : 2 * count]
    out_ref, *rest = refs[2 * count :]
    core, half = place()
    wide = x_ref[...].astype(jnp.float32)
    squares = squares_ref[...] + jnp.sum(wide * wide, axis=1, keepdims=True)
    rows = wide.shape[1] // 2
    mine = pl.ds(pl.multiple_of(half * rows, rows), rows)
    theirs = pl.ds(pl.multiple_of((1 - half) * rows, rows), rows)
    x = jnp.concatenate([x_ref[:, mine], x_ref[:, theirs]], axis=1)
    scale = lax.rsqrt(squares * scale_by + EPSILON) if scale_by else None
    block = brought[0].shape[1] // 4
    stores = []
    for j in range(4):
        at = slice(j * block, (j + 1) * block)
        w = [jnp.where(core == holder, a[:, at], b[:, at]) for a, b in zip(brought, copied)]
        total = base_ref[:, at] + dot(x, jnp.concatenate(w, axis=0))
        if scale_by:
            ready_ref, sem = rest
            ready_ref[j] = (total * scale).astype(jnp.bfloat16)
            store = pltpu.make_async_copy(ready_ref.at[j], out_ref.at[:, pl.ds(j * block, block)], sem.at[j])
            store.start()
            stores.append(store)
        else:
            out_ref[:, at] = total
    if not scale_by:
        rest[0][...] = squares
    for store in stores:
        store.wait()


def project(holder, scale_by, x, base, squares, pieces):
    rows, columns = base.shape
    if scale_by:
        shape = jax.ShapeDtypeStruct((rows, columns), jnp.bfloat16)
        scratch = [pltpu.VMEM((4, rows, columns // 4), jnp.bfloat16), pltpu.SemaphoreType.DMA((4,))]
    else:
        shape = (pltpu.VMEM((rows, columns), jnp.float32), pltpu.VMEM((rows, 1), jnp.float32))
        scratch = []
    return pl.pallas_call(
        functools.partial(project_kernel, holder, scale_by),
        out_shape=shape,
        in_specs=[VMEM] * (3 + len(pieces)),
        out_specs=HBM if scale_by else (VMEM, VMEM),
        scratch_shapes=scratch,
        compiler_params=grant(16),
        name="project",
    )(*near_core(x, base, squares, *pieces))


def step(queries, keys, values, rates, fast_w1, fast_w2, fast_w3, norm_gain, out_weight):
    tok_rows, width = queries.shape
    ctx_count = lax.axis_size("ctx")
    heads = lax.axis_size("head")
    bits = ctx_count.bit_length() - 1
    assert ctx_count == 1 << bits and bits >= 3 and heads == 4

    tail, *chunks = load(keys, values, norm_gain, out_weight)
    tail = lax.ppermute(tail, "ctx", [(i, i + 1) for i in range(ctx_count - 1)])

    over = [(i, i ^ (2 if i // heads & 1 else 1)) for i in range(ctx_count * heads)]
    again = [(i, i ^ 1) for i in range(ctx_count * heads) if i // heads & 1]
    cross = [(i, i ^ (2 if i & 1 else 4)) for i in range(ctx_count)]
    early, relay, far, late = [], [], [], []
    for j, chunk in enumerate(chunks):
        early.append(lax.ppermute(chunk, ("ctx", "head"), over))
        relay.append(lax.ppermute(early[j], ("ctx", "head"), again))
        far.append(lax.ppermute(early[j], "ctx", cross))
        late.append(lax.ppermute(relay[j], "ctx", [(i, i ^ (2 << j)) for i in range(1, ctx_count, 2)]))

    def shared(arrays):
        copies = []
        for array in arrays:
            copies.append(swap(array, "ctx", 1))
        return copies

    early_c, relay_c = shared(early), shared(relay)
    far_c, late_c = shared(far), shared(late)
    pieces = {
        1: (0, early + far + early_c + far_c),
        2: (1, early + far + early_c + far_c),
        3: (1, relay + late + relay_c + late_c),
    }

    give_a, act, scaled, g1, g3 = pushes(keys, values, rates, fast_w1, fast_w2, fast_w3)
    give_b = contract(False, act, scaled)
    keep_a = contract(True, keys, g1, g3)
    keep_b = contract(True, act, scaled)

    masks = [1 << b for b in range(1, bits)]
    crossing = [
        [(i, i ^ (backward if i & 1 else forward)) for i in range(ctx_count)]
        for forward, backward in zip(masks, masks[::-1])
    ]
    weights = []
    for give, keep, olds in ((give_a, keep_a, (fast_w1, fast_w3)), (give_b, keep_b, (fast_w2,))):
        got = swap(give, "ctx", 1)
        for pairs in crossing:
            keep, send = add(keep, got)
            got = lax.ppermute(send, "ctx", pairs)
        mine = renorm(keep, got, *olds)
        other = swap(mine, "ctx", 1)
        weights.append((mine, other))
    weights = (weights[1][0], weights[0][0], weights[1][1], weights[0][1])

    seen = window(queries, keys, values, tail)

    rows = tok_rows // heads
    blocks = {}
    for k in send_order(heads) + [0]:
        mixed = mix(k, queries, weights[1], weights[3], rows)
        combined = combine(k, mixed, seen, weights[0], weights[2])
        blocks[k] = swap(combined, "head", k) if k else combined
    base, squares = own_project(blocks[0], norm_gain, out_weight)
    for k in (1, 3, 2):
        scale_by = 1.0 / (heads * width) if k == 2 else None
        holder, brought = pieces[k]
        result = project(holder, scale_by, blocks[k], base, squares, brought)
        if scale_by is None:
            base, squares = result
    return result


def send_order(heads):
    return [heads - 1] + list(range(1, heads - 1))


def solution(mesh):
    placed = (
        P("ctx", "head"),
        P("ctx", "head"),
        P("ctx", "head"),
        P("ctx", "head"),
        P("head", None, None),
        P("head", None, None),
        P("head", None, None),
        P("head"),
        P("head", None),
    )
    return jax.shard_map(step, mesh=mesh, in_specs=placed, out_specs=P(("ctx", "head"), None), check_vma=False)
```

```python
import functools
import math

import jax
import jax.numpy as jnp
from jax import lax
from jax.experimental import pallas as pl
from jax.experimental.pallas import tpu as pltpu
from jax.sharding import PartitionSpec as P


WINDOW = 256
EPSILON = 1e-06

VMEM = pl.BlockSpec(memory_space=pltpu.VMEM)
HBM = pl.BlockSpec(memory_space=pltpu.HBM)


def near_core(*arrays):
    return [pltpu.with_memory_space_constraint(a, pltpu.VMEM) for a in arrays]


def far_core(*arrays):
    return [pltpu.with_memory_space_constraint(a, pltpu.HBM) for a in arrays]


def grant(mib):
    return pltpu.CompilerParams(vmem_limit_bytes=mib << 20)


def swap(value, axis, mask):
    return lax.ppermute(value, axis, [(i, i ^ mask) for i in range(lax.axis_size(axis))])


def dot(left, right, left_dim=1, right_dim=0):
    return lax.dot_general(
        left, right, (((left_dim,), (right_dim,)), ((), ())), preferred_element_type=jnp.float32
    )


def place():
    me = lax.axis_index("ctx").astype(jnp.int32)
    return me & 1, ((me >> 1) ^ (me >> 2)) & 1


def column(row, width):
    tall = jnp.transpose(jnp.broadcast_to(row, (128, row.shape[1])))
    return jnp.concatenate([tall] * (width // 128), axis=1)


def load_kernel(k_hbm, v_hbm, gain_hbm, w_hbm, tail_ref, low_ref, high_ref, w_ref, gain_ref, sem):
    rows, columns = w_ref.shape
    _, side = place()
    first = pl.multiple_of(side * rows, rows)
    last = pl.ds(k_hbm.shape[0] - WINDOW, WINDOW)
    steps = 4
    block = rows // steps
    moves = [(gain_hbm, gain_ref)]
    for i in range(steps):
        at = pl.ds(i * block, block)
        moves.append((w_hbm.at[pl.ds(first + i * block, block), :], w_ref.at[at, :]))
    moves += [(k_hbm.at[last, :], tail_ref.at[pl.ds(0, WINDOW), :])]
    moves += [(v_hbm.at[last, :], tail_ref.at[pl.ds(WINDOW, WINDOW), :])]
    copies = [pltpu.make_async_copy(src, dst, sem.at[j]) for j, (src, dst) in enumerate(moves)]
    for copy in copies:
        copy.start()
    copies[0].wait()
    gain = gain_ref[...].reshape(1, 2 * rows).astype(jnp.float32)
    gain = jnp.transpose(jnp.broadcast_to(jnp.where(side == 0, gain[:, :rows], gain[:, rows:]), (128, rows)))
    for i in range(steps):
        at = slice(i * block, (i + 1) * block)
        copies[1 + i].wait()
        to_ref, to = (low_ref, at) if i < steps // 2 else (high_ref, slice((i - 2) * block, (i - 1) * block))
        for left in range(0, columns, 128):
            here = slice(left, left + 128)
            to_ref[to, here] = (w_ref[at, here].astype(jnp.float32) * gain[at, :]).astype(jnp.bfloat16)
    for copy in copies[1 + steps :]:
        copy.wait()


def load(keys, values, gain, weight):
    piece = pltpu.VMEM((weight.shape[0] // 2, weight.shape[1]), jnp.bfloat16)
    chunk = pltpu.VMEM((weight.shape[0] // 4, weight.shape[1]), jnp.bfloat16)
    return pl.pallas_call(
        load_kernel,
        out_shape=[pltpu.VMEM((2 * WINDOW, keys.shape[1]), jnp.bfloat16), chunk, chunk],
        compiler_params=grant(8),
        in_specs=[HBM] * 4,
        out_specs=[VMEM] * 3,
        scratch_shapes=[piece, pltpu.VMEM(gain.shape, gain.dtype), pltpu.SemaphoreType.DMA((7,))],
        name="load",
    )(*far_core(keys, values, gain, weight))


def halves(width):
    core, _ = place()
    half = width // 2
    mine = pl.ds(pl.multiple_of(core * half, half), half)
    theirs = pl.ds(pl.multiple_of((1 - core) * half, half), half)
    return mine, theirs


def push_kernel(k_ref, v_ref, r_ref, w1_ref, w2_ref, w3_ref, give_ref, act_ref, sc_ref, g1_ref, g3_ref):
    rows, width = k_ref.shape
    steps = 4
    block = rows // steps
    for i in range(steps):
        at = slice(i * block, (i + 1) * block)
        k = k_ref[at, :]
        gate = dot(k, w1_ref[0])
        up = dot(k, w3_ref[0])
        rate = column(r_ref[:, at], width)
        scaled = (v_ref[at, :].astype(jnp.float32) * rate).astype(jnp.bfloat16)
        back = dot(scaled, w2_ref[0], 1, 1)
        s = jax.nn.sigmoid(gate)
        gs = gate * s
        act_ref[at, :] = (gs * up).astype(jnp.bfloat16)
        sc_ref[at, :] = scaled
        g1_ref[at, :] = (back * up * (s + gs * (1.0 - s))).astype(jnp.bfloat16)
        g3_ref[at, :] = (back * gs).astype(jnp.bfloat16)
    _, theirs = halves(width)
    for j, ref in enumerate((g1_ref, g3_ref)):
        give_ref[j] = dot(k_ref[...], ref[:, theirs], 0, 0).astype(jnp.bfloat16)


def pushes(keys, values, rates, w1, w2, w3):
    rows, width = keys.shape
    wide = pltpu.VMEM((rows, width), jnp.bfloat16)
    return pl.pallas_call(
        push_kernel,
        out_shape=[pltpu.VMEM((2, width, width // 2), jnp.bfloat16)] + [wide] * 4,
        compiler_params=grant(16),
        in_specs=[VMEM] * 6,
        out_specs=[VMEM] * 5,
        name="pushes",
    )(*near_core(keys, values, rates.reshape(1, rows), w1, w2, w3))


def contract_kernel(kept, left_ref, *refs):
    *rights, out_ref = refs
    mine, theirs = halves(left_ref.shape[1])
    for j, ref in enumerate(rights):
        out_ref[j] = dot(left_ref[...], ref[:, mine if kept else theirs], 0, 0).astype(out_ref.dtype)


def contract(kept, left, *rights):
    width = left.shape[1]
    dtype = jnp.float32 if kept else jnp.bfloat16
    return pl.pallas_call(
        functools.partial(contract_kernel, kept),
        out_shape=pltpu.VMEM((len(rights), width, width // 2), dtype),
        compiler_params=grant(12),
        in_specs=[VMEM] * (1 + len(rights)),
        out_specs=VMEM,
        name="contract",
    )(*near_core(left, *rights))


def add_kernel(keep_ref, got_ref, sum_ref, send_ref):
    total = keep_ref[...] + got_ref[...].astype(jnp.float32)
    sum_ref[...] = total
    send_ref[...] = total.astype(jnp.bfloat16)


def add(keep, got):
    return pl.pallas_call(
        add_kernel,
        out_shape=(pltpu.VMEM(keep.shape, jnp.float32), pltpu.VMEM(keep.shape, jnp.bfloat16)),
        compiler_params=grant(8),
        in_specs=[VMEM] * 2,
        out_specs=(VMEM,) * 2,
        name="add",
    )(*near_core(keep, got))


def renorm_kernel(keep_ref, got_ref, *refs):
    *weights, out_ref = refs
    half = keep_ref.shape[2]
    block = half // 2
    core, _ = place()
    for j, w_ref in enumerate(weights):
        for first in (0, block):
            at = slice(first, first + block)
            start = pl.multiple_of(core * half + first, block)
            old = w_ref[0, :, pl.ds(start, block)].astype(jnp.float32)
            new = old + (keep_ref[j, :, at] + got_ref[j, :, at].astype(jnp.float32))
            old_norm = jnp.sqrt(jnp.mean(old * old, axis=0, keepdims=True) + EPSILON)
            new_norm = jnp.sqrt(jnp.mean(new * new, axis=0, keepdims=True) + EPSILON)
            out_ref[j, :, at] = (new * (old_norm / new_norm)).astype(jnp.bfloat16)


def renorm(keep, got, *weights):
    return pl.pallas_call(
        renorm_kernel,
        out_shape=pltpu.VMEM(keep.shape, jnp.bfloat16),
        compiler_params=grant(8),
        in_specs=[VMEM] * (2 + len(weights)),
        out_specs=VMEM,
        name="renorm",
    )(*near_core(keep, got, *weights))


def window_kernel(q_hbm, k_hbm, v_hbm, tail_ref, out_ref, q_ref, k_ref, v_ref, sem):
    rows, width = q_ref.shape
    scale = 1.0 / math.sqrt(width)
    query = lax.broadcasted_iota(jnp.int32, (WINDOW, 2 * WINDOW), 0)
    key = lax.broadcasted_iota(jnp.int32, (WINDOW, 2 * WINDOW), 1)
    allowed = (key > query) & (key <= query + WINDOW)
    allowed_first = allowed & ((key >= WINDOW) | (lax.axis_index("ctx") > 0))
    count = rows // WINDOW
    loads = [[
        pltpu.make_async_copy(tail_ref.at[pl.ds(j * WINDOW, WINDOW), :], dst.at[pl.ds(0, WINDOW), :], sem.at[j])
        for j, dst in enumerate((k_ref, v_ref))
    ]]
    for i in range(count):
        at, after = pl.ds(i * WINDOW, WINDOW), pl.ds((i + 1) * WINDOW, WINDOW)
        loads.append([
            pltpu.make_async_copy(q_hbm.at[at, :], q_ref.at[at, :], sem.at[3 * i + 2]),
            pltpu.make_async_copy(k_hbm.at[at, :], k_ref.at[after, :], sem.at[3 * i + 3]),
            pltpu.make_async_copy(v_hbm.at[at, :], v_ref.at[after, :], sem.at[3 * i + 4]),
        ])
    for group in loads:
        for load in group:
            load.start()
    for load in loads[0]:
        load.wait()
    for i in range(count):
        for load in loads[i + 1]:
            load.wait()
        at = slice(i * WINDOW, (i + 1) * WINDOW)
        seen = slice(i * WINDOW, (i + 2) * WINDOW)
        scores = dot(q_ref[at, :], k_ref[seen, :], 1, 1) * scale
        scores = jnp.where(allowed_first if i == 0 else allowed, scores, -jnp.inf)
        peak = jnp.max(scores, axis=1, keepdims=True)
        exponent = jnp.exp(scores - peak)
        weights = exponent / jnp.sum(exponent, axis=1, keepdims=True)
        out_ref[at, :] = dot(weights.astype(jnp.bfloat16), v_ref[seen, :])


def window(queries, keys, values, tail):
    rows, width = queries.shape
    return pl.pallas_call(
        window_kernel,
        out_shape=pltpu.VMEM(queries.shape, jnp.float32),
        compiler_params=grant(24),
        in_specs=[HBM] * 3 + [VMEM],
        out_specs=VMEM,
        scratch_shapes=[pltpu.VMEM((rows, width), jnp.bfloat16)]
        + [pltpu.VMEM((rows + WINDOW, width), jnp.bfloat16)] * 2
        + [pltpu.SemaphoreType.DMA((2 + 3 * (rows // WINDOW),))],
        name="window",
    )(*far_core(queries, keys, values), *near_core(tail))


def mix_kernel(slot, q_ref, up_ref, up_c_ref, out_ref):
    rows, width = out_ref.shape
    here = pl.ds(pl.multiple_of((lax.axis_index("head").astype(jnp.int32) ^ slot) * rows, rows), rows)
    q = q_ref[here, :]
    half = width // 2
    for j, ref in enumerate((up_ref, up_c_ref)):
        gate = dot(q, ref[0])
        up = dot(q, ref[1])
        out_ref[:, j * half : (j + 1) * half] = (gate * jax.nn.sigmoid(gate) * up).astype(jnp.bfloat16)


def mix(slot, queries, up, up_c, rows):
    return pl.pallas_call(
        functools.partial(mix_kernel, slot),
        out_shape=pltpu.VMEM((rows, queries.shape[1]), jnp.bfloat16),
        compiler_params=grant(8),
        in_specs=[VMEM] * 3,
        out_specs=VMEM,
        name="mix",
    )(*near_core(queries, up, up_c))


def down_kernel(slot, mixed_ref, seen_ref, down_ref, down_c_ref, out_ref):
    rows, width = out_ref.shape
    own, rest = halves(width)
    here = pl.ds(pl.multiple_of((lax.axis_index("head").astype(jnp.int32) ^ slot) * rows, rows), rows)
    for ref, at in ((down_ref, own), (down_c_ref, rest)):
        down = jnp.concatenate([ref[0, own, :], ref[0, rest, :]], axis=0)
        out_ref[:, at] = (dot(mixed_ref[...], down) + seen_ref[here, at]).astype(jnp.bfloat16)


def combine(slot, mixed, seen, down, down_c):
    return pl.pallas_call(
        functools.partial(down_kernel, slot),
        out_shape=pltpu.VMEM(mixed.shape, jnp.bfloat16),
        compiler_params=grant(8),
        in_specs=[VMEM] * 4,
        out_specs=VMEM,
        name="combine",
    )(*near_core(mixed, seen, down, down_c))


def own_project_kernel(x_ref, gain_ref, w_ref, out_ref, squares_ref):
    wide = x_ref[...].astype(jnp.float32)
    squares_ref[...] = jnp.sum(wide * wide, axis=1, keepdims=True)
    gain = gain_ref[...].reshape(1, wide.shape[1]).astype(jnp.float32)
    x = (wide * gain).astype(jnp.bfloat16)
    out_ref[...] = dot(x, w_ref[...])


def own_project(x, gain, weight):
    return pl.pallas_call(
        own_project_kernel,
        out_shape=(
            pltpu.VMEM((x.shape[0], weight.shape[1]), jnp.float32),
            pltpu.VMEM((x.shape[0], 1), jnp.float32),
        ),
        compiler_params=grant(16),
        in_specs=[VMEM] * 3,
        out_specs=(VMEM, VMEM),
        name="own_project",
    )(*near_core(x, gain, weight))


def project_kernel(holder, scale_by, x_ref, base_ref, squares_ref, *refs):
    count = (len(refs) - (3 if scale_by else 2)) // 2
    brought, copied = refs[:count], refs[count : 2 * count]
    out_ref, *rest = refs[2 * count :]
    core, half = place()
    wide = x_ref[...].astype(jnp.float32)
    squares = squares_ref[...] + jnp.sum(wide * wide, axis=1, keepdims=True)
    rows = wide.shape[1] // 2
    mine = pl.ds(pl.multiple_of(half * rows, rows), rows)
    theirs = pl.ds(pl.multiple_of((1 - half) * rows, rows), rows)
    x = jnp.concatenate([x_ref[:, mine], x_ref[:, theirs]], axis=1)
    scale = lax.rsqrt(squares * scale_by + EPSILON) if scale_by else None
    block = brought[0].shape[1] // 4
    stores = []
    for j in range(4):
        at = slice(j * block, (j + 1) * block)
        w = [jnp.where(core == holder, a[:, at], b[:, at]) for a, b in zip(brought, copied)]
        total = base_ref[:, at] + dot(x, jnp.concatenate(w, axis=0))
        if scale_by:
            ready_ref, sem = rest
            ready_ref[j] = (total * scale).astype(jnp.bfloat16)
            store = pltpu.make_async_copy(ready_ref.at[j], out_ref.at[:, pl.ds(j * block, block)], sem.at[j])
            store.start()
            stores.append(store)
        else:
            out_ref[:, at] = total
    if not scale_by:
        rest[0][...] = squares
    for store in stores:
        store.wait()


def project(holder, scale_by, x, base, squares, pieces):
    rows, columns = base.shape
    if scale_by:
        shape = jax.ShapeDtypeStruct((rows, columns), jnp.bfloat16)
        scratch = [pltpu.VMEM((4, rows, columns // 4), jnp.bfloat16), pltpu.SemaphoreType.DMA((4,))]
    else:
        shape = (pltpu.VMEM((rows, columns), jnp.float32), pltpu.VMEM((rows, 1), jnp.float32))
        scratch = []
    return pl.pallas_call(
        functools.partial(project_kernel, holder, scale_by),
        out_shape=shape,
        in_specs=[VMEM] * (3 + len(pieces)),
        out_specs=HBM if scale_by else (VMEM, VMEM),
        scratch_shapes=scratch,
        compiler_params=grant(16),
        name="project",
    )(*near_core(x, base, squares, *pieces))


def step(queries, keys, values, rates, fast_w1, fast_w2, fast_w3, norm_gain, out_weight):
    tok_rows, width = queries.shape
    ctx_count = lax.axis_size("ctx")
    heads = lax.axis_size("head")
    bits = ctx_count.bit_length() - 1
    assert ctx_count == 1 << bits and bits >= 3 and heads == 4

    tail, *chunks = load(keys, values, norm_gain, out_weight)
    tail = lax.ppermute(tail, "ctx", [(i, i + 1) for i in range(ctx_count - 1)])

    over = [(i, i ^ (2 if i // heads & 1 else 1)) for i in range(ctx_count * heads)]
    again = [(i, i ^ 1) for i in range(ctx_count * heads) if i // heads & 1]
    cross = [(i, i ^ (2 if i & 1 else 4)) for i in range(ctx_count)]
    early, relay, far, late = [], [], [], []
    for j, chunk in enumerate(chunks):
        early.append(lax.ppermute(chunk, ("ctx", "head"), over))
        relay.append(lax.ppermute(early[j], ("ctx", "head"), again))
        far.append(lax.ppermute(early[j], "ctx", cross))
        late.append(lax.ppermute(relay[j], "ctx", [(i, i ^ (2 << j)) for i in range(1, ctx_count, 2)]))

    def shared(arrays):
        copies = []
        for array in arrays:
            copies.append(swap(array, "ctx", 1))
        return copies

    early_c, relay_c = shared(early), shared(relay)
    far_c, late_c = shared(far), shared(late)
    pieces = {
        1: (0, early + far + early_c + far_c),
        2: (1, early + far + early_c + far_c),
        3: (1, relay + late + relay_c + late_c),
    }

    give_a, act, scaled, g1, g3 = pushes(keys, values, rates, fast_w1, fast_w2, fast_w3)
    give_b = contract(False, act, scaled)
    keep_a = contract(True, keys, g1, g3)
    keep_b = contract(True, act, scaled)

    masks = [1 << b for b in range(1, bits)]
    crossing = [
        [(i, i ^ (backward if i & 1 else forward)) for i in range(ctx_count)]
        for forward, backward in zip(masks, masks[::-1])
    ]
    weights = []
    for give, keep, olds in ((give_a, keep_a, (fast_w1, fast_w3)), (give_b, keep_b, (fast_w2,))):
        got = swap(give, "ctx", 1)
        for pairs in crossing:
            keep, send = add(keep, got)
            got = lax.ppermute(send, "ctx", pairs)
        mine = renorm(keep, got, *olds)
        other = swap(mine, "ctx", 1)
        weights.append((mine, other))
    weights = (weights[1][0], weights[0][0], weights[1][1], weights[0][1])

    seen = window(queries, keys, values, tail)

    rows = tok_rows // heads
    blocks = {}
    for k in send_order(heads) + [0]:
        mixed = mix(k, queries, weights[1], weights[3], rows)
        combined = combine(k, mixed, seen, weights[0], weights[2])
        blocks[k] = swap(combined, "head", k) if k else combined
    base, squares = own_project(blocks[0], norm_gain, out_weight)
    for k in (3, 2, 1):
        scale_by = 1.0 / (heads * width) if k == 1 else None
        holder, brought = pieces[k]
        result = project(holder, scale_by, blocks[k], base, squares, brought)
        if scale_by is None:
            base, squares = result
    return result


def send_order(heads):
    return list(range(heads - 1, 0, -1))


def solution(mesh):
    placed = (
        P("ctx", "head"),
        P("ctx", "head"),
        P("ctx", "head"),
        P("ctx", "head"),
        P("head", None, None),
        P("head", None, None),
        P("head", None, None),
        P("head"),
        P("head", None),
    )
    return jax.shard_map(step, mesh=mesh, in_specs=placed, out_specs=P(("ctx", "head"), None), check_vma=False)
```

```python
import functools
import math

import jax
import jax.numpy as jnp
from jax import lax
from jax.experimental import pallas as pl
from jax.experimental.pallas import tpu as pltpu
from jax.sharding import PartitionSpec as P


WINDOW = 256
EPSILON = 1e-06

VMEM = pl.BlockSpec(memory_space=pltpu.VMEM)
HBM = pl.BlockSpec(memory_space=pltpu.HBM)


def near_core(*arrays):
    return [pltpu.with_memory_space_constraint(a, pltpu.VMEM) for a in arrays]


def far_core(*arrays):
    return [pltpu.with_memory_space_constraint(a, pltpu.HBM) for a in arrays]


def grant(mib):
    return pltpu.CompilerParams(vmem_limit_bytes=mib << 20)


def swap(value, axis, mask):
    return lax.ppermute(value, axis, [(i, i ^ mask) for i in range(lax.axis_size(axis))])


def dot(left, right, left_dim=1, right_dim=0):
    return lax.dot_general(
        left, right, (((left_dim,), (right_dim,)), ((), ())), preferred_element_type=jnp.float32
    )


def place():
    me = lax.axis_index("ctx").astype(jnp.int32)
    return me & 1, ((me >> 1) ^ (me >> 2)) & 1


def column(row, width):
    tall = jnp.transpose(jnp.broadcast_to(row, (128, row.shape[1])))
    return jnp.concatenate([tall] * (width // 128), axis=1)


def load_kernel(k_hbm, v_hbm, gain_hbm, w_hbm, tail_ref, low_ref, high_ref, w_ref, gain_ref, sem):
    rows, columns = w_ref.shape
    _, side = place()
    first = pl.multiple_of(side * rows, rows)
    last = pl.ds(k_hbm.shape[0] - WINDOW, WINDOW)
    steps = 4
    block = rows // steps
    moves = [(gain_hbm, gain_ref)]
    for i in range(steps):
        at = pl.ds(i * block, block)
        moves.append((w_hbm.at[pl.ds(first + i * block, block), :], w_ref.at[at, :]))
    moves += [(k_hbm.at[last, :], tail_ref.at[pl.ds(0, WINDOW), :])]
    moves += [(v_hbm.at[last, :], tail_ref.at[pl.ds(WINDOW, WINDOW), :])]
    copies = [pltpu.make_async_copy(src, dst, sem.at[j]) for j, (src, dst) in enumerate(moves)]
    for copy in copies:
        copy.start()
    copies[0].wait()
    gain = gain_ref[...].reshape(1, 2 * rows).astype(jnp.float32)
    gain = jnp.transpose(jnp.broadcast_to(jnp.where(side == 0, gain[:, :rows], gain[:, rows:]), (128, rows)))
    for i in range(steps):
        at = slice(i * block, (i + 1) * block)
        copies[1 + i].wait()
        to_ref, to = (low_ref, at) if i < steps // 2 else (high_ref, slice((i - 2) * block, (i - 1) * block))
        for left in range(0, columns, 128):
            here = slice(left, left + 128)
            to_ref[to, here] = (w_ref[at, here].astype(jnp.float32) * gain[at, :]).astype(jnp.bfloat16)
    for copy in copies[1 + steps :]:
        copy.wait()


def load(keys, values, gain, weight):
    piece = pltpu.VMEM((weight.shape[0] // 2, weight.shape[1]), jnp.bfloat16)
    chunk = pltpu.VMEM((weight.shape[0] // 4, weight.shape[1]), jnp.bfloat16)
    return pl.pallas_call(
        load_kernel,
        out_shape=[pltpu.VMEM((2 * WINDOW, keys.shape[1]), jnp.bfloat16), chunk, chunk],
        compiler_params=grant(8),
        in_specs=[HBM] * 4,
        out_specs=[VMEM] * 3,
        scratch_shapes=[piece, pltpu.VMEM(gain.shape, gain.dtype), pltpu.SemaphoreType.DMA((7,))],
        name="load",
    )(*far_core(keys, values, gain, weight))


def halves(width):
    core, _ = place()
    half = width // 2
    mine = pl.ds(pl.multiple_of(core * half, half), half)
    theirs = pl.ds(pl.multiple_of((1 - core) * half, half), half)
    return mine, theirs


def push_kernel(k_ref, v_ref, r_ref, w1_ref, w2_ref, w3_ref, give_ref, act_ref, sc_ref, g1_ref, g3_ref):
    rows, width = k_ref.shape
    steps = 4
    block = rows // steps
    for i in range(steps):
        at = slice(i * block, (i + 1) * block)
        k = k_ref[at, :]
        gate = dot(k, w1_ref[0])
        up = dot(k, w3_ref[0])
        rate = column(r_ref[:, at], width)
        scaled = (v_ref[at, :].astype(jnp.float32) * rate).astype(jnp.bfloat16)
        back = dot(scaled, w2_ref[0], 1, 1)
        s = jax.nn.sigmoid(gate)
        gs = gate * s
        act_ref[at, :] = (gs * up).astype(jnp.bfloat16)
        sc_ref[at, :] = scaled
        g1_ref[at, :] = (back * up * (s + gs * (1.0 - s))).astype(jnp.bfloat16)
        g3_ref[at, :] = (back * gs).astype(jnp.bfloat16)
    _, theirs = halves(width)
    for j, ref in enumerate((g1_ref, g3_ref)):
        give_ref[j] = dot(k_ref[...], ref[:, theirs], 0, 0).astype(jnp.bfloat16)


def pushes(keys, values, rates, w1, w2, w3):
    rows, width = keys.shape
    wide = pltpu.VMEM((rows, width), jnp.bfloat16)
    return pl.pallas_call(
        push_kernel,
        out_shape=[pltpu.VMEM((2, width, width // 2), jnp.bfloat16)] + [wide] * 4,
        compiler_params=grant(16),
        in_specs=[VMEM] * 6,
        out_specs=[VMEM] * 5,
        name="pushes",
    )(*near_core(keys, values, rates.reshape(1, rows), w1, w2, w3))


def contract_kernel(kept, left_ref, *refs):
    *rights, out_ref = refs
    mine, theirs = halves(left_ref.shape[1])
    for j, ref in enumerate(rights):
        out_ref[j] = dot(left_ref[...], ref[:, mine if kept else theirs], 0, 0).astype(out_ref.dtype)


def contract(kept, left, *rights):
    width = left.shape[1]
    dtype = jnp.float32 if kept else jnp.bfloat16
    return pl.pallas_call(
        functools.partial(contract_kernel, kept),
        out_shape=pltpu.VMEM((len(rights), width, width // 2), dtype),
        compiler_params=grant(12),
        in_specs=[VMEM] * (1 + len(rights)),
        out_specs=VMEM,
        name="contract",
    )(*near_core(left, *rights))


def add_kernel(keep_ref, got_ref, sum_ref, send_ref):
    total = keep_ref[...] + got_ref[...].astype(jnp.float32)
    sum_ref[...] = total
    send_ref[...] = total.astype(jnp.bfloat16)


def add(keep, got):
    return pl.pallas_call(
        add_kernel,
        out_shape=(pltpu.VMEM(keep.shape, jnp.float32), pltpu.VMEM(keep.shape, jnp.bfloat16)),
        compiler_params=grant(8),
        in_specs=[VMEM] * 2,
        out_specs=(VMEM,) * 2,
        name="add",
    )(*near_core(keep, got))


def renorm_kernel(keep_ref, got_ref, *refs):
    *weights, out_ref = refs
    half = keep_ref.shape[2]
    block = half // 2
    core, _ = place()
    for j, w_ref in enumerate(weights):
        for first in (0, block):
            at = slice(first, first + block)
            start = pl.multiple_of(core * half + first, block)
            old = w_ref[0, :, pl.ds(start, block)].astype(jnp.float32)
            new = old + (keep_ref[j, :, at] + got_ref[j, :, at].astype(jnp.float32))
            old_norm = jnp.sqrt(jnp.mean(old * old, axis=0, keepdims=True) + EPSILON)
            new_norm = jnp.sqrt(jnp.mean(new * new, axis=0, keepdims=True) + EPSILON)
            out_ref[j, :, at] = (new * (old_norm / new_norm)).astype(jnp.bfloat16)


def renorm(keep, got, *weights):
    return pl.pallas_call(
        renorm_kernel,
        out_shape=pltpu.VMEM(keep.shape, jnp.bfloat16),
        compiler_params=grant(8),
        in_specs=[VMEM] * (2 + len(weights)),
        out_specs=VMEM,
        name="renorm",
    )(*near_core(keep, got, *weights))


def window_kernel(q_hbm, k_hbm, v_hbm, tail_ref, out_ref, q_ref, k_ref, v_ref, sem):
    rows, width = q_ref.shape
    scale = 1.0 / math.sqrt(width)
    query = lax.broadcasted_iota(jnp.int32, (WINDOW, 2 * WINDOW), 0)
    key = lax.broadcasted_iota(jnp.int32, (WINDOW, 2 * WINDOW), 1)
    allowed = (key > query) & (key <= query + WINDOW)
    allowed_first = allowed & ((key >= WINDOW) | (lax.axis_index("ctx") > 0))
    count = rows // WINDOW
    loads = [[
        pltpu.make_async_copy(tail_ref.at[pl.ds(j * WINDOW, WINDOW), :], dst.at[pl.ds(0, WINDOW), :], sem.at[j])
        for j, dst in enumerate((k_ref, v_ref))
    ]]
    for i in range(count):
        at, after = pl.ds(i * WINDOW, WINDOW), pl.ds((i + 1) * WINDOW, WINDOW)
        loads.append([
            pltpu.make_async_copy(q_hbm.at[at, :], q_ref.at[at, :], sem.at[3 * i + 2]),
            pltpu.make_async_copy(k_hbm.at[at, :], k_ref.at[after, :], sem.at[3 * i + 3]),
            pltpu.make_async_copy(v_hbm.at[at, :], v_ref.at[after, :], sem.at[3 * i + 4]),
        ])
    for group in loads:
        for load in group:
            load.start()
    for load in loads[0]:
        load.wait()
    for i in range(count):
        for load in loads[i + 1]:
            load.wait()
        at = slice(i * WINDOW, (i + 1) * WINDOW)
        seen = slice(i * WINDOW, (i + 2) * WINDOW)
        scores = dot(q_ref[at, :], k_ref[seen, :], 1, 1) * scale
        scores = jnp.where(allowed_first if i == 0 else allowed, scores, -jnp.inf)
        peak = jnp.max(scores, axis=1, keepdims=True)
        exponent = jnp.exp(scores - peak)
        weights = exponent / jnp.sum(exponent, axis=1, keepdims=True)
        out_ref[at, :] = dot(weights.astype(jnp.bfloat16), v_ref[seen, :])


def window(queries, keys, values, tail):
    rows, width = queries.shape
    return pl.pallas_call(
        window_kernel,
        out_shape=pltpu.VMEM(queries.shape, jnp.float32),
        compiler_params=grant(24),
        in_specs=[HBM] * 3 + [VMEM],
        out_specs=VMEM,
        scratch_shapes=[pltpu.VMEM((rows, width), jnp.bfloat16)]
        + [pltpu.VMEM((rows + WINDOW, width), jnp.bfloat16)] * 2
        + [pltpu.SemaphoreType.DMA((2 + 3 * (rows // WINDOW),))],
        name="window",
    )(*far_core(queries, keys, values), *near_core(tail))


def mix_kernel(slot, q_ref, up_ref, up_c_ref, out_ref):
    rows, width = out_ref.shape
    here = pl.ds(pl.multiple_of((lax.axis_index("head").astype(jnp.int32) ^ slot) * rows, rows), rows)
    q = q_ref[here, :]
    half = width // 2
    for j, ref in enumerate((up_ref, up_c_ref)):
        gate = dot(q, ref[0])
        up = dot(q, ref[1])
        out_ref[:, j * half : (j + 1) * half] = (gate * jax.nn.sigmoid(gate) * up).astype(jnp.bfloat16)


def mix(slot, queries, up, up_c, rows):
    return pl.pallas_call(
        functools.partial(mix_kernel, slot),
        out_shape=pltpu.VMEM((rows, queries.shape[1]), jnp.bfloat16),
        compiler_params=grant(8),
        in_specs=[VMEM] * 3,
        out_specs=VMEM,
        name="mix",
    )(*near_core(queries, up, up_c))


def down_kernel(slot, mixed_ref, seen_ref, down_ref, down_c_ref, out_ref):
    rows, width = out_ref.shape
    own, rest = halves(width)
    here = pl.ds(pl.multiple_of((lax.axis_index("head").astype(jnp.int32) ^ slot) * rows, rows), rows)
    for ref, at in ((down_ref, own), (down_c_ref, rest)):
        down = jnp.concatenate([ref[0, own, :], ref[0, rest, :]], axis=0)
        out_ref[:, at] = (dot(mixed_ref[...], down) + seen_ref[here, at]).astype(jnp.bfloat16)


def combine(slot, mixed, seen, down, down_c):
    return pl.pallas_call(
        functools.partial(down_kernel, slot),
        out_shape=pltpu.VMEM(mixed.shape, jnp.bfloat16),
        compiler_params=grant(8),
        in_specs=[VMEM] * 4,
        out_specs=VMEM,
        name="combine",
    )(*near_core(mixed, seen, down, down_c))


def own_project_kernel(x_ref, gain_ref, w_ref, out_ref, squares_ref):
    wide = x_ref[...].astype(jnp.float32)
    squares_ref[...] = jnp.sum(wide * wide, axis=1, keepdims=True)
    gain = gain_ref[...].reshape(1, wide.shape[1]).astype(jnp.float32)
    x = (wide * gain).astype(jnp.bfloat16)
    out_ref[...] = dot(x, w_ref[...])


def own_project(x, gain, weight):
    return pl.pallas_call(
        own_project_kernel,
        out_shape=(
            pltpu.VMEM((x.shape[0], weight.shape[1]), jnp.float32),
            pltpu.VMEM((x.shape[0], 1), jnp.float32),
        ),
        compiler_params=grant(16),
        in_specs=[VMEM] * 3,
        out_specs=(VMEM, VMEM),
        name="own_project",
    )(*near_core(x, gain, weight))


def project_kernel(holder, scale_by, x_ref, base_ref, squares_ref, *refs):
    count = (len(refs) - (3 if scale_by else 2)) // 2
    brought, copied = refs[:count], refs[count : 2 * count]
    out_ref, *rest = refs[2 * count :]
    core, half = place()
    wide = x_ref[...].astype(jnp.float32)
    squares = squares_ref[...] + jnp.sum(wide * wide, axis=1, keepdims=True)
    rows = wide.shape[1] // 2
    mine = pl.ds(pl.multiple_of(half * rows, rows), rows)
    theirs = pl.ds(pl.multiple_of((1 - half) * rows, rows), rows)
    x = jnp.concatenate([x_ref[:, mine], x_ref[:, theirs]], axis=1)
    scale = lax.rsqrt(squares * scale_by + EPSILON) if scale_by else None
    parts = 2 if scale_by else 4
    block = brought[0].shape[1] // parts
    stores = []
    for j in range(parts):
        at = slice(j * block, (j + 1) * block)
        w = [jnp.where(core == holder, a[:, at], b[:, at]) for a, b in zip(brought, copied)]
        total = base_ref[:, at] + dot(x, jnp.concatenate(w, axis=0))
        if scale_by:
            ready_ref, sem = rest
            ready_ref[j] = (total * scale).astype(jnp.bfloat16)
            store = pltpu.make_async_copy(ready_ref.at[j], out_ref.at[:, pl.ds(j * block, block)], sem.at[j])
            store.start()
            stores.append(store)
        else:
            out_ref[:, at] = total
    if not scale_by:
        rest[0][...] = squares
    for store in stores:
        store.wait()


def project(holder, scale_by, x, base, squares, pieces):
    rows, columns = base.shape
    if scale_by:
        shape = jax.ShapeDtypeStruct((rows, columns), jnp.bfloat16)
        scratch = [pltpu.VMEM((2, rows, columns // 2), jnp.bfloat16), pltpu.SemaphoreType.DMA((2,))]
    else:
        shape = (pltpu.VMEM((rows, columns), jnp.float32), pltpu.VMEM((rows, 1), jnp.float32))
        scratch = []
    return pl.pallas_call(
        functools.partial(project_kernel, holder, scale_by),
        out_shape=shape,
        in_specs=[VMEM] * (3 + len(pieces)),
        out_specs=HBM if scale_by else (VMEM, VMEM),
        scratch_shapes=scratch,
        compiler_params=grant(16),
        name="project",
    )(*near_core(x, base, squares, *pieces))


def step(queries, keys, values, rates, fast_w1, fast_w2, fast_w3, norm_gain, out_weight):
    tok_rows, width = queries.shape
    ctx_count = lax.axis_size("ctx")
    heads = lax.axis_size("head")
    bits = ctx_count.bit_length() - 1
    assert ctx_count == 1 << bits and bits >= 3 and heads == 4

    tail, *chunks = load(keys, values, norm_gain, out_weight)
    tail = lax.ppermute(tail, "ctx", [(i, i + 1) for i in range(ctx_count - 1)])

    over = [(i, i ^ (2 if i // heads & 1 else 1)) for i in range(ctx_count * heads)]
    again = [(i, i ^ 1) for i in range(ctx_count * heads) if i // heads & 1]
    cross = [(i, i ^ (2 if i & 1 else 4)) for i in range(ctx_count)]
    early, relay, far, late = [], [], [], []
    for j, chunk in enumerate(chunks):
        early.append(lax.ppermute(chunk, ("ctx", "head"), over))
        relay.append(lax.ppermute(early[j], ("ctx", "head"), again))
        far.append(lax.ppermute(early[j], "ctx", cross))
        late.append(lax.ppermute(relay[j], "ctx", [(i, i ^ (2 << j)) for i in range(1, ctx_count, 2)]))

    def shared(arrays):
        copies = []
        for array in arrays:
            copies.append(swap(array, "ctx", 1))
        return copies

    early_c, relay_c = shared(early), shared(relay)
    far_c, late_c = shared(far), shared(late)
    pieces = {
        1: (0, early + far + early_c + far_c),
        2: (1, early + far + early_c + far_c),
        3: (1, relay + late + relay_c + late_c),
    }

    give_a, act, scaled, g1, g3 = pushes(keys, values, rates, fast_w1, fast_w2, fast_w3)
    give_b = contract(False, act, scaled)
    keep_a = contract(True, keys, g1, g3)
    keep_b = contract(True, act, scaled)

    masks = [1 << b for b in range(1, bits)]
    crossing = [
        [(i, i ^ (backward if i & 1 else forward)) for i in range(ctx_count)]
        for forward, backward in zip(masks, masks[::-1])
    ]
    weights = []
    for give, keep, olds in ((give_a, keep_a, (fast_w1, fast_w3)), (give_b, keep_b, (fast_w2,))):
        got = swap(give, "ctx", 1)
        for pairs in crossing:
            keep, send = add(keep, got)
            got = lax.ppermute(send, "ctx", pairs)
        mine = renorm(keep, got, *olds)
        other = swap(mine, "ctx", 1)
        weights.append((mine, other))
    weights = (weights[1][0], weights[0][0], weights[1][1], weights[0][1])

    seen = window(queries, keys, values, tail)

    rows = tok_rows // heads
    blocks = {}
    for k in send_order(heads) + [0]:
        mixed = mix(k, queries, weights[1], weights[3], rows)
        combined = combine(k, mixed, seen, weights[0], weights[2])
        blocks[k] = swap(combined, "head", k) if k else combined
    base, squares = own_project(blocks[0], norm_gain, out_weight)
    for k in (1, 3, 2):
        scale_by = 1.0 / (heads * width) if k == 2 else None
        holder, brought = pieces[k]
        result = project(holder, scale_by, blocks[k], base, squares, brought)
        if scale_by is None:
            base, squares = result
    return result


def send_order(heads):
    return [heads - 1] + list(range(1, heads - 1))


def solution(mesh):
    placed = (
        P("ctx", "head"),
        P("ctx", "head"),
        P("ctx", "head"),
        P("ctx", "head"),
        P("head", None, None),
        P("head", None, None),
        P("head", None, None),
        P("head"),
        P("head", None),
    )
    return jax.shard_map(step, mesh=mesh, in_specs=placed, out_specs=P(("ctx", "head"), None), check_vma=False)
```
